32 devices in a mesh: leaf: 8 (over z, x), pair: 4 (over y, core).
Axes of the slice: x: 2, y: 2, z: 4, core: 2. Of those that a mesh axis runs over, the one named last changes fastest.
Arguments:
- points: float32 [64, 65536], P(None, ('pair', 'leaf')), may hold values from -6 to 6
- inv_scales: float32 [64], replicated, may hold values from 0.05 to 0.3
- direction: float32 [32, 65536], P(None, ('pair', 'leaf')), may hold values from -6 to 6
- residual: float32 [32, 65536], P(None, ('pair', 'leaf'))
- skeleton: int32 [32, 32], P(('pair', 'leaf')), may hold values from 0 to 2047, as said below
Outputs:
- product: float32 [32, 65536], P(None, ('pair', 'leaf'))
- dots: float32 [2, 32], replicated
The draws below stay inside these ranges and needn't reach their ends.
Inputs may be any that keep to these rules, and one draw needn't show every extreme that they name: `skeleton`: each row holds 32 distinct indices of points inside its own block of 2048, among them the block's first and last point.
All inputs are finite; a program needn't handle non-finite values.
Results may differ from the reference program's by a relative error of at most 0.0003.
Values sent between devices are 32-bit elements; how exact they have to be, the bound alone decides.
A program may use at most 64 MiB of HBM per device.

```python
import math
import jax
import jax.numpy as jnp
from jax import lax

F = 64
R = 32
SKEL = 32
LEAF_PTS = 2048
NBLOCKS = 32
NPTS = 65536
N_LEAF = 8
N_PAIR = 4


def draw_residual(key, part):
    key_base = jax.random.fold_in(key, 11)
    ramp = jnp.exp(math.log(3.0) * jnp.arange(NPTS, dtype=jnp.float32) / NPTS)
    values = jax.random.normal(key_base, (R, NPTS), jnp.float32) * ramp[None, :]
    return values.astype(jnp.float32)


def draw_skeleton(key, part):
    keys = jax.random.split(jax.random.fold_in(key, 21), NBLOCKS)
    inner = jax.vmap(lambda one_key: jax.random.permutation(one_key, LEAF_PTS - 2)[:SKEL - 2] + 1)(keys)
    first = jnp.zeros((NBLOCKS, 1), jnp.int32)
    last = jnp.full((NBLOCKS, 1), LEAF_PTS - 1, jnp.int32)
    picks = jnp.concatenate([first, inner.astype(jnp.int32), last], axis=1)
    return picks.astype(jnp.int32)


def levels(key, dims, cuts, low, top_value):
    def one(dim, parts):
        draws = jax.random.uniform(jax.random.fold_in(jax.random.fold_in(key, 6), dim), (parts,), jnp.float32, low / len(cuts), top_value / len(cuts))
        return jnp.repeat(jnp.exp(draws), dims[dim] // parts).reshape((-1,) + (1,) * (len(dims) - dim - 1))

    gain = one(*cuts[0])
    for cut in cuts[1:]:
        gain = gain * one(*cut)
    return gain


def scatter_about(own_key, dims, scale, bound, cuts=(), kind=jnp.bfloat16):
    array = scale * jax.random.normal(own_key, dims, jnp.float32)
    if cuts:
        array = array * levels(own_key, dims, cuts, -0.22, 0.18)
    return jnp.clip(array, -bound, bound).astype(kind)


def setup_inputs(seed: int = 0) -> dict:
    streams_of = jax.random.split(jax.random.key(seed), 6)
    points = scatter_about(streams_of[0], (F, NPTS), 1.0, 6.0, ((1, 32),), jnp.float32)
    inv_scales = jnp.clip(jnp.exp(jax.random.uniform(streams_of[1], (F,), jnp.float32, math.log(0.05), math.log(0.3))), 0.05, 0.3)
    direction = scatter_about(streams_of[2], (R, NPTS), 1.0, 6.0, ((1, 32),), jnp.float32)
    residual = draw_residual(jax.random.fold_in(streams_of[5], 71), 0)
    skeleton = draw_skeleton(jax.random.fold_in(streams_of[5], 71), 0)
    return {"points": points, "inv_scales": inv_scales, "direction": direction, "residual": residual, "skeleton": skeleton}


root_three = math.sqrt(3.0)
nugget = 0.5
far_weight = 0.125

def matern(left, right):
    norm_left = lax.optimization_barrier(jnp.sum(left * left, axis=0))
    norm_right = lax.optimization_barrier(jnp.sum(right * right, axis=0))
    cross = lax.dot_general(left, right, (((0,), (0,)), ((), ())), precision=lax.Precision.HIGHEST, preferred_element_type=jnp.float32)
    dist_sq = norm_left[:, None] + norm_right[None, :] - 2.0 * cross
    scaled_dist = root_three * jnp.sqrt(jnp.maximum(dist_sq, 0.0))
    return (1.0 + scaled_dist) * jnp.exp(-scaled_dist)

def matmul(left, right):
    return jnp.dot(left, right, precision=lax.Precision.HIGHEST, preferred_element_type=jnp.float32)

def reference(points, inv_scales, direction, residual, skeleton):
    nblk = N_LEAF * N_PAIR
    scaled = points * inv_scales[:, None]
    zblocks = jnp.transpose(scaled.reshape(F, nblk, LEAF_PTS), (1, 0, 2))
    vblocks = jnp.transpose(direction.reshape(R, nblk, LEAF_PTS), (1, 0, 2))
    position = jnp.arange(nblk) % N_LEAF
    has_left = (position > 0).astype(jnp.float32)
    has_right = (position < N_LEAF - 1).astype(jnp.float32)
    zero_z = jnp.zeros((1, F, LEAF_PTS), jnp.float32)
    zero_v = jnp.zeros((1, R, LEAF_PTS), jnp.float32)
    z_left = jnp.concatenate([zero_z, zblocks[:-1]], axis=0)
    z_right = jnp.concatenate([zblocks[1:], zero_z], axis=0)
    v_left = jnp.concatenate([zero_v, vblocks[:-1]], axis=0) * has_left[:, None, None]
    v_right = jnp.concatenate([vblocks[1:], zero_v], axis=0) * has_right[:, None, None]
    skel_pts = jnp.take_along_axis(zblocks, skeleton.astype(jnp.int32)[:, None, :], axis=2)

    def coeff_of(index):
        return matmul(vblocks[index], matern(zblocks[index], skel_pts[index]))
    coeffs = lax.map(coeff_of, jnp.arange(nblk))
    all_pts = jnp.transpose(skel_pts, (1, 0, 2)).reshape(F, nblk * SKEL)
    all_coeff = jnp.transpose(coeffs, (1, 0, 2)).reshape(R, nblk * SKEL)
    col_block = jnp.arange(nblk * SKEL) // SKEL
    amplitude = 1.0 / math.sqrt(3.0 * LEAF_PTS)

    def block_product(index):
        own_z = zblocks[index]
        cols_z = jnp.concatenate([z_left[index], own_z, z_right[index]], axis=1)
        cols_v = jnp.concatenate([v_left[index], vblocks[index], v_right[index]], axis=1)
        near = matmul(cols_v, matern(cols_z, own_z))
        far_mask = (col_block // N_LEAF != index // N_LEAF) | (jnp.abs(col_block % N_LEAF - index % N_LEAF) > 1)
        masked = all_coeff * far_mask.astype(jnp.float32)[None, :]
        own_pts = skel_pts[index]
        q_coeff = matmul(masked, matern(all_pts, own_pts))
        spread = matern(own_z, own_pts)
        far = lax.dot_general(q_coeff, spread, (((1,), (1,)), ((), ())), precision=lax.Precision.HIGHEST, preferred_element_type=jnp.float32)
        return nugget * vblocks[index] + amplitude * (near + far_weight * far)
    blocks_out = lax.map(block_product, jnp.arange(nblk))
    product = jnp.transpose(blocks_out, (1, 0, 2)).reshape(R, nblk * LEAF_PTS)
    total = nblk * LEAF_PTS
    squares = lax.optimization_barrier(jnp.sum(residual * residual, axis=1)) / total
    curvature = lax.optimization_barrier(jnp.sum(direction * product, axis=1)) / total
    return (product, jnp.stack([squares, curvature], axis=0))
```

```python
import functools
import math

import jax
import jax.numpy as jnp
from jax import lax
from jax.experimental import pallas as pl
from jax.experimental.pallas import tpu as pltpu
from jax.sharding import PartitionSpec as P

root_three = math.sqrt(3.0)
log2e = 1.4426950408889634
ln2 = 1.0 / log2e
nugget = 0.5
far_weight = 0.125
tiny = 1e-30
f32 = jnp.float32
bf16 = jnp.bfloat16
TI = 256
CC = 512
FIRST = 2
CH = 256


def matern_of(u):
    u = jnp.maximum(u, tiny)
    t = u * lax.rsqrt(u)
    return (log2e + t) * jnp.exp2(-t)


def bdot(a, b):
    return jnp.dot(a, b, preferred_element_type=f32)


def bdot_nt(a, b):
    return lax.dot_general(a, b, (((1,), (1,)), ((), ())), preferred_element_type=f32)


def split(x):
    h = x.astype(bf16)
    return h, (x - h.astype(f32)).astype(bf16)


def kernel(
    nleaf, npair, nblk_total,
    pts_ref, inv_ref, dir_ref, res_ref, skel_ref,
    prod_ref, dots_ref,
    xb_p, xb_d, zb_p, zb_d, ret_out, ret_in, b_ref, st_ref, dd_ref, acc_ref, pacc_ref, ks_ref, ag_ref, red_a, red_b, tmp_ref, curv_ref,
    hs_sem, hr_sem, fs_sem, fr_sem, es_sem, er_sem, ps_sem, pr_sem, as_sem, ar_sem, bs_sem, br_sem, cs_sem, cr_sem, ds_sem, dr_sem,
):
    feats, n = pts_ref.shape
    rhs = dir_ref.shape[0]
    nskel = skel_ref.shape[1]
    leaf = lax.axis_index("leaf")
    pair = lax.axis_index("pair")

    leaf_odd = lax.rem(leaf, 2)
    pair_odd = lax.rem(pair, 2)
    is_main = leaf_odd == pair_odd
    is_help = leaf_odd != pair_odd
    slot = jnp.where(is_main, 0, 1)
    step = 1 - 2 * leaf_odd
    other = pair + 1 - 2 * pair_odd
    main_pair = jnp.where(is_main, pair, other)
    far_leaf = leaf + 2 * step
    chip_two = jnp.logical_and(far_leaf >= 0, far_leaf < nleaf)
    helping = jnp.logical_and(is_help, chip_two)
    has_pair = jnp.logical_or(is_main, chip_two)
    back_leaf = leaf - 2 * step
    back_ok = jnp.logical_and(is_main, jnp.logical_and(back_leaf >= 0, back_leaf < nleaf))
    home_step = 1 - 2 * pair_odd
    home_leaf = leaf - home_step
    home_far = home_leaf + 2 * home_step
    home_two = jnp.logical_and(is_help, jnp.logical_and(home_far >= 0, home_far < nleaf))

    def remote(src, dst, ss, rs, **dev):
        return pltpu.make_async_remote_copy(
            src_ref=src, dst_ref=dst, send_sem=ss, recv_sem=rs, device_id=dev,
            device_id_type=pl.DeviceIdType.MESH)

    def leaf_peer(k):
        return lax.rem(leaf + k, nleaf)

    def pair_peer(k):
        return lax.rem(pair + k, npair)

    barrier = pltpu.get_barrier_semaphore()

    def greet(**dev):
        pl.semaphore_signal(barrier, inc=1, device_id=dev, device_id_type=pl.DeviceIdType.MESH)

    for k in range(1, nleaf):
        greet(leaf=leaf_peer(k))
    for k in range(1, npair):
        greet(pair=pair_peer(k))

    @pl.when(back_ok)
    def _():
        greet(leaf=back_leaf, pair=other)

    @pl.when(helping)
    def _():
        greet(leaf=far_leaf, pair=other)
        greet(leaf=leaf + step, pair=other)

    @pl.when(home_two)
    def _():
        greet(leaf=home_leaf, pair=other)

    def chunk(ci):
        return pl.ds(pl.multiple_of(ci * CC, CC), CC)

    def block_copies(ci, src_p, src_d, dst_p, dst_d, ss, rs, dev):
        cols = chunk(ci)
        return (
            remote(src_p.at[:, cols], dst_p.at[:, cols], ss.at[0, ci], rs.at[0, ci], **dev),
            remote(src_d.at[:, cols], dst_d.at[:, cols], ss.at[1, ci], rs.at[1, ci], **dev),
        )

    def to_main(ci):
        return block_copies(ci, pts_ref, dir_ref, xb_p, xb_d, hs_sem, hr_sem, dict(leaf=home_leaf, pair=pair))

    def to_help(ci):
        return block_copies(ci, pts_ref, dir_ref, zb_p, zb_d, hs_sem, hr_sem, dict(leaf=back_leaf, pair=other))

    def relay(ci):
        return block_copies(ci, xb_p, xb_d, xb_p, xb_d, fs_sem, fr_sem, dict(leaf=leaf, pair=other))

    def give_back(ci):
        cols = chunk(ci)
        return remote(ret_out.at[:, cols], ret_in.at[slot, :, cols], es_sem.at[ci], er_sem.at[slot, ci], leaf=leaf + step, pair=main_pair)

    def give_rows():
        return remote(pacc_ref, ret_in.at[0], ps_sem, pr_sem, leaf=far_leaf, pair=other)

    nc = n // CC

    def send_block(lo, hi):
        @pl.when(is_help)
        def _():
            for ci in range(lo, hi):
                for c in to_main(ci):
                    c.start()

        @pl.when(back_ok)
        def _():
            for ci in range(lo, hi):
                for c in to_help(ci):
                    c.start()

    eye = lax.broadcasted_iota(jnp.int32, (feats, feats), 0) == lax.broadcasted_iota(jnp.int32, (feats, feats), 1)
    inv_col = jnp.sum(jnp.where(eye, jnp.broadcast_to(inv_ref[...], (feats, feats)), 0.0), axis=1, keepdims=True) * (root_three * log2e)

    def norm_rows(norm):
        n1 = norm.astype(bf16).astype(f32)
        n2 = (norm - n1).astype(bf16).astype(f32)
        return jnp.concatenate([n1, n2, norm - n1 - n2], axis=0)

    def parts(p_src, cols):
        p = p_src[:, cols] * inv_col
        h, l = split(p)
        hf, lf = h.astype(f32), l.astype(f32)
        q = hf + lf
        norm = norm_rows(jnp.sum(q * q, axis=0, keepdims=True))
        return h, l, hf, lf, norm

    def as_cols(h, l, norm):
        w = norm.shape[1]
        ext = jnp.concatenate([jnp.ones((3, w), f32), norm, jnp.zeros((feats - 6, w), f32)], axis=0)
        return jnp.concatenate([h, l, h, ext.astype(bf16)], axis=0)

    def as_rows(hf, lf, norm):
        w = norm.shape[1]
        ext = jnp.concatenate([norm, jnp.ones((3, w), f32), jnp.zeros((feats - 6, w), f32)], axis=0)
        h2 = hf * -2.0
        return jnp.concatenate([h2, h2, lf * -2.0, ext], axis=0).T.astype(bf16)

    def both_halves(d_src, cols):
        return jnp.concatenate(split(d_src[:, cols]), axis=0)

    @pl.loop(0, n // CH)
    def _(ci):
        cols = pl.ds(pl.multiple_of(ci * CH, CH), CH)
        h, l, hf, lf, norm = parts(pts_ref, cols)
        b_ref[:, cols] = as_cols(h, l, norm)
        st_ref[0, cols, :] = as_rows(hf, lf, norm)
        dd_ref[0, :, cols] = both_halves(dir_ref, cols)
        acc_ref[:, cols] = jnp.zeros((rhs, CH), f32)
        pacc_ref[:, cols] = jnp.zeros((rhs, CH), f32)

    extra = jnp.where(back_ok, 1, 0) + jnp.where(helping, 2, 0) + jnp.where(home_two, 1, 0)
    pl.semaphore_wait(barrier, nleaf - 1 + npair - 1 + extra)

    send_block(0, FIRST)

    nt = n // TI

    def tiles(st, rows_of, count, b):
        nxt = bdot(st[rows_of(0), :], b)
        for i in range(count):
            u = nxt
            if i + 1 < count:
                nxt = bdot(st[rows_of(i + 1), :], b)
            now = (i,) + split(matern_of(u))
            if i:
                yield held
            held = now
        yield held

    def own_block():
        st = st_ref.at[0]
        dd = dd_ref.at[0]

        @pl.loop(0, nt)
        def _(jt):
            cols = pl.ds(pl.multiple_of(jt * TI, TI), TI)
            b = b_ref[:, cols]
            ddj = dd[:, cols]
            a1 = jnp.zeros((2 * rhs, TI), f32)
            a2 = jnp.zeros((rhs, TI), f32)

            def rows_of(d):
                return pl.ds(pl.multiple_of(lax.rem(jt + nt - d, nt) * TI, TI), TI)

            later = []
            for d, kh, kl in tiles(st, rows_of, nt // 2 + 1, b):
                rows = rows_of(d)
                a1 = a1 + bdot(dd[:, rows], kh)
                a2 = a2 + bdot(dd[:rhs, rows], kl)
                if 0 < d and 2 * d < nt:
                    r1 = bdot_nt(ddj, kh)
                    later.append((rows, r1[:rhs] + r1[rhs:] + bdot_nt(ddj[:rhs], kl)))
            acc_ref[:, cols] += a1[:rhs] + a1[rhs:] + a2
            for rows, part in later:
                acc_ref[:, rows] += part

    def pair_chunk(ci):
        @pl.when(is_main)
        def _():
            for c in to_main(ci):
                c.wait_recv()

            @pl.when(chip_two)
            def _():
                for c in relay(ci):
                    c.start()

        @pl.when(is_help)
        def _():
            for c in relay(ci):
                c.wait_recv()

        st = st_ref.at[slot]
        dd = dd_ref.at[slot]

        @pl.loop(0, CC // TI)
        def _(half):
            cols = pl.ds(pl.multiple_of(ci * CC + half * TI, TI), TI)
            h, l, _, _, norm = parts(xb_p, cols)
            b = as_cols(h, l, norm)
            ddj = both_halves(xb_d, cols)
            a1 = jnp.zeros((2 * rhs, TI), f32)
            a2 = jnp.zeros((rhs, TI), f32)
            for it, kh, kl in tiles(st, lambda i: slice(i * TI, (i + 1) * TI), nt, b):
                rows = slice(it * TI, (it + 1) * TI)
                a1 = a1 + bdot(dd[:, rows], kh)
                a2 = a2 + bdot(dd[:rhs, rows], kl)
                r1 = bdot_nt(ddj, kh)
                pacc_ref[:, rows] += r1[:rhs] + r1[rhs:] + bdot_nt(ddj[:rhs], kl)
            ret_out[:, cols] = a1[:rhs] + a1[rhs:] + a2

        give_back(ci).start()

    onehot = (lax.broadcasted_iota(jnp.int32, (n, nskel), 0) == jnp.broadcast_to(skel_ref[...], (n, nskel)))
    onehot = jnp.where(onehot, 1.0, 0.0).astype(bf16)
    picked = bdot(b_ref[: 2 * feats, :], onehot)
    skel_rows = (picked[:feats] + picked[feats:]).T
    norm_s = jnp.sum(skel_rows * skel_rows, axis=1, keepdims=True)
    sh, sl = split(skel_rows)
    sh, sl = sh.astype(f32) * -2.0, sl.astype(f32) * -2.0
    n1 = norm_s.astype(bf16).astype(f32)
    n2 = (norm_s - n1).astype(bf16).astype(f32)
    lane_s = lax.broadcasted_iota(jnp.int32, (nskel, feats), 1)
    ext_s = jnp.where(lane_s == 0, n1, jnp.where(lane_s == 1, n2, jnp.where(lane_s == 2, norm_s - n1 - n2, jnp.where(lane_s < 6, 1.0, 0.0))))
    ksh, ksl = split(matern_of(bdot(jnp.concatenate([sh, sh, sl, ext_s], axis=1).astype(bf16), b_ref[...])))
    ks_ref[...] = jnp.concatenate([ksh, ksl], axis=0)
    part = bdot_nt(ks_ref[...], dd_ref[0])
    coeff_t = part[:nskel, :rhs] + part[:nskel, rhs:] + part[nskel:, :rhs] + part[nskel:, rhs:]
    pad = jnp.zeros((nskel, 128 - feats - rhs), f32)
    pack = jnp.concatenate([skel_rows, coeff_t, pad], axis=1)
    my_rows = pl.ds(pl.multiple_of(leaf * nskel, 8), nskel)
    ag_ref[pair, my_rows, :] = pack
    tmp_ref[...] = jnp.concatenate([skel_rows, jnp.zeros((nskel, 128 - feats), f32)], axis=1)

    stage_a = [
        remote(ag_ref.at[pair, my_rows, :], ag_ref.at[pair, my_rows, :], as_sem.at[k], ar_sem.at[k], leaf=leaf_peer(k))
        for k in range(1, nleaf)
    ]
    for c in stage_a:
        c.start()

    send_block(FIRST, nc)
    own_block()

    @pl.when(helping)
    def _():
        for ci in range(nc):
            for c in to_help(ci):
                c.wait_recv()

        @pl.loop(0, n // CH)
        def _(ci):
            cols = pl.ds(pl.multiple_of(ci * CH, CH), CH)
            _, _, hf, lf, norm = parts(zb_p, cols)
            st_ref[1, cols, :] = as_rows(hf, lf, norm)
            dd_ref[1, :, cols] = both_halves(zb_d, cols)

    stage_b = [
        remote(ag_ref.at[pair], ag_ref.at[pair], bs_sem.at[k], br_sem.at[k], pair=pair_peer(k))
        for k in range(1, npair)
    ]

    @pl.loop(0, nc)
    def _(ci):
        @pl.when(ci == 1)
        def _():
            for k, c in enumerate(stage_a, 1):
                src_rows = pl.ds(pl.multiple_of(lax.rem(leaf + nleaf - k, nleaf) * nskel, 8), nskel)
                remote(ag_ref.at[pair, src_rows, :], ag_ref.at[pair, src_rows, :], as_sem.at[k], ar_sem.at[k], leaf=leaf_peer(k)).wait_recv()
            for c in stage_a:
                c.wait_send()
            for c in stage_b:
                c.start()

        @pl.when(has_pair)
        def _():
            pair_chunk(ci)

    @pl.when(helping)
    def _():
        give_rows().start()

    for k, c in enumerate(stage_b, 1):
        src = lax.rem(pair + npair - k, npair)
        remote(ag_ref.at[src], ag_ref.at[src], bs_sem.at[k], br_sem.at[k], pair=pair_peer(k)).wait_recv()
    for c in stage_b:
        c.wait_send()

    width = nleaf * nskel
    own_rows = tmp_ref[...]
    own_norm = jnp.sum(own_rows * own_rows, axis=1, keepdims=True)
    own_both = jnp.concatenate(split(own_rows), axis=0)
    is_pt = jnp.where(lax.broadcasted_iota(jnp.int32, (8, 128), 1) < feats, 1.0, 0.0).astype(bf16)
    column_leaf = lax.div(lax.broadcasted_iota(jnp.int32, (nskel, width), 1), nskel)
    near_mask = jnp.abs(column_leaf - leaf) <= 1
    q_t = jnp.zeros((nskel, 128), f32)
    for p in range(npair):
        ah, al = split(ag_ref[p])
        ar = ah.astype(f32) + al.astype(f32)
        sq = ar * ar
        s0, r1 = sq.astype(bf16), sq - sq.astype(bf16).astype(f32)
        s1, s2 = split(r1)
        norm_all = (bdot_nt(is_pt, s0) + bdot_nt(is_pt, s1) + bdot_nt(is_pt, s2))[0:1, :]
        cross = bdot_nt(own_both, ah) + bdot_nt(own_both, al)
        w = matern_of(own_norm + norm_all - 2.0 * (cross[:nskel] + cross[nskel:]))
        same = jnp.full((nskel, width), pair, jnp.int32) == p
        w = jnp.where(jnp.logical_and(same, near_mask), 0.0, w)
        wh, wl = split(w)
        part = bdot(jnp.concatenate([wh, wl], axis=0), ah)
        q_t = q_t + part[:nskel] + part[nskel:] + bdot(wh, al)
    q_t = q_t[:, feats : feats + rhs]
    qh, ql = split(q_t.T)
    far = bdot(jnp.concatenate([qh, ql], axis=0), ks_ref[:nskel, :])
    far = far[:rhs] + far[rhs:] + bdot(qh, ks_ref[nskel:, :])
    amplitude = 1.0 / math.sqrt(3.0 * n)
    near_scale = amplitude * ln2
    far_scale = amplitude * far_weight * ln2 * ln2 * ln2
    direction = dir_ref[...]
    base = nugget * direction + near_scale * acc_ref[...] + far_scale * far

    @pl.when(is_main)
    def _():
        pair_part = near_scale * pacc_ref[...]
        product = base + pair_part
        prod_ref[...] = product
        curv_ref[...] = jnp.broadcast_to(jnp.sum(direction * (product + pair_part), axis=1, keepdims=True), (rhs, 128))

    @pl.when(is_help)
    def _():
        prod_ref[...] = base
        curv_ref[...] = jnp.broadcast_to(jnp.sum(direction * base, axis=1, keepdims=True), (rhs, 128))

    @pl.when(helping)
    def _():
        shared = jnp.sum(zb_d[...] * pacc_ref[...], axis=1, keepdims=True)
        curv_ref[...] += jnp.broadcast_to((2.0 * near_scale) * shared, (rhs, 128))

    residual = res_ref[...]
    squares = jnp.sum(residual * residual, axis=1, keepdims=True)
    lane = lax.broadcasted_iota(jnp.int32, (rhs, 128), 1)
    both = jnp.where(lane == 0, squares, jnp.where(lane == 1, curv_ref[...], 0.0))
    both = jnp.concatenate([both, jnp.zeros((128 - rhs, 128), f32)], axis=0).T[0:8, :]
    red_a[leaf] = both
    sends = [
        remote(red_a.at[leaf], red_a.at[leaf], cs_sem.at[k], cr_sem.at[k], leaf=leaf_peer(k))
        for k in range(1, nleaf)
    ]
    for c in sends:
        c.start()
    for k in range(1, nleaf):
        src = lax.rem(leaf + nleaf - k, nleaf)
        remote(red_a.at[src], red_a.at[src], cs_sem.at[k], cr_sem.at[k], leaf=leaf_peer(k)).wait_recv()
    total = red_a[0]
    for k in range(1, nleaf):
        total = total + red_a[k]
    red_b[pair] = total
    sends_b = [
        remote(red_b.at[pair], red_b.at[pair], ds_sem.at[k], dr_sem.at[k], pair=pair_peer(k))
        for k in range(1, npair)
    ]
    for c in sends_b:
        c.start()
    for k in range(1, npair):
        src = lax.rem(pair + npair - k, npair)
        remote(red_b.at[src], red_b.at[src], ds_sem.at[k], dr_sem.at[k], pair=pair_peer(k)).wait_recv()
    total = red_b[0]
    for k in range(1, npair):
        total = total + red_b[k]

    dots_ref[...] = total[0:2, :rhs] * (1.0 / nblk_total)

    def returned(k, ci):
        cols = chunk(ci)
        return remote(ret_out.at[:, cols], ret_in.at[k, :, cols], es_sem.at[ci], er_sem.at[k, ci], leaf=home_leaf, pair=pair)

    @pl.when(back_ok)
    def _():
        give_rows().wait_recv()
        prod_ref[...] += near_scale * ret_in[0]

    @pl.when(is_help)
    def _():
        for ci in range(nc):
            returned(0, ci).wait_recv()
        prod_ref[...] += near_scale * ret_in[0]

    @pl.when(home_two)
    def _():
        for ci in range(nc):
            returned(1, ci).wait_recv()
        prod_ref[...] += near_scale * ret_in[1]

    for c in sends + sends_b:
        c.wait_send()

    @pl.when(has_pair)
    def _():
        for ci in range(nc):
            give_back(ci).wait_send()

    @pl.when(helping)
    def _():
        give_rows().wait_send()

    @pl.when(jnp.logical_and(is_main, chip_two))
    def _():
        for ci in range(nc):
            for c in relay(ci):
                c.wait_send()

    @pl.when(is_help)
    def _():
        for ci in range(nc):
            for c in to_main(ci):
                c.wait_send()

    @pl.when(back_ok)
    def _():
        for ci in range(nc):
            for c in to_help(ci):
                c.wait_send()


def on_device(points, inv_scales, direction, residual, skeleton):
    feats, n = points.shape
    rhs = direction.shape[0]
    nskel = skeleton.shape[1]
    nleaf = lax.axis_size("leaf")
    npair = lax.axis_size("pair")
    vmem = pl.BlockSpec(memory_space=pltpu.VMEM)
    dma = pltpu.SemaphoreType.DMA
    nc = n // CC
    return pl.pallas_call(
        functools.partial(kernel, nleaf, npair, n * nleaf * npair),
        out_shape=(jax.ShapeDtypeStruct((rhs, n), f32), jax.ShapeDtypeStruct((2, rhs), f32)),
        in_specs=[vmem] * 5,
        out_specs=(vmem, vmem),
        scratch_shapes=[
            pltpu.VMEM((feats, n), f32),
            pltpu.VMEM((rhs, n), f32),
            pltpu.VMEM((feats, n), f32),
            pltpu.VMEM((rhs, n), f32),
            pltpu.VMEM((rhs, n), f32),
            pltpu.VMEM((2, rhs, n), f32),
            pltpu.VMEM((4 * feats, n), bf16),
            pltpu.VMEM((2, n, 4 * feats), bf16),
            pltpu.VMEM((2, 2 * rhs, n), bf16),
            pltpu.VMEM((rhs, n), f32),
            pltpu.VMEM((rhs, n), f32),
            pltpu.VMEM((2 * nskel, n), bf16),
            pltpu.VMEM((npair, nleaf * nskel, 128), f32),
            pltpu.VMEM((nleaf, 8, 128), f32),
            pltpu.VMEM((npair, 8, 128), f32),
            pltpu.VMEM((nskel, 128), f32),
            pltpu.VMEM((rhs, 128), f32),
            dma((2, nc)), dma((2, nc)),
            dma((2, nc)), dma((2, nc)),
            dma((nc,)), dma((2, nc)),
            dma, dma,
            dma((nleaf,)), dma((nleaf,)),
            dma((npair,)), dma((npair,)),
            dma((nleaf,)), dma((nleaf,)),
            dma((npair,)), dma((npair,)),
        ],
        compiler_params=pltpu.CompilerParams(collective_id=0, has_side_effects=True, vmem_limit_bytes=60 * 1024 * 1024),
        name="matern_step",
    )(points, inv_scales.reshape(1, feats), direction, residual, skeleton)


def solution(mesh):
    return jax.shard_map(
        on_device,
        mesh=mesh,
        in_specs=(
            P(None, ("pair", "leaf")),
            P(),
            P(None, ("pair", "leaf")),
            P(None, ("pair", "leaf")),
            P(("pair", "leaf"), None),
        ),
        out_specs=(P(None, ("pair", "leaf")), P()),
        check_vma=False,
    )
```

```python
import functools
import math

import jax
import jax.numpy as jnp
from jax import lax
from jax.experimental import pallas as pl
from jax.experimental.pallas import tpu as pltpu
from jax.sharding import PartitionSpec as P

root_three = math.sqrt(3.0)
neg_log2e = -1.4426950408889634
nugget = 0.5
far_weight = 0.125
tiny = 1e-30
f32 = jnp.float32
bf16 = jnp.bfloat16
TI = 256
CC = 512
FIRST = 4
CH = 256


def matern_of(u):
    u = jnp.maximum(u, tiny)
    t = u * lax.rsqrt(u)
    return (1.0 + t) * jnp.exp2(t * neg_log2e)


def split(x):
    h = x.astype(bf16)
    return h, (x - h.astype(f32)).astype(bf16)


def kernel(
    nleaf, npair, nblk_total,
    pts_ref, inv_ref, dir_ref, res_ref, skel_ref,
    prod_ref, dots_ref,
    xb_p, xb_d, zb_p, zb_d, ret_out, ret_in, b_ref, st_ref, dd_ref, w_ref, acc_ref, pacc_ref, ks_ref, ag_ref, red_a, red_b, tmp_ref, curv_ref,
    hs_sem, hr_sem, fs_sem, fr_sem, es_sem, er_sem, ps_sem, pr_sem, as_sem, ar_sem, bs_sem, br_sem, cs_sem, cr_sem, ds_sem, dr_sem,
):
    feats, n = pts_ref.shape
    rhs = dir_ref.shape[0]
    nskel = skel_ref.shape[1]
    leaf = lax.axis_index("leaf")
    pair = lax.axis_index("pair")

    leaf_odd = lax.rem(leaf, 2)
    pair_odd = lax.rem(pair, 2)
    is_main = leaf_odd == pair_odd
    is_help = leaf_odd != pair_odd
    slot = jnp.where(is_main, 0, 1)
    step = 1 - 2 * leaf_odd
    other = pair + 1 - 2 * pair_odd
    main_pair = jnp.where(is_main, pair, other)
    far_leaf = leaf + 2 * step
    chip_two = jnp.logical_and(far_leaf >= 0, far_leaf < nleaf)
    helping = jnp.logical_and(is_help, chip_two)
    has_pair = jnp.logical_or(is_main, chip_two)
    back_leaf = leaf - 2 * step
    back_ok = jnp.logical_and(is_main, jnp.logical_and(back_leaf >= 0, back_leaf < nleaf))
    home_step = 1 - 2 * pair_odd
    home_leaf = leaf - home_step
    home_far = home_leaf + 2 * home_step
    home_two = jnp.logical_and(is_help, jnp.logical_and(home_far >= 0, home_far < nleaf))

    def remote(src, dst, ss, rs, **dev):
        return pltpu.make_async_remote_copy(
            src_ref=src, dst_ref=dst, send_sem=ss, recv_sem=rs, device_id=dev,
            device_id_type=pl.DeviceIdType.MESH)

    def leaf_peer(k):
        return lax.rem(leaf + k, nleaf)

    def pair_peer(k):
        return lax.rem(pair + k, npair)

    barrier = pltpu.get_barrier_semaphore()

    def greet(**dev):
        pl.semaphore_signal(barrier, inc=1, device_id=dev, device_id_type=pl.DeviceIdType.MESH)

    for k in range(1, nleaf):
        greet(leaf=leaf_peer(k))
    for k in range(1, npair):
        greet(pair=pair_peer(k))

    @pl.when(back_ok)
    def _():
        greet(leaf=back_leaf, pair=other)

    @pl.when(helping)
    def _():
        greet(leaf=far_leaf, pair=other)
        greet(leaf=leaf + step, pair=other)

    @pl.when(home_two)
    def _():
        greet(leaf=home_leaf, pair=other)

    def chunk(ci):
        return pl.ds(pl.multiple_of(ci * CC, CC), CC)

    def block_copies(ci, src_p, src_d, dst_p, dst_d, ss, rs, dev):
        cols = chunk(ci)
        return (
            remote(src_p.at[:, cols], dst_p.at[:, cols], ss.at[0, ci], rs.at[0, ci], **dev),
            remote(src_d.at[:, cols], dst_d.at[:, cols], ss.at[1, ci], rs.at[1, ci], **dev),
        )

    def to_main(ci):
        return block_copies(ci, pts_ref, dir_ref, xb_p, xb_d, hs_sem, hr_sem, dict(leaf=home_leaf, pair=pair))

    def to_help(ci):
        return block_copies(ci, pts_ref, dir_ref, zb_p, zb_d, hs_sem, hr_sem, dict(leaf=back_leaf, pair=other))

    def relay(ci):
        return block_copies(ci, xb_p, xb_d, xb_p, xb_d, fs_sem, fr_sem, dict(leaf=leaf, pair=other))

    def give_back(ci):
        cols = chunk(ci)
        return remote(ret_out.at[:, cols], ret_in.at[slot, :, cols], es_sem.at[ci], er_sem.at[slot, ci], leaf=leaf + step, pair=main_pair)

    def give_rows():
        return remote(pacc_ref, ret_in.at[0], ps_sem, pr_sem, leaf=far_leaf, pair=other)

    nc = n // CC

    def send_block(lo, hi):
        @pl.when(is_help)
        def _():
            for ci in range(lo, hi):
                for c in to_main(ci):
                    c.start()

        @pl.when(back_ok)
        def _():
            for ci in range(lo, hi):
                for c in to_help(ci):
                    c.start()

    eye = lax.broadcasted_iota(jnp.int32, (feats, feats), 0) == lax.broadcasted_iota(jnp.int32, (feats, feats), 1)
    inv_col = jnp.sum(jnp.where(eye, jnp.broadcast_to(inv_ref[...], (feats, feats)), 0.0), axis=1, keepdims=True) * root_three

    def norm_rows(norm):
        n1 = norm.astype(bf16).astype(f32)
        n2 = (norm - n1).astype(bf16).astype(f32)
        return jnp.concatenate([n1, n2, norm - n1 - n2], axis=0)

    def parts(p_src, cols):
        p = p_src[:, cols] * inv_col
        h, l = split(p)
        hf, lf = h.astype(f32), l.astype(f32)
        q = hf + lf
        norm = norm_rows(jnp.sum(q * q, axis=0, keepdims=True))
        return h, l, hf, lf, norm

    def as_cols(h, l, norm):
        w = norm.shape[1]
        ext = jnp.concatenate([jnp.ones((3, w), f32), norm, jnp.zeros((feats - 6, w), f32)], axis=0)
        return jnp.concatenate([h, l, h, ext.astype(bf16)], axis=0)

    def as_rows(hf, lf, norm):
        w = norm.shape[1]
        ext = jnp.concatenate([norm, jnp.ones((3, w), f32), jnp.zeros((feats - 6, w), f32)], axis=0)
        h2 = hf * -2.0
        return jnp.concatenate([h2, h2, lf * -2.0, ext], axis=0).T.astype(bf16)

    def both_halves(d_src, cols):
        return jnp.concatenate(split(d_src[:, cols]), axis=0)

    def as_weights(dd):
        w = dd.shape[1]
        return jnp.concatenate([dd.astype(f32), jnp.zeros((128 - 2 * rhs, w), f32)], axis=0).T.astype(bf16)

    @pl.loop(0, n // CH)
    def _(ci):
        cols = pl.ds(pl.multiple_of(ci * CH, CH), CH)
        h, l, hf, lf, norm = parts(pts_ref, cols)
        b_ref[0, :, cols] = as_cols(h, l, norm)
        st_ref[cols, :] = as_rows(hf, lf, norm)
        dd = both_halves(dir_ref, cols)
        dd_ref[:, cols] = dd
        w_ref[0, cols, :] = as_weights(dd)
        ks_ref[3 * nskel :, cols] = jnp.zeros((TI - 3 * nskel, CH), bf16)
        acc_ref[:, cols] = jnp.zeros((rhs, CH), f32)
        pacc_ref[:, cols] = jnp.zeros((rhs, CH), f32)

    extra = jnp.where(back_ok, 1, 0) + jnp.where(helping, 2, 0) + jnp.where(home_two, 1, 0)
    pl.semaphore_wait(barrier, nleaf - 1 + npair - 1 + extra)

    send_block(0, FIRST)

    nt = n // TI

    def sweep(plan, xs, ys, rs):
        stage = [0, 0]

        def push(v, m):
            k = stage[m]
            stage[m] = 1 - k
            pltpu.matmul_push_rhs(v, k, m)
            return k

        def cross(t):
            pltpu.matmul_acc_lhs(xs[t % 2], plan[t]["rows"](), load_staged_rhs=push(plan[t]["cols"](), 1))

        def spend(t, k):
            p = plan[t]
            if p["turn"] is not None:
                w = p["weights"]()
                w = jnp.concatenate([w, jnp.zeros_like(w)], axis=1)
                pltpu.matmul_acc_lhs(rs[p["turn"]], k, load_staged_rhs=push(w, 0))
            m = t % 2
            dd = p["dd"]()
            pltpu.matmul_acc_lhs(ys[m], dd[:rhs], load_staged_rhs=push(k, m))
            pltpu.matmul_acc_lhs(ys[m], dd[rhs:])

        def finish(t):
            p = plan[t]
            p["out"](pltpu.matmul_pop(ys[t % 2]))
            if p["turned"] is not None:
                r = pltpu.matmul_pop(rs[p["turn"]])[:, :128].T
                p["turned"](r[:rhs] + r[rhs : 2 * rhs])

        count = len(plan)
        cross(0)
        held = None
        for t in range(count + 2):
            k = None
            if t < count:
                k = matern_of(pltpu.matmul_pop(xs[t % 2])).astype(bf16)
            if t + 1 < count:
                cross(t + 1)
            if 0 < t <= count:
                spend(t - 1, held)
            held = k
            if t > 1:
                finish(t - 2)

    def own_block(xs, ys, rs):
        @pl.loop(0, nt // 2)
        def _(k):
            plan = []
            for i in range(2):
                def tile(d, i=i):
                    return pl.ds(pl.multiple_of(lax.rem(2 * k + i + nt - d, nt) * TI, TI), TI)

                def add(cols):
                    def go(v):
                        acc_ref[:, cols] += v
                    return go

                rows = tile(0)
                for d in range(nt // 2 + 1):
                    cols = tile(d)
                    both = 0 < d and 2 * d < nt
                    plan.append(dict(
                        rows=lambda rows=rows: st_ref[rows, :],
                        cols=lambda cols=cols: b_ref[0, :, cols],
                        weights=lambda cols=cols: w_ref[0, cols, :],
                        dd=lambda rows=rows: dd_ref[:, rows],
                        turn=i if both else None,
                        out=add(cols),
                        turned=add(rows) if both and 2 * (d + 1) >= nt else None,
                    ))
            sweep(plan, xs, ys, rs)

    def pair_chunk(ci, xs, ys, rs):
        @pl.when(is_main)
        def _():
            for c in to_main(ci):
                c.wait_recv()

            @pl.when(chip_two)
            def _():
                for c in relay(ci):
                    c.start()

        @pl.when(is_help)
        def _():
            for c in relay(ci):
                c.wait_recv()

        plan = []
        for i in range(CC // TI):
            rows = pl.ds(pl.multiple_of(ci * CC + i * TI, TI), TI)
            _, _, hf, lf, norm = parts(xb_p, rows)
            st = as_rows(hf, lf, norm)
            dd = both_halves(xb_d, rows)

            def turned(v, rows=rows):
                ret_out[:, rows] = v

            for jt in range(nt):
                cols = slice(jt * TI, (jt + 1) * TI)

                def add(v, cols=cols):
                    pacc_ref[:, cols] += v

                plan.append(dict(
                    rows=lambda st=st: st,
                    cols=lambda cols=cols: b_ref[slot, :, cols],
                    weights=lambda cols=cols: w_ref[slot, cols, :],
                    dd=lambda dd=dd: dd,
                    turn=i,
                    out=add,
                    turned=turned if jt == nt - 1 else None,
                ))
        sweep(plan, xs, ys, rs)
        give_back(ci).start()

    def wide(w):
        return jnp.concatenate([w, jnp.zeros((w.shape[0], TI - w.shape[1]), w.dtype)], axis=1)

    def deep_dot(accs, lhs, rhs_of, count):
        for k in range(count):
            m, r = k % 2, (k // 2) % 2
            pltpu.matmul_push_rhs(rhs_of(k), r, m)
            pltpu.matmul_acc_lhs(accs[m], lhs(k), load_staged_rhs=r)
        return pltpu.matmul_pop(accs[0]) + pltpu.matmul_pop(accs[1])

    def block(k):
        return slice(k * TI, (k + 1) * TI)

    def skeleton(p0, p1, c0, c1, f0, f1):
        index = jnp.broadcast_to(wide(skel_ref[...] + 1), (TI, TI)) - 1

        def chosen(k):
            return jnp.where(lax.broadcasted_iota(jnp.int32, (TI, TI), 0) + k * TI == index, 1.0, 0.0).astype(bf16)

        picked = deep_dot((p0, p1), lambda k: b_ref[0, : 2 * feats, block(k)], chosen, n // TI)[:, :128]
        skel_rows = (picked[:feats] + picked[feats:]).T[:nskel]
        norm_s = jnp.sum(skel_rows * skel_rows, axis=1, keepdims=True)
        sh, sl = split(skel_rows)
        sh, sl = sh.astype(f32) * -2.0, sl.astype(f32) * -2.0
        n1 = norm_s.astype(bf16).astype(f32)
        n2 = (norm_s - n1).astype(bf16).astype(f32)
        lane_s = lax.broadcasted_iota(jnp.int32, (nskel, feats), 1)
        ext_s = jnp.where(lane_s == 0, n1, jnp.where(lane_s == 1, n2, jnp.where(lane_s == 2, norm_s - n1 - n2, jnp.where(lane_s < 6, 1.0, 0.0))))
        probe = jnp.concatenate([sh, sh, sl, ext_s], axis=1).astype(bf16)
        cs = (c0, c1)
        for k in range(n // TI):
            m, r = k % 2, (k // 2) % 2
            pltpu.matmul_push_rhs(b_ref[0, :, block(k)], r, m)
            pltpu.matmul_acc_lhs(cs[m], probe, load_staged_rhs=r)
            h, l = split(matern_of(pltpu.matmul_pop(cs[m])))
            ks_ref[: 3 * nskel, block(k)] = jnp.concatenate([h, l, h], axis=0)
        part = deep_dot((f0, f1), lambda k: ks_ref[: 2 * nskel, block(k)], lambda k: wide(w_ref[0, block(k), :]), n // TI)
        coeff_t = part[:nskel, :rhs] + part[:nskel, rhs : 2 * rhs] + part[nskel:, :rhs] + part[nskel:, rhs : 2 * rhs]
        pad = jnp.zeros((nskel, 128 - feats - rhs - 2), f32)
        ag_ref[pair, my_rows, :] = jnp.concatenate([skel_rows, coeff_t, n1, norm_s - n1, pad], axis=1)
        tmp_ref[...] = jnp.concatenate([skel_rows, jnp.zeros((nskel, 128 - feats), f32)], axis=1)

    my_rows = pl.ds(pl.multiple_of(leaf * nskel, 8), nskel)
    pl.run_scoped(
        skeleton,
        pltpu.ACC(0)((2 * feats, TI), f32), pltpu.ACC(1)((2 * feats, TI), f32),
        pltpu.ACC(0)((nskel, TI), f32), pltpu.ACC(1)((nskel, TI), f32),
        pltpu.ACC(0)((2 * nskel, TI), f32), pltpu.ACC(1)((2 * nskel, TI), f32),
    )

    stage_a = [
        remote(ag_ref.at[pair, my_rows, :], ag_ref.at[pair, my_rows, :], as_sem.at[k], ar_sem.at[k], leaf=leaf_peer(k))
        for k in range(1, nleaf)
    ]
    for c in stage_a:
        c.start()

    stage_b = [
        remote(ag_ref.at[pair], ag_ref.at[pair], bs_sem.at[k], br_sem.at[k], pair=pair_peer(k))
        for k in range(1, npair)
    ]

    def near(x0, x1, y0, y1, r0, r1):
        xs, ys, rs = (x0, x1), (y0, y1), (r0, r1)
        own_block(xs, ys, rs)

        @pl.when(helping)
        def _():
            for ci in range(nc):
                for c in to_help(ci):
                    c.wait_recv()

            @pl.loop(0, n // CH)
            def _(ci):
                cols = pl.ds(pl.multiple_of(ci * CH, CH), CH)
                h, l, _, _, norm = parts(zb_p, cols)
                b_ref[1, :, cols] = as_cols(h, l, norm)
                w_ref[1, cols, :] = as_weights(both_halves(zb_d, cols))

        @pl.loop(0, nc)
        def _(ci):
            @pl.when(ci == 1)
            def _():
                for k, c in enumerate(stage_a, 1):
                    src_rows = pl.ds(pl.multiple_of(lax.rem(leaf + nleaf - k, nleaf) * nskel, 8), nskel)
                    remote(ag_ref.at[pair, src_rows, :], ag_ref.at[pair, src_rows, :], as_sem.at[k], ar_sem.at[k], leaf=leaf_peer(k)).wait_recv()
                for c in stage_a:
                    c.wait_send()
                for c in stage_b:
                    c.start()

            @pl.when(has_pair)
            def _():
                pair_chunk(ci, xs, ys, rs)

    pl.run_scoped(
        near,
        pltpu.ACC(1)((TI, TI), f32), pltpu.ACC(1)((TI, TI), f32),
        pltpu.ACC(0)((rhs, TI), f32), pltpu.ACC(1)((rhs, TI), f32),
        pltpu.ACC(0)((TI, TI), f32), pltpu.ACC(0)((TI, TI), f32),
    )

    @pl.when(helping)
    def _():
        give_rows().start()

    for k, c in enumerate(stage_b, 1):
        src = lax.rem(pair + npair - k, npair)
        remote(ag_ref.at[src], ag_ref.at[src], bs_sem.at[k], br_sem.at[k], pair=pair_peer(k)).wait_recv()
    for c in stage_b:
        c.wait_send()

    def far_field(u0, u1, q0, q1, g0, g1):
        us, qs, gs = (u0, u1), (q0, q1), (g0, g1)
        own_rows = tmp_ref[...]
        own_norm = jnp.sum(own_rows * own_rows, axis=1, keepdims=True)
        oh, ol = split(own_rows)
        lane_o = lax.broadcasted_iota(jnp.int32, (nskel, 128), 1)
        ones = jnp.logical_and(lane_o >= feats + rhs, lane_o < feats + rhs + 2)
        oh = jnp.where(ones, 1.0, oh.astype(f32) * -2.0).astype(bf16)
        ol = (ol.astype(f32) * -2.0).astype(bf16)
        probe = jnp.concatenate([jnp.concatenate([oh, oh], axis=1), jnp.concatenate([ol, jnp.zeros_like(ol)], axis=1)], axis=0)
        blocks = nleaf * nskel // TI
        for p in range(npair):
            for g in range(blocks):
                m = (p * blocks + g) % 2
                both = jnp.concatenate(split(ag_ref[p, block(g), :]), axis=1)
                pltpu.matmul_push_rhs(both, 0, m, transpose=True)
                pltpu.matmul_acc_lhs(us[m], probe, load_staged_rhs=0)
                u = pltpu.matmul_pop(us[m])
                w = matern_of(own_norm + u[:nskel] + u[nskel:])
                column_leaf = lax.div(lax.broadcasted_iota(jnp.int32, (nskel, TI), 1) + g * TI, nskel)
                near_mask = jnp.abs(column_leaf - leaf) <= 1
                same = jnp.full((nskel, TI), pair, jnp.int32) == p
                w = jnp.where(jnp.logical_and(same, near_mask), 0.0, w)
                pltpu.matmul_push_rhs(both, 1, m)
                pltpu.matmul_acc_lhs(qs[m], jnp.concatenate(split(w), axis=0), load_staged_rhs=1)
        q = pltpu.matmul_pop(qs[0]) + pltpu.matmul_pop(qs[1])
        q = q[:, :128] + q[:, 128:]
        q_t = (q[:nskel] + q[nskel:])[:, feats : feats + rhs]
        qh, ql = split(q_t.T)
        probe = wide(jnp.concatenate([qh, qh, ql], axis=1))
        for k in range(n // TI):
            m, r = k % 2, (k // 2) % 2
            pltpu.matmul_push_rhs(ks_ref[:, block(k)], r, m)
            pltpu.matmul_acc_lhs(gs[m], probe, load_staged_rhs=r)
            acc_ref[:, block(k)] += far_weight * pltpu.matmul_pop(gs[m])

    pl.run_scoped(
        far_field,
        pltpu.ACC(0)((2 * nskel, TI), f32), pltpu.ACC(1)((2 * nskel, TI), f32),
        pltpu.ACC(0)((2 * nskel, TI), f32), pltpu.ACC(1)((2 * nskel, TI), f32),
        pltpu.ACC(0)((rhs, TI), f32), pltpu.ACC(1)((rhs, TI), f32),
    )
    amplitude = 1.0 / math.sqrt(3.0 * n)
    direction = dir_ref[...]
    base = nugget * direction + amplitude * acc_ref[...]

    @pl.when(is_main)
    def _():
        pair_part = amplitude * pacc_ref[...]
        product = base + pair_part
        prod_ref[...] = product
        curv_ref[...] = jnp.broadcast_to(jnp.sum(direction * (product + pair_part), axis=1, keepdims=True), (rhs, 128))

    @pl.when(is_help)
    def _():
        prod_ref[...] = base
        curv_ref[...] = jnp.broadcast_to(jnp.sum(direction * base, axis=1, keepdims=True), (rhs, 128))

    @pl.when(helping)
    def _():
        shared = jnp.sum(zb_d[...] * pacc_ref[...], axis=1, keepdims=True)
        curv_ref[...] += jnp.broadcast_to((2.0 * amplitude) * shared, (rhs, 128))

    residual = res_ref[...]
    squares = jnp.sum(residual * residual, axis=1, keepdims=True)
    lane = lax.broadcasted_iota(jnp.int32, (rhs, 128), 1)
    both = jnp.where(lane == 0, squares, jnp.where(lane == 1, curv_ref[...], 0.0))
    both = jnp.concatenate([both, jnp.zeros((128 - rhs, 128), f32)], axis=0).T[0:8, :]
    red_a[leaf] = both
    sends = [
        remote(red_a.at[leaf], red_a.at[leaf], cs_sem.at[k], cr_sem.at[k], leaf=leaf_peer(k))
        for k in range(1, nleaf)
    ]
    for c in sends:
        c.start()
    for k in range(1, nleaf):
        src = lax.rem(leaf + nleaf - k, nleaf)
        remote(red_a.at[src], red_a.at[src], cs_sem.at[k], cr_sem.at[k], leaf=leaf_peer(k)).wait_recv()
    total = red_a[0]
    for k in range(1, nleaf):
        total = total + red_a[k]
    red_b[pair] = total
    sends_b = [
        remote(red_b.at[pair], red_b.at[pair], ds_sem.at[k], dr_sem.at[k], pair=pair_peer(k))
        for k in range(1, npair)
    ]
    for c in sends_b:
        c.start()
    for k in range(1, npair):
        src = lax.rem(pair + npair - k, npair)
        remote(red_b.at[src], red_b.at[src], ds_sem.at[k], dr_sem.at[k], pair=pair_peer(k)).wait_recv()
    total = red_b[0]
    for k in range(1, npair):
        total = total + red_b[k]

    dots_ref[...] = total[0:2, :rhs] * (1.0 / nblk_total)

    def returned(k, ci):
        cols = chunk(ci)
        return remote(ret_out.at[:, cols], ret_in.at[k, :, cols], es_sem.at[ci], er_sem.at[k, ci], leaf=home_leaf, pair=pair)

    @pl.when(back_ok)
    def _():
        give_rows().wait_recv()
        prod_ref[...] += amplitude * ret_in[0]

    @pl.when(is_help)
    def _():
        for ci in range(nc):
            returned(0, ci).wait_recv()
        prod_ref[...] += amplitude * ret_in[0]

    @pl.when(home_two)
    def _():
        for ci in range(nc):
            returned(1, ci).wait_recv()
        prod_ref[...] += amplitude * ret_in[1]

    for c in sends + sends_b:
        c.wait_send()

    @pl.when(has_pair)
    def _():
        for ci in range(nc):
            give_back(ci).wait_send()

    @pl.when(helping)
    def _():
        give_rows().wait_send()

    @pl.when(jnp.logical_and(is_main, chip_two))
    def _():
        for ci in range(nc):
            for c in relay(ci):
                c.wait_send()

    @pl.when(is_help)
    def _():
        for ci in range(nc):
            for c in to_main(ci):
                c.wait_send()

    @pl.when(back_ok)
    def _():
        for ci in range(nc):
            for c in to_help(ci):
                c.wait_send()


def on_device(points, inv_scales, direction, residual, skeleton):
    feats, n = points.shape
    rhs = direction.shape[0]
    nskel = skeleton.shape[1]
    nleaf = lax.axis_size("leaf")
    npair = lax.axis_size("pair")
    vmem = pl.BlockSpec(memory_space=pltpu.VMEM)
    dma = pltpu.SemaphoreType.DMA
    nc = n // CC
    return pl.pallas_call(
        functools.partial(kernel, nleaf, npair, n * nleaf * npair),
        out_shape=(jax.ShapeDtypeStruct((rhs, n), f32), jax.ShapeDtypeStruct((2, rhs), f32)),
        in_specs=[vmem] * 5,
        out_specs=(vmem, vmem),
        scratch_shapes=[
            pltpu.VMEM((feats, n), f32),
            pltpu.VMEM((rhs, n), f32),
            pltpu.VMEM((feats, n), f32),
            pltpu.VMEM((rhs, n), f32),
            pltpu.VMEM((rhs, n), f32),
            pltpu.VMEM((2, rhs, n), f32),
            pltpu.VMEM((2, 4 * feats, n), bf16),
            pltpu.VMEM((n, 4 * feats), bf16),
            pltpu.VMEM((2 * rhs, n), bf16),
            pltpu.VMEM((2, n, 128), bf16),
            pltpu.VMEM((rhs, n), f32),
            pltpu.VMEM((rhs, n), f32),
            pltpu.VMEM((TI, n), bf16),
            pltpu.VMEM((npair, nleaf * nskel, 128), f32),
            pltpu.VMEM((nleaf, 8, 128), f32),
            pltpu.VMEM((npair, 8, 128), f32),
            pltpu.VMEM((nskel, 128), f32),
            pltpu.VMEM((rhs, 128), f32),
            dma((2, nc)), dma((2, nc)),
            dma((2, nc)), dma((2, nc)),
            dma((nc,)), dma((2, nc)),
            dma, dma,
            dma((nleaf,)), dma((nleaf,)),
            dma((npair,)), dma((npair,)),
            dma((nleaf,)), dma((nleaf,)),
            dma((npair,)), dma((npair,)),
        ],
        compiler_params=pltpu.CompilerParams(collective_id=0, has_side_effects=True, vmem_limit_bytes=60 * 1024 * 1024),
        name="matern_step",
    )(points, inv_scales.reshape(1, feats), direction, residual, skeleton)


def solution(mesh):
    return jax.shard_map(
        on_device,
        mesh=mesh,
        in_specs=(
            P(None, ("pair", "leaf")),
            P(),
            P(None, ("pair", "leaf")),
            P(None, ("pair", "leaf")),
            P(("pair", "leaf"), None),
        ),
        out_specs=(P(None, ("pair", "leaf")), P()),
        check_vma=False,
    )
```

```python
import functools
import math

import jax
import jax.numpy as jnp
from jax import lax
from jax.experimental import pallas as pl
from jax.experimental.pallas import tpu as pltpu
from jax.sharding import PartitionSpec as P

root_three = math.sqrt(3.0)
neg_log2e = -1.4426950408889634
nugget = 0.5
far_weight = 0.125
tiny = 1e-30
f32 = jnp.float32
bf16 = jnp.bfloat16
TI = 256
CC = 512
FIRST = 3
CH = 256


def matern_of(u):
    u = jnp.maximum(u, tiny)
    t = u * lax.rsqrt(u)
    return (1.0 + t) * jnp.exp2(t * neg_log2e)


def split(x):
    h = x.astype(bf16)
    return h, (x - h.astype(f32)).astype(bf16)


def kernel(
    nleaf, npair, nblk_total,
    pts_ref, inv_ref, dir_ref, res_ref, skel_ref,
    prod_ref, dots_ref,
    xb_p, xb_d, zb_p, zb_d, ret_out, ret_in, b_ref, st_ref, dd_ref, w_ref, acc_ref, pacc_ref, ks_ref, ag_ref, tg_ref, qo_ref, qi_ref, sz_ref, dz_ref, red_a, red_b, curv_ref,
    hs_sem, hr_sem, fs_sem, fr_sem, es_sem, er_sem, ps_sem, pr_sem, as_sem, ar_sem, bs_sem, br_sem, qs_sem, qr_sem, cs_sem, cr_sem, ds_sem, dr_sem,
):
    feats, n = pts_ref.shape
    rhs = dir_ref.shape[0]
    nskel = skel_ref.shape[1]
    leaf = lax.axis_index("leaf")
    pair = lax.axis_index("pair")

    leaf_odd = lax.rem(leaf, 2)
    pair_odd = lax.rem(pair, 2)
    is_main = leaf_odd == pair_odd
    is_help = leaf_odd != pair_odd
    slot = jnp.where(is_main, 0, 1)
    step = 1 - 2 * leaf_odd
    other = pair + 1 - 2 * pair_odd
    main_pair = jnp.where(is_main, pair, other)
    far_leaf = leaf + 2 * step
    chip_two = jnp.logical_and(far_leaf >= 0, far_leaf < nleaf)
    helping = jnp.logical_and(is_help, chip_two)
    has_pair = jnp.logical_or(is_main, chip_two)
    back_leaf = leaf - 2 * step
    back_ok = jnp.logical_and(is_main, jnp.logical_and(back_leaf >= 0, back_leaf < nleaf))
    home_step = 1 - 2 * pair_odd
    home_leaf = leaf - home_step
    home_far = home_leaf + 2 * home_step
    home_two = jnp.logical_and(is_help, jnp.logical_and(home_far >= 0, home_far < nleaf))

    def remote(src, dst, ss, rs, **dev):
        return pltpu.make_async_remote_copy(
            src_ref=src, dst_ref=dst, send_sem=ss, recv_sem=rs, device_id=dev,
            device_id_type=pl.DeviceIdType.MESH)

    def leaf_peer(k):
        return lax.rem(leaf + k, nleaf)

    def pair_peer(k):
        return lax.rem(pair + k, npair)

    barrier = pltpu.get_barrier_semaphore()

    def greet(**dev):
        pl.semaphore_signal(barrier, inc=1, device_id=dev, device_id_type=pl.DeviceIdType.MESH)

    for k in range(1, nleaf):
        greet(leaf=leaf_peer(k))
    for k in range(1, npair):
        greet(pair=pair_peer(k))

    @pl.when(back_ok)
    def _():
        greet(leaf=back_leaf, pair=other)

    @pl.when(helping)
    def _():
        greet(leaf=far_leaf, pair=other)
        greet(leaf=leaf + step, pair=other)

    @pl.when(home_two)
    def _():
        greet(leaf=home_leaf, pair=other)

    def chunk(ci):
        return pl.ds(pl.multiple_of(ci * CC, CC), CC)

    def block_copies(ci, src_p, src_d, dst_p, dst_d, ss, rs, dev):
        cols = chunk(ci)
        return (
            remote(src_p.at[:, cols], dst_p.at[:, cols], ss.at[0, ci], rs.at[0, ci], **dev),
            remote(src_d.at[:, cols], dst_d.at[:, cols], ss.at[1, ci], rs.at[1, ci], **dev),
        )

    def to_main(ci):
        return block_copies(ci, pts_ref, dir_ref, xb_p, xb_d, hs_sem, hr_sem, dict(leaf=home_leaf, pair=pair))

    def to_help(ci):
        return block_copies(ci, pts_ref, dir_ref, zb_p, zb_d, hs_sem, hr_sem, dict(leaf=back_leaf, pair=other))

    def relay(ci):
        return block_copies(ci, xb_p, xb_d, xb_p, xb_d, fs_sem, fr_sem, dict(leaf=leaf, pair=other))

    def give_back(ci):
        cols = chunk(ci)
        return remote(ret_out.at[:, cols], ret_in.at[slot, :, cols], es_sem.at[ci], er_sem.at[slot, ci], leaf=leaf + step, pair=main_pair)

    def give_rows():
        return remote(pacc_ref, ret_in.at[0], ps_sem, pr_sem, leaf=far_leaf, pair=other)

    nc = n // CC

    def send_block(lo, hi):
        @pl.when(is_help)
        def _():
            for ci in range(lo, hi):
                for c in to_main(ci):
                    c.start()

        @pl.when(back_ok)
        def _():
            for ci in range(lo, hi):
                for c in to_help(ci):
                    c.start()

    eye = lax.broadcasted_iota(jnp.int32, (feats, feats), 0) == lax.broadcasted_iota(jnp.int32, (feats, feats), 1)
    inv_col = jnp.sum(jnp.where(eye, jnp.broadcast_to(inv_ref[...], (feats, feats)), 0.0), axis=1, keepdims=True) * root_three

    def norm_rows(norm):
        n1 = norm.astype(bf16).astype(f32)
        n2 = (norm - n1).astype(bf16).astype(f32)
        return jnp.concatenate([n1, n2, norm - n1 - n2], axis=0)

    def parts(p_src, cols):
        p = p_src[:, cols] * inv_col
        h, l = split(p)
        hf, lf = h.astype(f32), l.astype(f32)
        q = hf + lf
        norm = norm_rows(jnp.sum(q * q, axis=0, keepdims=True))
        return h, l, hf, lf, norm

    def as_cols(h, l, norm):
        w = norm.shape[1]
        ext = jnp.concatenate([jnp.ones((3, w), f32), norm, jnp.zeros((feats - 6, w), f32)], axis=0)
        return jnp.concatenate([h, l, h, ext.astype(bf16)], axis=0)

    def as_rows(hf, lf, norm):
        w = norm.shape[1]
        ext = jnp.concatenate([norm, jnp.ones((3, w), f32), jnp.zeros((feats - 6, w), f32)], axis=0)
        h2 = hf * -2.0
        return jnp.concatenate([h2, h2, lf * -2.0, ext], axis=0).T.astype(bf16)

    def both_halves(d_src, cols):
        return jnp.concatenate(split(d_src[:, cols]), axis=0)

    def as_weights(dd):
        w = dd.shape[1]
        return jnp.concatenate([dd.astype(f32), jnp.zeros((128 - 2 * rhs, w), f32)], axis=0).T.astype(bf16)

    @pl.loop(0, n // CH)
    def _(ci):
        cols = pl.ds(pl.multiple_of(ci * CH, CH), CH)
        h, l, hf, lf, norm = parts(pts_ref, cols)
        b_ref[0, :, cols] = as_cols(h, l, norm)
        st_ref[cols, :] = as_rows(hf, lf, norm)
        dd = both_halves(dir_ref, cols)
        dd_ref[:, cols] = dd
        w_ref[0, cols, :] = as_weights(dd)
        ks_ref[3 * nskel :, cols] = jnp.zeros((TI - 3 * nskel, CH), bf16)
        acc_ref[:, cols] = jnp.zeros((rhs, CH), f32)
        pacc_ref[:, cols] = jnp.zeros((rhs, CH), f32)

    extra = jnp.where(back_ok, 1, 0) + jnp.where(helping, 2, 0) + jnp.where(home_two, 1, 0)
    pl.semaphore_wait(barrier, nleaf - 1 + npair - 1 + extra)

    send_block(0, FIRST)

    nt = n // TI

    def sweep(plan, xs, ys, rs):
        stage = [0, 0]

        def push(v, m):
            k = stage[m]
            stage[m] = 1 - k
            pltpu.matmul_push_rhs(v, k, m)
            return k

        def cross(t):
            pltpu.matmul_acc_lhs(xs[t % 2], plan[t]["rows"](), load_staged_rhs=push(plan[t]["cols"](), 1))

        def spend(t, k):
            p = plan[t]
            if p["turn"] is not None:
                w = p["weights"]()
                w = jnp.concatenate([w, jnp.zeros_like(w)], axis=1)
                pltpu.matmul_acc_lhs(rs[p["turn"]], k, load_staged_rhs=push(w, 0))
            m = t % 2
            dd = p["dd"]()
            pltpu.matmul_acc_lhs(ys[m], dd[:rhs], load_staged_rhs=push(k, m))
            pltpu.matmul_acc_lhs(ys[m], dd[rhs:])

        def finish(t):
            p = plan[t]
            p["out"](pltpu.matmul_pop(ys[t % 2]))
            if p["turned"] is not None:
                r = pltpu.matmul_pop(rs[p["turn"]])[:, :128].T
                p["turned"](r[:rhs] + r[rhs : 2 * rhs])

        count = len(plan)
        cross(0)
        held = None
        for t in range(count + 2):
            k = None
            if t < count:
                k = matern_of(pltpu.matmul_pop(xs[t % 2])).astype(bf16)
            if t + 1 < count:
                cross(t + 1)
            if 0 < t <= count:
                spend(t - 1, held)
            held = k
            if t > 1:
                finish(t - 2)

    def own_block(xs, ys, rs):
        @pl.loop(0, nt // 2)
        def _(k):
            plan = []
            for i in range(2):
                def tile(d, i=i):
                    return pl.ds(pl.multiple_of(lax.rem(2 * k + i + nt - d, nt) * TI, TI), TI)

                def add(cols):
                    def go(v):
                        acc_ref[:, cols] += v
                    return go

                rows = tile(0)
                for d in range(nt // 2 + 1):
                    cols = tile(d)
                    both = 0 < d and 2 * d < nt
                    plan.append(dict(
                        rows=lambda rows=rows: st_ref[rows, :],
                        cols=lambda cols=cols: b_ref[0, :, cols],
                        weights=lambda cols=cols: w_ref[0, cols, :],
                        dd=lambda rows=rows: dd_ref[:, rows],
                        turn=i if both else None,
                        out=add(cols),
                        turned=add(rows) if both and 2 * (d + 1) >= nt else None,
                    ))
            sweep(plan, xs, ys, rs)

    def get_chunk(ci):
        for c in to_main(ci):
            c.wait_recv()

        @pl.when(chip_two)
        def _():
            for c in relay(ci):
                c.start()

    def cross_tile(st, dd, cols, where, turn, turned):
        def add(v):
            pacc_ref[:, cols] += v

        return dict(
            rows=st,
            cols=lambda: b_ref[where, :, cols],
            weights=lambda: w_ref[where, cols, :],
            dd=dd,
            turn=turn,
            out=add,
            turned=turned,
        )

    def main_chunk(ci, xs, ys, rs):
        plan = []
        for i in range(CC // TI):
            rows = pl.ds(pl.multiple_of(ci * CC + i * TI, TI), TI)
            _, _, hf, lf, norm = parts(xb_p, rows)
            st = as_rows(hf, lf, norm)
            dd = both_halves(xb_d, rows)

            def turned(v, rows=rows):
                ret_out[:, rows] = v

            for jt in range(nt):
                cols = slice(jt * TI, (jt + 1) * TI)
                plan.append(cross_tile(lambda st=st: st, lambda dd=dd: dd, cols, 0, i % 2, turned if jt == nt - 1 else None))
        sweep(plan, xs, ys, rs)
        give_back(ci).start()

    def help_columns(ci):
        for c in to_help(ci):
            c.wait_recv()
        for i in range(CC // CH):
            cols = slice(ci * CC + i * CH, ci * CC + (i + 1) * CH)
            h, l, _, _, norm = parts(zb_p, cols)
            b_ref[1, :, cols] = as_cols(h, l, norm)
            w_ref[1, cols, :] = as_weights(both_halves(zb_d, cols))

    def help_rows(ci):
        for c in relay(ci):
            c.wait_recv()
        for i in range(CC // CH):
            rows = slice(ci * CC + i * CH, ci * CC + (i + 1) * CH)
            _, _, hf, lf, norm = parts(xb_p, rows)
            sz_ref[rows, :] = as_rows(hf, lf, norm)
            dz_ref[:, rows] = both_halves(xb_d, rows)

    def help_part(pieces, xs, ys, rs):
        plan = []
        turn = 0
        for it, lo, hi in pieces:
            rows = slice(it * TI, (it + 1) * TI)

            def turned(v, rows=rows, fresh=lo == 0):
                if fresh:
                    ret_out[:, rows] = v
                else:
                    ret_out[:, rows] += v

            for jt in range(lo, hi):
                cols = slice(jt * TI, (jt + 1) * TI)
                plan.append(cross_tile(
                    lambda rows=rows: sz_ref[rows, :], lambda rows=rows: dz_ref[:, rows], cols, 1, turn,
                    turned if jt == hi - 1 else None))
            turn = 1 - turn
        sweep(plan, xs, ys, rs)

    def wide(w):
        return jnp.concatenate([w, jnp.zeros((w.shape[0], TI - w.shape[1]), w.dtype)], axis=1)

    def deep_dot(accs, lhs, rhs_of, count):
        for k in range(count):
            m, r = k % 2, (k // 2) % 2
            pltpu.matmul_push_rhs(rhs_of(k), r, m)
            pltpu.matmul_acc_lhs(accs[m], lhs(k), load_staged_rhs=r)
        return pltpu.matmul_pop(accs[0]) + pltpu.matmul_pop(accs[1])

    def block(k):
        return slice(k * TI, (k + 1) * TI)

    def skeleton(p0, p1, c0, c1, f0, f1):
        index = jnp.broadcast_to(wide(skel_ref[...] + 1), (TI, TI)) - 1

        def chosen(k):
            return jnp.where(lax.broadcasted_iota(jnp.int32, (TI, TI), 0) + k * TI == index, 1.0, 0.0).astype(bf16)

        picked = deep_dot((p0, p1), lambda k: b_ref[0, : 2 * feats, block(k)], chosen, n // TI)[:, :128]
        skel_rows = (picked[:feats] + picked[feats:]).T[:nskel]
        norm_s = jnp.sum(skel_rows * skel_rows, axis=1, keepdims=True)
        sh, sl = split(skel_rows)
        sh, sl = sh.astype(f32) * -2.0, sl.astype(f32) * -2.0
        n1 = norm_s.astype(bf16).astype(f32)
        n2 = (norm_s - n1).astype(bf16).astype(f32)
        lane_s = lax.broadcasted_iota(jnp.int32, (nskel, feats), 1)
        ext_s = jnp.where(lane_s == 0, n1, jnp.where(lane_s == 1, n2, jnp.where(lane_s == 2, norm_s - n1 - n2, jnp.where(lane_s < 6, 1.0, 0.0))))
        probe = jnp.concatenate([sh, sh, sl, ext_s], axis=1).astype(bf16)
        cs = (c0, c1)
        for k in range(n // TI):
            m, r = k % 2, (k // 2) % 2
            pltpu.matmul_push_rhs(b_ref[0, :, block(k)], r, m)
            pltpu.matmul_acc_lhs(cs[m], probe, load_staged_rhs=r)
            h, l = split(matern_of(pltpu.matmul_pop(cs[m])))
            ks_ref[: 3 * nskel, block(k)] = jnp.concatenate([h, l, h], axis=0)
        part = deep_dot((f0, f1), lambda k: ks_ref[: 2 * nskel, block(k)], lambda k: wide(w_ref[0, block(k), :]), n // TI)
        coeff_t = part[:nskel, :rhs] + part[:nskel, rhs : 2 * rhs] + part[nskel:, :rhs] + part[nskel:, rhs : 2 * rhs]
        pad = jnp.zeros((nskel, 128 - feats - rhs - 2), f32)
        pack = jnp.concatenate([skel_rows, coeff_t, n1, norm_s - n1, pad], axis=1)
        ag_ref[my_rows, :] = pack
        tg_ref[pair] = pack

    my_rows = pl.ds(pl.multiple_of(leaf * nskel, 8), nskel)
    pl.run_scoped(
        skeleton,
        pltpu.ACC(0)((2 * feats, TI), f32), pltpu.ACC(1)((2 * feats, TI), f32),
        pltpu.ACC(0)((nskel, TI), f32), pltpu.ACC(1)((nskel, TI), f32),
        pltpu.ACC(0)((2 * nskel, TI), f32), pltpu.ACC(1)((2 * nskel, TI), f32),
    )

    stage_a = [
        remote(ag_ref.at[my_rows, :], ag_ref.at[my_rows, :], as_sem.at[k], ar_sem.at[k], leaf=leaf_peer(k))
        for k in range(1, nleaf)
    ]
    stage_t = [
        remote(tg_ref.at[pair], tg_ref.at[pair], bs_sem.at[k], br_sem.at[k], pair=pair_peer(k))
        for k in range(1, npair)
    ]
    stage_q = [
        remote(qo_ref.at[pair_peer(k)], qi_ref.at[pair], qs_sem.at[k], qr_sem.at[k], pair=pair_peer(k))
        for k in range(1, npair)
    ]
    for c in stage_a + stage_t:
        c.start()
    send_block(FIRST, nc)

    group = TI // (2 * nskel)

    def far_field(xs, rs):
        for k, c in enumerate(stage_a, 1):
            src_rows = pl.ds(pl.multiple_of(lax.rem(leaf + nleaf - k, nleaf) * nskel, 8), nskel)
            remote(ag_ref.at[src_rows, :], ag_ref.at[src_rows, :], as_sem.at[k], ar_sem.at[k], leaf=leaf_peer(k)).wait_recv()
        for k, c in enumerate(stage_t, 1):
            src = lax.rem(pair + npair - k, npair)
            remote(tg_ref.at[src], tg_ref.at[src], bs_sem.at[k], br_sem.at[k], pair=pair_peer(k)).wait_recv()
        lane_o = lax.broadcasted_iota(jnp.int32, (nskel, 128), 1)
        ones = jnp.logical_and(lane_o >= feats + rhs, lane_o < feats + rhs + 2)
        for first in range(0, npair, group):
            probes, norms = [], []
            for p in range(first, first + group):
                target = jnp.where(lane_o < feats, tg_ref[p], 0.0)
                norms.append(jnp.sum(target * target, axis=1, keepdims=True))
                oh, ol = split(target)
                oh = jnp.where(ones, 1.0, oh.astype(f32) * -2.0).astype(bf16)
                ol = (ol.astype(f32) * -2.0).astype(bf16)
                probes += [jnp.concatenate([oh, oh], axis=1), jnp.concatenate([ol, jnp.zeros_like(ol)], axis=1)]
            probe = jnp.concatenate(probes, axis=0)
            for g in range(nleaf * nskel // TI):
                both = jnp.concatenate(split(ag_ref[block(g), :]), axis=1)
                pltpu.matmul_push_rhs(both, 0, 0, transpose=True)
                pltpu.matmul_acc_lhs(rs[0], probe, load_staged_rhs=0)
                u = pltpu.matmul_pop(rs[0])
                near_mask = jnp.abs(lax.div(lax.broadcasted_iota(jnp.int32, (nskel, TI), 1) + g * TI, nskel) - leaf) <= 1
                weights = []
                for i in range(group):
                    lo = 2 * i * nskel
                    w = matern_of(norms[i] + u[lo : lo + nskel] + u[lo + nskel : lo + 2 * nskel])
                    same = jnp.full((nskel, TI), pair, jnp.int32) == first + i
                    weights += list(split(jnp.where(jnp.logical_and(same, near_mask), 0.0, w)))
                pltpu.matmul_push_rhs(both, 0, 1)
                pltpu.matmul_acc_lhs(xs[0], jnp.concatenate(weights, axis=0), load_staged_rhs=0)
            q = pltpu.matmul_pop(xs[0])
            q = q[:, :128] + q[:, 128:]
            for i in range(group):
                lo = 2 * i * nskel
                qo_ref[first + i] = q[lo : lo + nskel] + q[lo + nskel : lo + 2 * nskel]
        for c in stage_q:
            c.start()

    def near(x0, x1, y0, y1, r0, r1):
        xs, ys, rs = (x0, x1), (y0, y1), (r0, r1)
        own_block(xs, ys, rs)

        per = CC // TI

        @pl.when(is_main)
        def _():
            get_chunk(0)

            @pl.loop(0, nc - 1)
            def _(ci):
                get_chunk(ci + 1)
                main_chunk(ci, xs, ys, rs)

        @pl.when(helping)
        def _():
            for ci in range(nc - 1):
                help_columns(ci)
                help_rows(ci)
                if ci == 0:
                    continue
                if ci == 1:
                    pieces = [(it, 0, 2 * per) for it in range(2 * per)]
                else:
                    pieces = [(it, ci * per, (ci + 1) * per) for it in range(ci * per)]
                    pieces += [(it, 0, (ci + 1) * per) for it in range(ci * per, (ci + 1) * per)]
                help_part(pieces, xs, ys, rs)

        far_field(xs, rs)

        @pl.when(is_main)
        def _():
            main_chunk(nc - 1, xs, ys, rs)

        @pl.when(helping)
        def _():
            ci = nc - 1
            help_columns(ci)
            help_rows(ci)
            pieces = [(it, ci * per, (ci + 1) * per) for it in range(ci * per)]
            pieces += [(it, 0, (ci + 1) * per) for it in range(ci * per, (ci + 1) * per)]
            help_part(pieces, xs, ys, rs)
            for c in range(nc):
                give_back(c).start()

    pl.run_scoped(
        near,
        pltpu.ACC(1)((TI, TI), f32), pltpu.ACC(1)((TI, TI), f32),
        pltpu.ACC(0)((rhs, TI), f32), pltpu.ACC(1)((rhs, TI), f32),
        pltpu.ACC(0)((TI, TI), f32), pltpu.ACC(0)((TI, TI), f32),
    )

    @pl.when(helping)
    def _():
        give_rows().start()

    def spread(g0, g1):
        gs = (g0, g1)
        q_t = qo_ref[pair]
        for k in range(1, npair):
            src = lax.rem(pair + npair - k, npair)
            remote(qo_ref.at[src], qi_ref.at[src], qs_sem.at[k], qr_sem.at[k], pair=pair_peer(k)).wait_recv()
            q_t = q_t + qi_ref[src]
        qh, ql = split(q_t[:, feats : feats + rhs].T)
        probe = wide(jnp.concatenate([qh, qh, ql], axis=1))
        for k in range(n // TI):
            m, r = k % 2, (k // 2) % 2
            pltpu.matmul_push_rhs(ks_ref[:, block(k)], r, m)
            pltpu.matmul_acc_lhs(gs[m], probe, load_staged_rhs=r)
            acc_ref[:, block(k)] += far_weight * pltpu.matmul_pop(gs[m])

    pl.run_scoped(spread, pltpu.ACC(0)((rhs, TI), f32), pltpu.ACC(1)((rhs, TI), f32))
    amplitude = 1.0 / math.sqrt(3.0 * n)
    direction = dir_ref[...]
    base = nugget * direction + amplitude * acc_ref[...]

    @pl.when(is_main)
    def _():
        pair_part = amplitude * pacc_ref[...]
        product = base + pair_part
        prod_ref[...] = product
        curv_ref[...] = jnp.broadcast_to(jnp.sum(direction * (product + pair_part), axis=1, keepdims=True), (rhs, 128))

    @pl.when(is_help)
    def _():
        prod_ref[...] = base
        curv_ref[...] = jnp.broadcast_to(jnp.sum(direction * base, axis=1, keepdims=True), (rhs, 128))

    @pl.when(helping)
    def _():
        shared = jnp.sum(zb_d[...] * pacc_ref[...], axis=1, keepdims=True)
        curv_ref[...] += jnp.broadcast_to((2.0 * amplitude) * shared, (rhs, 128))

    residual = res_ref[...]
    squares = jnp.sum(residual * residual, axis=1, keepdims=True)
    lane = lax.broadcasted_iota(jnp.int32, (rhs, 128), 1)
    both = jnp.where(lane == 0, squares, jnp.where(lane == 1, curv_ref[...], 0.0))
    both = jnp.concatenate([both, jnp.zeros((128 - rhs, 128), f32)], axis=0).T[0:8, :]
    red_a[leaf] = both
    sends = [
        remote(red_a.at[leaf], red_a.at[leaf], cs_sem.at[k], cr_sem.at[k], leaf=leaf_peer(k))
        for k in range(1, nleaf)
    ]
    for c in sends:
        c.start()
    for k in range(1, nleaf):
        src = lax.rem(leaf + nleaf - k, nleaf)
        remote(red_a.at[src], red_a.at[src], cs_sem.at[k], cr_sem.at[k], leaf=leaf_peer(k)).wait_recv()
    total = red_a[0]
    for k in range(1, nleaf):
        total = total + red_a[k]
    red_b[pair] = total
    sends_b = [
        remote(red_b.at[pair], red_b.at[pair], ds_sem.at[k], dr_sem.at[k], pair=pair_peer(k))
        for k in range(1, npair)
    ]
    for c in sends_b:
        c.start()
    for k in range(1, npair):
        src = lax.rem(pair + npair - k, npair)
        remote(red_b.at[src], red_b.at[src], ds_sem.at[k], dr_sem.at[k], pair=pair_peer(k)).wait_recv()
    total = red_b[0]
    for k in range(1, npair):
        total = total + red_b[k]

    dots_ref[...] = total[0:2, :rhs] * (1.0 / nblk_total)

    def returned(k, ci):
        cols = chunk(ci)
        return remote(ret_out.at[:, cols], ret_in.at[k, :, cols], es_sem.at[ci], er_sem.at[k, ci], leaf=home_leaf, pair=pair)

    @pl.when(back_ok)
    def _():
        give_rows().wait_recv()
        prod_ref[...] += amplitude * ret_in[0]

    @pl.when(is_help)
    def _():
        for ci in range(nc):
            returned(0, ci).wait_recv()
        prod_ref[...] += amplitude * ret_in[0]

    @pl.when(home_two)
    def _():
        for ci in range(nc):
            returned(1, ci).wait_recv()
        prod_ref[...] += amplitude * ret_in[1]

    for c in sends + sends_b + stage_a + stage_t + stage_q:
        c.wait_send()

    @pl.when(has_pair)
    def _():
        for ci in range(nc):
            give_back(ci).wait_send()

    @pl.when(helping)
    def _():
        give_rows().wait_send()

    @pl.when(jnp.logical_and(is_main, chip_two))
    def _():
        for ci in range(nc):
            for c in relay(ci):
                c.wait_send()

    @pl.when(is_help)
    def _():
        for ci in range(nc):
            for c in to_main(ci):
                c.wait_send()

    @pl.when(back_ok)
    def _():
        for ci in range(nc):
            for c in to_help(ci):
                c.wait_send()


def on_device(points, inv_scales, direction, residual, skeleton):
    feats, n = points.shape
    rhs = direction.shape[0]
    nskel = skeleton.shape[1]
    nleaf = lax.axis_size("leaf")
    npair = lax.axis_size("pair")
    vmem = pl.BlockSpec(memory_space=pltpu.VMEM)
    dma = pltpu.SemaphoreType.DMA
    nc = n // CC
    return pl.pallas_call(
        functools.partial(kernel, nleaf, npair, n * nleaf * npair),
        out_shape=(jax.ShapeDtypeStruct((rhs, n), f32), jax.ShapeDtypeStruct((2, rhs), f32)),
        in_specs=[vmem] * 5,
        out_specs=(vmem, vmem),
        scratch_shapes=[
            pltpu.VMEM((feats, n), f32),
            pltpu.VMEM((rhs, n), f32),
            pltpu.VMEM((feats, n), f32),
            pltpu.VMEM((rhs, n), f32),
            pltpu.VMEM((rhs, n), f32),
            pltpu.VMEM((2, rhs, n), f32),
            pltpu.VMEM((2, 4 * feats, n), bf16),
            pltpu.VMEM((n, 4 * feats), bf16),
            pltpu.VMEM((2 * rhs, n), bf16),
            pltpu.VMEM((2, n, 128), bf16),
            pltpu.VMEM((rhs, n), f32),
            pltpu.VMEM((rhs, n), f32),
            pltpu.VMEM((TI, n), bf16),
            pltpu.VMEM((nleaf * nskel, 128), f32),
            pltpu.VMEM((npair, nskel, 128), f32),
            pltpu.VMEM((npair, nskel, 128), f32),
            pltpu.VMEM((npair, nskel, 128), f32),
            pltpu.VMEM((n, 4 * feats), bf16),
            pltpu.VMEM((2 * rhs, n), bf16),
            pltpu.VMEM((nleaf, 8, 128), f32),
            pltpu.VMEM((npair, 8, 128), f32),
            pltpu.VMEM((rhs, 128), f32),
            dma((2, nc)), dma((2, nc)),
            dma((2, nc)), dma((2, nc)),
            dma((nc,)), dma((2, nc)),
            dma, dma,
            dma((nleaf,)), dma((nleaf,)),
            dma((npair,)), dma((npair,)),
            dma((npair,)), dma((npair,)),
            dma((nleaf,)), dma((nleaf,)),
            dma((npair,)), dma((npair,)),
        ],
        compiler_params=pltpu.CompilerParams(collective_id=0, has_side_effects=True, vmem_limit_bytes=60 * 1024 * 1024),
        name="matern_step",
    )(points, inv_scales.reshape(1, feats), direction, residual, skeleton)


def solution(mesh):
    return jax.shard_map(
        on_device,
        mesh=mesh,
        in_specs=(
            P(None, ("pair", "leaf")),
            P(),
            P(None, ("pair", "leaf")),
            P(None, ("pair", "leaf")),
            P(("pair", "leaf"), None),
        ),
        out_specs=(P(None, ("pair", "leaf")), P()),
        check_vma=False,
    )
```

```python
import functools
import math

import jax
import jax.numpy as jnp
from jax import lax
from jax.experimental import pallas as pl
from jax.experimental.pallas import tpu as pltpu
from jax.sharding import PartitionSpec as P

root_three = math.sqrt(3.0)
neg_log2e = -1.4426950408889634
nugget = 0.5
far_weight = 0.125
tiny = 1e-30
f32 = jnp.float32
bf16 = jnp.bfloat16
TI = 256
CC = 512
FIRST = 4
EARLY = 2
CH = 256


def matern_of(u):
    u = jnp.maximum(u, tiny)
    t = u * lax.rsqrt(u)
    return (1.0 + t) * jnp.exp2(t * neg_log2e)


def split(x):
    h = x.astype(bf16)
    return h, (x - h.astype(f32)).astype(bf16)


def kernel(
    nleaf, npair,
    pts_hbm, inv_hbm, dir_hbm, res_hbm, skel_hbm,
    prod_hbm, dots_hbm,
    pts_ref, inv_ref, dir_ref, res_ref, skel_ref, prod_ref, dots_ref,
    xb_p, xb_d, zb_p, zb_d, ret_out, ret_in, b_ref, st_ref, dd_ref, w_ref, acc_ref, pacc_ref, ks_ref, ag_ref, tg_ref, qo_ref, qi_ref, sz_ref, dz_ref, red_a, red_b, curv_ref,
    in_sem, out_sem, hs_sem, hr_sem, fs_sem, fr_sem, es_sem, er_sem, ps_sem, pr_sem, as_sem, ar_sem, bs_sem, br_sem, qs_sem, qr_sem, cs_sem, cr_sem, ds_sem, dr_sem,
):
    feats, n = pts_ref.shape
    rhs = dir_ref.shape[0]
    nskel = skel_ref.shape[1]
    leaf = lax.axis_index("leaf")
    pair = lax.axis_index("pair")

    leaf_odd = lax.rem(leaf, 2)
    pair_odd = lax.rem(pair, 2)
    is_main = leaf_odd == pair_odd
    is_help = leaf_odd != pair_odd
    slot = jnp.where(is_main, 0, 1)
    step = 1 - 2 * leaf_odd
    other = pair + 1 - 2 * pair_odd
    main_pair = jnp.where(is_main, pair, other)
    far_leaf = leaf + 2 * step
    chip_two = jnp.logical_and(far_leaf >= 0, far_leaf < nleaf)
    helping = jnp.logical_and(is_help, chip_two)
    has_pair = jnp.logical_or(is_main, chip_two)
    back_leaf = leaf - 2 * step
    back_ok = jnp.logical_and(is_main, jnp.logical_and(back_leaf >= 0, back_leaf < nleaf))
    home_step = 1 - 2 * pair_odd
    home_leaf = leaf - home_step
    home_far = home_leaf + 2 * home_step
    home_two = jnp.logical_and(is_help, jnp.logical_and(home_far >= 0, home_far < nleaf))

    def remote(src, dst, ss, rs, **dev):
        return pltpu.make_async_remote_copy(
            src_ref=src, dst_ref=dst, send_sem=ss, recv_sem=rs, device_id=dev,
            device_id_type=pl.DeviceIdType.MESH)

    def leaf_peer(k):
        return lax.rem(leaf + k, nleaf)

    def pair_peer(k):
        return lax.rem(pair + k, npair)

    loads = [
        pltpu.make_async_copy(src, dst, in_sem.at[k])
        for k, (src, dst) in enumerate((
            (inv_hbm, inv_ref), (pts_hbm, pts_ref), (dir_hbm, dir_ref), (skel_hbm, skel_ref), (res_hbm, res_ref)))
    ]
    for c in loads:
        c.start()

    barrier = pltpu.get_barrier_semaphore()

    def greet(**dev):
        pl.semaphore_signal(barrier, inc=1, device_id=dev, device_id_type=pl.DeviceIdType.MESH)

    for k in range(1, nleaf):
        greet(leaf=leaf_peer(k))
    for k in range(1, npair):
        greet(pair=pair_peer(k))

    @pl.when(back_ok)
    def _():
        greet(leaf=back_leaf, pair=other)

    @pl.when(helping)
    def _():
        greet(leaf=far_leaf, pair=other)
        greet(leaf=leaf + step, pair=other)

    @pl.when(home_two)
    def _():
        greet(leaf=home_leaf, pair=other)

    def chunk(ci):
        return pl.ds(pl.multiple_of(ci * CC, CC), CC)

    def block_copies(ci, src_p, src_d, dst_p, dst_d, ss, rs, dev):
        cols = chunk(ci)
        return (
            remote(src_p.at[:, cols], dst_p.at[:, cols], ss.at[0, ci], rs.at[0, ci], **dev),
            remote(src_d.at[:, cols], dst_d.at[:, cols], ss.at[1, ci], rs.at[1, ci], **dev),
        )

    def to_main(ci):
        return block_copies(ci, pts_ref, dir_ref, xb_p, xb_d, hs_sem, hr_sem, dict(leaf=home_leaf, pair=pair))

    def to_help(ci):
        return block_copies(ci, pts_ref, dir_ref, zb_p, zb_d, hs_sem, hr_sem, dict(leaf=back_leaf, pair=other))

    def relay(ci):
        return block_copies(ci, xb_p, xb_d, xb_p, xb_d, fs_sem, fr_sem, dict(leaf=leaf, pair=other))

    def give_back(ci):
        cols = chunk(ci)
        return remote(ret_out.at[:, cols], ret_in.at[slot, :, cols], es_sem.at[ci], er_sem.at[slot, ci], leaf=leaf + step, pair=main_pair)

    def give_rows(ci):
        cols = chunk(ci)
        return remote(pacc_ref.at[:, cols], ret_in.at[0, :, cols], ps_sem.at[ci], pr_sem.at[ci], leaf=far_leaf, pair=other)

    nc = n // CC

    def send_block(lo, hi):
        @pl.when(is_help)
        def _():
            for ci in range(lo, hi):
                for c in to_main(ci):
                    c.start()

        @pl.when(back_ok)
        def _():
            for ci in range(lo, hi):
                for c in to_help(ci):
                    c.start()

    for c in loads[:4]:
        c.wait()

    eye = lax.broadcasted_iota(jnp.int32, (feats, feats), 0) == lax.broadcasted_iota(jnp.int32, (feats, feats), 1)
    inv_col = jnp.sum(jnp.where(eye, jnp.broadcast_to(inv_ref[...], (feats, feats)), 0.0), axis=1, keepdims=True) * root_three

    def norm_rows(norm):
        n1 = norm.astype(bf16).astype(f32)
        n2 = (norm - n1).astype(bf16).astype(f32)
        return jnp.concatenate([n1, n2, norm - n1 - n2], axis=0)

    def parts(p_src, cols):
        p = p_src[:, cols] * inv_col
        h, l = split(p)
        hf, lf = h.astype(f32), l.astype(f32)
        q = hf + lf
        norm = norm_rows(jnp.sum(q * q, axis=0, keepdims=True))
        return h, l, hf, lf, norm

    def as_cols(h, l, norm):
        w = norm.shape[1]
        ext = jnp.concatenate([jnp.ones((3, w), f32), norm, jnp.zeros((feats - 6, w), f32)], axis=0)
        return jnp.concatenate([h, l, h, ext.astype(bf16)], axis=0)

    def as_rows(hf, lf, norm):
        w = norm.shape[1]
        ext = jnp.concatenate([norm, jnp.ones((3, w), f32), jnp.zeros((feats - 6, w), f32)], axis=0)
        h2 = hf * -2.0
        return jnp.concatenate([h2, h2, lf * -2.0, ext], axis=0).T.astype(bf16)

    def both_halves(d_src, cols):
        return jnp.concatenate(split(d_src[:, cols]), axis=0)

    def as_weights(dd):
        w = dd.shape[1]
        return jnp.concatenate([dd.astype(f32), jnp.zeros((128 - 2 * rhs, w), f32)], axis=0).T.astype(bf16)

    def prepare(ci):
        cols = pl.ds(pl.multiple_of(ci * CH, CH), CH)
        h, l, hf, lf, norm = parts(pts_ref, cols)
        b_ref[0, :, cols] = as_cols(h, l, norm)
        st_ref[cols, :] = as_rows(hf, lf, norm)
        dd = both_halves(dir_ref, cols)
        dd_ref[:, cols] = dd
        w_ref[0, cols, :] = as_weights(dd)
        ks_ref[3 * nskel :, cols] = jnp.zeros((TI - 3 * nskel, CH), bf16)
        acc_ref[:, cols] = jnp.zeros((rhs, CH), f32)
        pacc_ref[:, cols] = jnp.zeros((rhs, CH), f32)

    pl.loop(0, EARLY)(prepare)

    extra = jnp.where(back_ok, 1, 0) + jnp.where(helping, 2, 0) + jnp.where(home_two, 1, 0)
    pl.semaphore_wait(barrier, nleaf - 1 + npair - 1 + extra)

    send_block(0, FIRST)

    pl.loop(EARLY, n // CH)(prepare)

    nt = n // TI

    def sweep(plan, xs, ys, rs):
        stage = [0, 0]

        def push(v, m):
            k = stage[m]
            stage[m] = 1 - k
            pltpu.matmul_push_rhs(v, k, m)
            return k

        def cross(t):
            pltpu.matmul_acc_lhs(xs[t % 2], plan[t]["rows"](), load_staged_rhs=push(plan[t]["cols"](), 1))

        def spend(t, k):
            p = plan[t]
            if p["turn"] is not None:
                w = p["weights"]()
                w = jnp.concatenate([w, jnp.zeros_like(w)], axis=1)
                pltpu.matmul_acc_lhs(rs[p["turn"]], k, load_staged_rhs=push(w, 0))
            m = t % 2
            dd = p["dd"]()
            pltpu.matmul_acc_lhs(ys[m], dd[:rhs], load_staged_rhs=push(k, m))
            pltpu.matmul_acc_lhs(ys[m], dd[rhs:])

        def finish(t):
            p = plan[t]
            p["out"](pltpu.matmul_pop(ys[t % 2]))
            if p["turned"] is not None:
                r = pltpu.matmul_pop(rs[p["turn"]])[:, :128].T
                p["turned"](r[:rhs] + r[rhs : 2 * rhs])
            for go in p.get("then", ()):
                go()

        count = len(plan)
        cross(0)
        held = None
        for t in range(count + 2):
            k = None
            if t < count:
                k = matern_of(pltpu.matmul_pop(xs[t % 2])).astype(bf16)
            if t + 1 < count:
                cross(t + 1)
            if 0 < t <= count:
                spend(t - 1, held)
            held = k
            if t > 1:
                finish(t - 2)

    def get_chunk(ci):
        for c in to_main(ci):
            c.wait_recv()

        @pl.when(chip_two)
        def _():
            for c in relay(ci):
                c.start()

    def own_block(xs, ys, rs):
        @pl.loop(0, nt // 2)
        def _(k):
            @pl.when(jnp.logical_and(is_main, k == nt // 2 - 1))
            def _():
                get_chunk(0)

            plan = []
            for i in range(2):
                def tile(d, i=i):
                    return pl.ds(pl.multiple_of(lax.rem(2 * k + i + nt - d, nt) * TI, TI), TI)

                def add(cols):
                    def go(v):
                        acc_ref[:, cols] += v
                    return go

                rows = tile(0)
                for d in range(nt // 2 + 1):
                    cols = tile(d)
                    both = 0 < d and 2 * d < nt
                    plan.append(dict(
                        rows=lambda rows=rows: st_ref[rows, :],
                        cols=lambda cols=cols: b_ref[0, :, cols],
                        weights=lambda cols=cols: w_ref[0, cols, :],
                        dd=lambda rows=rows: dd_ref[:, rows],
                        turn=i if both else None,
                        out=add(cols),
                        turned=add(rows) if both and 2 * (d + 1) >= nt else None,
                    ))
            sweep(plan, xs, ys, rs)

    def cross_tile(st, dd, cols, where, turn, turned):
        def add(v):
            pacc_ref[:, cols] += v

        return dict(
            rows=st,
            cols=lambda: b_ref[where, :, cols],
            weights=lambda: w_ref[where, cols, :],
            dd=dd,
            turn=turn,
            out=add,
            turned=turned,
        )

    def main_chunk(ci, xs, ys, rs):
        plan = []
        for i in range(CC // TI):
            rows = pl.ds(pl.multiple_of(ci * CC + i * TI, TI), TI)
            _, _, hf, lf, norm = parts(xb_p, rows)
            st = as_rows(hf, lf, norm)
            dd = both_halves(xb_d, rows)

            def turned(v, rows=rows):
                ret_out[:, rows] = v

            for jt in range(nt):
                cols = slice(jt * TI, (jt + 1) * TI)
                plan.append(cross_tile(lambda st=st: st, lambda dd=dd: dd, cols, 0, i % 2, turned if jt == nt - 1 else None))
        sweep(plan, xs, ys, rs)
        give_back(ci).start()

    def help_columns(ci):
        for c in to_help(ci):
            c.wait_recv()
        for i in range(CC // CH):
            cols = slice(ci * CC + i * CH, ci * CC + (i + 1) * CH)
            h, l, _, _, norm = parts(zb_p, cols)
            b_ref[1, :, cols] = as_cols(h, l, norm)
            w_ref[1, cols, :] = as_weights(both_halves(zb_d, cols))

    def help_rows(ci):
        for c in relay(ci):
            c.wait_recv()
        for i in range(CC // CH):
            rows = slice(ci * CC + i * CH, ci * CC + (i + 1) * CH)
            _, _, hf, lf, norm = parts(xb_p, rows)
            sz_ref[rows, :] = as_rows(hf, lf, norm)
            dz_ref[:, rows] = both_halves(xb_d, rows)

    def help_part(ci, xs, ys, rs):
        per = CC // TI
        last = ci == nc - 1
        early, late = ci * per, (ci + 1) * per
        pieces = [(it, 0, early) for it in range(early, late)] if ci else []
        pieces += [(it, early, late) for it in range(early)]
        pieces += [(it, early, late) for it in range(early, late)]
        done = {}
        if last:
            done[per - 1] = [give_rows(c) for c in range(ci)]
            done[per + early - 1] = [give_back(c) for c in range(ci)]
            done[len(pieces) - 1] = [give_back(ci), give_rows(ci)]
        plan = []
        for k, (it, lo, hi) in enumerate(pieces):
            rows = slice(it * TI, (it + 1) * TI)

            def turned(v, rows=rows, fresh=lo == 0):
                if fresh:
                    ret_out[:, rows] = v
                else:
                    ret_out[:, rows] += v

            for jt in range(lo, hi):
                cols = slice(jt * TI, (jt + 1) * TI)
                plan.append(cross_tile(
                    lambda rows=rows: sz_ref[rows, :], lambda rows=rows: dz_ref[:, rows], cols, 1, k % 2,
                    turned if jt == hi - 1 else None))
            plan[-1]["then"] = [c.start for c in done.get(k, ())]
        sweep(plan, xs, ys, rs)

    def wide(w):
        return jnp.concatenate([w, jnp.zeros((w.shape[0], TI - w.shape[1]), w.dtype)], axis=1)

    def deep_dot(accs, lhs, rhs_of, count):
        for k in range(count):
            m, r = k % 2, (k // 2) % 2
            pltpu.matmul_push_rhs(rhs_of(k), r, m)
            pltpu.matmul_acc_lhs(accs[m], lhs(k), load_staged_rhs=r)
        return pltpu.matmul_pop(accs[0]) + pltpu.matmul_pop(accs[1])

    def block(k):
        return slice(k * TI, (k + 1) * TI)

    def skeleton(p0, p1, c0, c1, f0, f1):
        index = jnp.broadcast_to(wide(skel_ref[...] + 1), (TI, TI)) - 1

        def chosen(k):
            return jnp.where(lax.broadcasted_iota(jnp.int32, (TI, TI), 0) + k * TI == index, 1.0, 0.0).astype(bf16)

        picked = deep_dot((p0, p1), lambda k: b_ref[0, : 2 * feats, block(k)], chosen, n // TI)[:, :128]
        skel_rows = (picked[:feats] + picked[feats:]).T[:nskel]
        norm_s = jnp.sum(skel_rows * skel_rows, axis=1, keepdims=True)
        sh, sl = split(skel_rows)
        sh, sl = sh.astype(f32) * -2.0, sl.astype(f32) * -2.0
        n1 = norm_s.astype(bf16).astype(f32)
        n2 = (norm_s - n1).astype(bf16).astype(f32)
        lane_s = lax.broadcasted_iota(jnp.int32, (nskel, feats), 1)
        ext_s = jnp.where(lane_s == 0, n1, jnp.where(lane_s == 1, n2, jnp.where(lane_s == 2, norm_s - n1 - n2, jnp.where(lane_s < 6, 1.0, 0.0))))
        probe = jnp.concatenate([sh, sh, sl, ext_s], axis=1).astype(bf16)
        cs = (c0, c1)
        for k in range(n // TI):
            m, r = k % 2, (k // 2) % 2
            pltpu.matmul_push_rhs(b_ref[0, :, block(k)], r, m)
            pltpu.matmul_acc_lhs(cs[m], probe, load_staged_rhs=r)
            h, l = split(matern_of(pltpu.matmul_pop(cs[m])))
            ks_ref[: 3 * nskel, block(k)] = jnp.concatenate([h, l, h], axis=0)
        part = deep_dot((f0, f1), lambda k: ks_ref[: 2 * nskel, block(k)], lambda k: wide(w_ref[0, block(k), :]), n // TI)
        coeff_t = part[:nskel, :rhs] + part[:nskel, rhs : 2 * rhs] + part[nskel:, :rhs] + part[nskel:, rhs : 2 * rhs]
        pad = jnp.zeros((nskel, 128 - feats - rhs - 2), f32)
        pack = jnp.concatenate([skel_rows, coeff_t, n1, norm_s - n1, pad], axis=1)
        ag_ref[my_rows, :] = pack
        tg_ref[pair] = pack

    my_rows = pl.ds(pl.multiple_of(leaf * nskel, 8), nskel)
    pl.run_scoped(
        skeleton,
        pltpu.ACC(0)((2 * feats, TI), f32), pltpu.ACC(1)((2 * feats, TI), f32),
        pltpu.ACC(0)((nskel, TI), f32), pltpu.ACC(1)((nskel, TI), f32),
        pltpu.ACC(0)((2 * nskel, TI), f32), pltpu.ACC(1)((2 * nskel, TI), f32),
    )

    stage_a = [
        remote(ag_ref.at[my_rows, :], ag_ref.at[my_rows, :], as_sem.at[k], ar_sem.at[k], leaf=leaf_peer(k))
        for k in range(1, nleaf)
    ]
    stage_t = [
        remote(tg_ref.at[pair], tg_ref.at[pair], bs_sem.at[k], br_sem.at[k], pair=pair_peer(k))
        for k in range(1, npair)
    ]
    stage_q = [
        remote(qo_ref.at[pair_peer(k)], qi_ref.at[pair], qs_sem.at[k], qr_sem.at[k], pair=pair_peer(k))
        for k in range(1, npair)
    ]
    for c in stage_a + stage_t:
        c.start()
    send_block(FIRST, nc)

    group = TI // (2 * nskel)

    def far_field(xs, rs):
        for k, c in enumerate(stage_a, 1):
            src_rows = pl.ds(pl.multiple_of(lax.rem(leaf + nleaf - k, nleaf) * nskel, 8), nskel)
            remote(ag_ref.at[src_rows, :], ag_ref.at[src_rows, :], as_sem.at[k], ar_sem.at[k], leaf=leaf_peer(k)).wait_recv()
        for k, c in enumerate(stage_t, 1):
            src = lax.rem(pair + npair - k, npair)
            remote(tg_ref.at[src], tg_ref.at[src], bs_sem.at[k], br_sem.at[k], pair=pair_peer(k)).wait_recv()
        lane_o = lax.broadcasted_iota(jnp.int32, (nskel, 128), 1)
        ones = jnp.logical_and(lane_o >= feats + rhs, lane_o < feats + rhs + 2)
        for first in range(0, npair, group):
            probes, norms = [], []
            for p in range(first, first + group):
                target = jnp.where(lane_o < feats, tg_ref[p], 0.0)
                norms.append(jnp.sum(target * target, axis=1, keepdims=True))
                oh, ol = split(target)
                oh = jnp.where(ones, 1.0, oh.astype(f32) * -2.0).astype(bf16)
                ol = (ol.astype(f32) * -2.0).astype(bf16)
                probes += [jnp.concatenate([oh, oh], axis=1), jnp.concatenate([ol, jnp.zeros_like(ol)], axis=1)]
            probe = jnp.concatenate(probes, axis=0)
            for g in range(nleaf * nskel // TI):
                both = jnp.concatenate(split(ag_ref[block(g), :]), axis=1)
                pltpu.matmul_push_rhs(both, 0, 0, transpose=True)
                pltpu.matmul_acc_lhs(rs[0], probe, load_staged_rhs=0)
                u = pltpu.matmul_pop(rs[0])
                near_mask = jnp.abs(lax.div(lax.broadcasted_iota(jnp.int32, (nskel, TI), 1) + g * TI, nskel) - leaf) <= 1
                weights = []
                for i in range(group):
                    lo = 2 * i * nskel
                    w = matern_of(norms[i] + u[lo : lo + nskel] + u[lo + nskel : lo + 2 * nskel])
                    same = jnp.full((nskel, TI), pair, jnp.int32) == first + i
                    weights += list(split(jnp.where(jnp.logical_and(same, near_mask), 0.0, w)))
                pltpu.matmul_push_rhs(both, 0, 1)
                pltpu.matmul_acc_lhs(xs[0], jnp.concatenate(weights, axis=0), load_staged_rhs=0)
            q = pltpu.matmul_pop(xs[0])
            q = q[:, :128] + q[:, 128:]
            for i in range(group):
                lo = 2 * i * nskel
                qo_ref[first + i] = q[lo : lo + nskel] + q[lo + nskel : lo + 2 * nskel]
        for c in stage_q:
            c.start()

    def near(x0, x1, y0, y1, r0, r1):
        xs, ys, rs = (x0, x1), (y0, y1), (r0, r1)
        own_block(xs, ys, rs)

        @pl.when(is_main)
        def _():
            @pl.loop(0, nc - 1)
            def _(ci):
                get_chunk(ci + 1)
                main_chunk(ci, xs, ys, rs)

        @pl.when(helping)
        def _():
            for ci in range(nc - 1):
                help_columns(ci)
                help_rows(ci)
                help_part(ci, xs, ys, rs)

        far_field(xs, rs)

        @pl.when(is_main)
        def _():
            main_chunk(nc - 1, xs, ys, rs)

        @pl.when(helping)
        def _():
            help_columns(nc - 1)
            help_rows(nc - 1)
            help_part(nc - 1, xs, ys, rs)

    pl.run_scoped(
        near,
        pltpu.ACC(1)((TI, TI), f32), pltpu.ACC(1)((TI, TI), f32),
        pltpu.ACC(0)((rhs, TI), f32), pltpu.ACC(1)((rhs, TI), f32),
        pltpu.ACC(0)((TI, TI), f32), pltpu.ACC(0)((TI, TI), f32),
    )

    def spread(g0, g1):
        gs = (g0, g1)
        q_t = qo_ref[pair]
        for k in range(1, npair):
            src = lax.rem(pair + npair - k, npair)
            remote(qo_ref.at[src], qi_ref.at[src], qs_sem.at[k], qr_sem.at[k], pair=pair_peer(k)).wait_recv()
            q_t = q_t + qi_ref[src]
        qh, ql = split(q_t[:, feats : feats + rhs].T)
        probe = wide(jnp.concatenate([qh, qh, ql], axis=1))
        for k in range(n // TI):
            m, r = k % 2, (k // 2) % 2
            pltpu.matmul_push_rhs(ks_ref[:, block(k)], r, m)
            pltpu.matmul_acc_lhs(gs[m], probe, load_staged_rhs=r)
            acc_ref[:, block(k)] += far_weight * pltpu.matmul_pop(gs[m])

    pl.run_scoped(spread, pltpu.ACC(0)((rhs, TI), f32), pltpu.ACC(1)((rhs, TI), f32))
    amplitude = 1.0 / math.sqrt(3.0 * n)
    direction = dir_ref[...]
    base = nugget * direction + amplitude * acc_ref[...]

    @pl.when(is_main)
    def _():
        pair_part = amplitude * pacc_ref[...]
        prod_ref[...] = base + pair_part
        curv_ref[...] = jnp.broadcast_to(jnp.sum(direction * (base + 2.0 * pair_part), axis=1, keepdims=True), (rhs, 128))

    @pl.when(is_help)
    def _():
        prod_ref[...] = base
        curv_ref[...] = jnp.broadcast_to(jnp.sum(direction * base, axis=1, keepdims=True), (rhs, 128))

    @pl.when(helping)
    def _():
        shared = jnp.sum(zb_d[...] * pacc_ref[...], axis=1, keepdims=True)
        curv_ref[...] += jnp.broadcast_to((2.0 * amplitude) * shared, (rhs, 128))

    loads[4].wait()
    residual = res_ref[...]
    squares = jnp.sum(residual * residual, axis=1, keepdims=True)
    lane = lax.broadcasted_iota(jnp.int32, (rhs, 128), 1)
    both = jnp.where(lane == 0, squares, jnp.where(lane == 1, curv_ref[...], 0.0))
    both = jnp.concatenate([both, jnp.zeros((128 - rhs, 128), f32)], axis=0).T
    both = jnp.concatenate([both[0:1, :rhs], both[1:2, :rhs], jnp.zeros((1, 128 - 2 * rhs), f32)], axis=1)
    one_stage = nleaf * npair <= 64
    sends_b = []
    if one_stage:
        def partial(l, p):
            return red_a.at[p * nleaf + l]

        red_a[pair * nleaf + leaf] = both
        hops = [(a, b) for b in range(npair) for a in range(nleaf) if a or b]
        sends = [
            remote(partial(leaf, pair), partial(leaf, pair), cs_sem.at[a, b], cr_sem.at[a, b], leaf=leaf_peer(a), pair=pair_peer(b))
            for a, b in hops
        ]
    else:
        red_a[leaf] = both
        sends = [
            remote(red_a.at[leaf], red_a.at[leaf], cs_sem.at[k, 0], cr_sem.at[k, 0], leaf=leaf_peer(k))
            for k in range(1, nleaf)
        ]
    for c in sends:
        c.start()

    def returned(k, ci):
        cols = chunk(ci)
        return remote(ret_out.at[:, cols], ret_in.at[k, :, cols], es_sem.at[ci], er_sem.at[k, ci], leaf=home_leaf, pair=pair)

    @pl.when(back_ok)
    def _():
        for ci in range(nc):
            give_rows(ci).wait_recv()
        prod_ref[...] += amplitude * ret_in[0]

    @pl.when(is_help)
    def _():
        for ci in range(nc):
            returned(0, ci).wait_recv()
        prod_ref[...] += amplitude * ret_in[0]

    @pl.when(home_two)
    def _():
        for ci in range(nc):
            returned(1, ci).wait_recv()
        prod_ref[...] += amplitude * ret_in[1]

    store = pltpu.make_async_copy(prod_ref, prod_hbm, out_sem)
    store.start()

    if one_stage:
        for a, b in hops:
            src = partial(lax.rem(leaf + nleaf - a, nleaf), lax.rem(pair + npair - b, npair))
            remote(src, src, cs_sem.at[a, b], cr_sem.at[a, b], leaf=leaf_peer(a), pair=pair_peer(b)).wait_recv()
        total = jnp.sum(red_a[...], axis=0)
    else:
        for k in range(1, nleaf):
            src = lax.rem(leaf + nleaf - k, nleaf)
            remote(red_a.at[src], red_a.at[src], cs_sem.at[k, 0], cr_sem.at[k, 0], leaf=leaf_peer(k)).wait_recv()
        red_b[pair] = jnp.sum(red_a[:nleaf], axis=0)
        sends_b = [
            remote(red_b.at[pair], red_b.at[pair], ds_sem.at[k], dr_sem.at[k], pair=pair_peer(k))
            for k in range(1, npair)
        ]
        for c in sends_b:
            c.start()
        for k in range(1, npair):
            src = lax.rem(pair + npair - k, npair)
            remote(red_b.at[src], red_b.at[src], ds_sem.at[k], dr_sem.at[k], pair=pair_peer(k)).wait_recv()
        total = jnp.sum(red_b[...], axis=0)
    total = total * (1.0 / (n * nleaf * npair))
    dots_ref[...] = jnp.concatenate([total[:, :rhs], total[:, rhs : 2 * rhs]], axis=0)
    store_dots = pltpu.make_async_copy(dots_ref, dots_hbm, in_sem.at[0])
    store_dots.start()

    for c in sends + sends_b + stage_a + stage_t + stage_q:
        c.wait_send()

    @pl.when(has_pair)
    def _():
        for ci in range(nc):
            give_back(ci).wait_send()

    @pl.when(helping)
    def _():
        for ci in range(nc):
            give_rows(ci).wait_send()

    @pl.when(jnp.logical_and(is_main, chip_two))
    def _():
        for ci in range(nc):
            for c in relay(ci):
                c.wait_send()

    @pl.when(is_help)
    def _():
        for ci in range(nc):
            for c in to_main(ci):
                c.wait_send()

    @pl.when(back_ok)
    def _():
        for ci in range(nc):
            for c in to_help(ci):
                c.wait_send()

    store.wait()
    store_dots.wait()


def on_device(points, inv_scales, direction, residual, skeleton):
    feats, n = points.shape
    rhs = direction.shape[0]
    nskel = skeleton.shape[1]
    nleaf = lax.axis_size("leaf")
    npair = lax.axis_size("pair")
    anywhere = pl.BlockSpec(memory_space=pl.ANY)
    dma = pltpu.SemaphoreType.DMA
    nc = n // CC
    return pl.pallas_call(
        functools.partial(kernel, nleaf, npair),
        out_shape=(jax.ShapeDtypeStruct((rhs, n), f32), jax.ShapeDtypeStruct((2, rhs), f32)),
        in_specs=[pl.BlockSpec(memory_space=pltpu.HBM)] * 5,
        out_specs=(anywhere, anywhere),
        scratch_shapes=[
            pltpu.VMEM((feats, n), f32),
            pltpu.VMEM((1, feats), f32),
            pltpu.VMEM((rhs, n), f32),
            pltpu.VMEM((rhs, n), f32),
            pltpu.VMEM((1, nskel), jnp.int32),
            pltpu.VMEM((rhs, n), f32),
            pltpu.VMEM((2, rhs), f32),
            pltpu.VMEM((feats, n), f32),
            pltpu.VMEM((rhs, n), f32),
            pltpu.VMEM((feats, n), f32),
            pltpu.VMEM((rhs, n), f32),
            pltpu.VMEM((rhs, n), f32),
            pltpu.VMEM((2, rhs, n), f32),
            pltpu.VMEM((2, 4 * feats, n), bf16),
            pltpu.VMEM((n, 4 * feats), bf16),
            pltpu.VMEM((2 * rhs, n), bf16),
            pltpu.VMEM((2, n, 128), bf16),
            pltpu.VMEM((rhs, n), f32),
            pltpu.VMEM((rhs, n), f32),
            pltpu.VMEM((TI, n), bf16),
            pltpu.VMEM((nleaf * nskel, 128), f32),
            pltpu.VMEM((npair, nskel, 128), f32),
            pltpu.VMEM((npair, nskel, 128), f32),
            pltpu.VMEM((npair, nskel, 128), f32),
            pltpu.VMEM((n, 4 * feats), bf16),
            pltpu.VMEM((2 * rhs, n), bf16),
            pltpu.VMEM((nleaf * npair if nleaf * npair <= 64 else nleaf, 1, 128), f32),
            pltpu.VMEM((npair, 1, 128), f32),
            pltpu.VMEM((rhs, 128), f32),
            dma((5,)), dma,
            dma((2, nc)), dma((2, nc)),
            dma((2, nc)), dma((2, nc)),
            dma((nc,)), dma((2, nc)),
            dma((nc,)), dma((nc,)),
            dma((nleaf,)), dma((nleaf,)),
            dma((npair,)), dma((npair,)),
            dma((npair,)), dma((npair,)),
            dma((nleaf, npair)), dma((nleaf, npair)),
            dma((npair,)), dma((npair,)),
        ],
        compiler_params=pltpu.CompilerParams(collective_id=0, has_side_effects=True, vmem_limit_bytes=40 * 1024 * 1024),
        name="matern_step",
    )(*[pltpu.with_memory_space_constraint(v, pltpu.HBM) for v in (points, inv_scales.reshape(1, feats), direction, residual, skeleton)])


def solution(mesh):
    return jax.shard_map(
        on_device,
        mesh=mesh,
        in_specs=(
            P(None, ("pair", "leaf")),
            P(),
            P(None, ("pair", "leaf")),
            P(None, ("pair", "leaf")),
            P(("pair", "leaf"), None),
        ),
        out_specs=(P(None, ("pair", "leaf")), P()),
        check_vma=False,
    )
```

```python
import functools
import math

import jax
import jax.numpy as jnp
from jax import lax
from jax.experimental import pallas as pl
from jax.experimental.pallas import tpu as pltpu
from jax.sharding import PartitionSpec as P

root_three = math.sqrt(3.0)
neg_log2e = -1.4426950408889634
nugget = 0.5
far_weight = 0.125
tiny = 1e-30
f32 = jnp.float32
bf16 = jnp.bfloat16
TI = 256
CC = 512
FIRST = 3
EARLY = 2
AHEAD = 8
CH = 256


def matern_of(u):
    u = jnp.maximum(u, tiny)
    t = u * lax.rsqrt(u)
    return (1.0 + t) * jnp.exp2(t * neg_log2e)


def split(x):
    h = x.astype(bf16)
    return h, (x - h.astype(f32)).astype(bf16)


def kernel(
    nleaf, npair,
    pts_hbm, inv_hbm, dir_hbm, res_hbm, skel_hbm,
    prod_hbm, dots_hbm,
    pts_ref, inv_ref, dir_ref, res_ref, skel_ref, prod_ref, dots_ref,
    xb_p, xb_d, zb_p, zb_d, ret_out, fwd_ref, ret_in, b_ref, st_ref, dd_ref, w_ref, acc_ref, pacc_ref, ks_ref, ag_ref, tg_ref, qo_ref, qi_ref, sz_ref, dz_ref, red_a, red_b, curv_ref,
    in_sem, out_sem, hs_sem, hr_sem, fs_sem, fr_sem, es_sem, er_sem, gs_sem, gr_sem, ps_sem, pr_sem, as_sem, ar_sem, bs_sem, br_sem, qs_sem, qr_sem, cs_sem, cr_sem, ds_sem, dr_sem,
):
    feats, n = pts_ref.shape
    rhs = dir_ref.shape[0]
    nskel = skel_ref.shape[1]
    leaf = lax.axis_index("leaf")
    pair = lax.axis_index("pair")

    leaf_odd = lax.rem(leaf, 2)
    pair_odd = lax.rem(pair, 2)
    is_main = leaf_odd == pair_odd
    is_help = leaf_odd != pair_odd
    step = 1 - 2 * leaf_odd
    other = pair + 1 - 2 * pair_odd
    far_leaf = leaf + 2 * step
    chip_two = jnp.logical_and(far_leaf >= 0, far_leaf < nleaf)
    helping = jnp.logical_and(is_help, chip_two)
    back_leaf = leaf - 2 * step
    back_ok = jnp.logical_and(is_main, jnp.logical_and(back_leaf >= 0, back_leaf < nleaf))
    home_step = 1 - 2 * pair_odd
    home_leaf = leaf - home_step
    home_far = home_leaf + 2 * home_step
    home_two = jnp.logical_and(is_help, jnp.logical_and(home_far >= 0, home_far < nleaf))

    def remote(src, dst, ss, rs, **dev):
        return pltpu.make_async_remote_copy(
            src_ref=src, dst_ref=dst, send_sem=ss, recv_sem=rs, device_id=dev,
            device_id_type=pl.DeviceIdType.MESH)

    def leaf_peer(k):
        return lax.rem(leaf + k, nleaf)

    def pair_peer(k):
        return lax.rem(pair + k, npair)

    loads = [
        pltpu.make_async_copy(src, dst, in_sem.at[k])
        for k, (src, dst) in enumerate((
            (inv_hbm, inv_ref), (pts_hbm, pts_ref), (dir_hbm, dir_ref), (skel_hbm, skel_ref), (res_hbm, res_ref)))
    ]
    for c in loads:
        c.start()

    barrier = pltpu.get_barrier_semaphore()

    def greet(**dev):
        pl.semaphore_signal(barrier, inc=1, device_id=dev, device_id_type=pl.DeviceIdType.MESH)

    for k in range(1, nleaf):
        greet(leaf=leaf_peer(k))
    for k in range(1, npair):
        greet(pair=pair_peer(k))

    @pl.when(back_ok)
    def _():
        greet(leaf=back_leaf, pair=other)

    @pl.when(helping)
    def _():
        greet(leaf=far_leaf, pair=other)

    def chunk(ci):
        return pl.ds(pl.multiple_of(ci * CC, CC), CC)

    def block_copies(ci, src_p, src_d, dst_p, dst_d, ss, rs, dev):
        cols = chunk(ci)
        return (
            remote(src_p.at[:, cols], dst_p.at[:, cols], ss.at[0, ci], rs.at[0, ci], **dev),
            remote(src_d.at[:, cols], dst_d.at[:, cols], ss.at[1, ci], rs.at[1, ci], **dev),
        )

    def to_main(ci):
        return block_copies(ci, pts_ref, dir_ref, xb_p, xb_d, hs_sem, hr_sem, dict(leaf=home_leaf, pair=pair))

    def to_help(ci):
        return block_copies(ci, pts_ref, dir_ref, zb_p, zb_d, hs_sem, hr_sem, dict(leaf=back_leaf, pair=other))

    def relay(ci):
        return block_copies(ci, xb_p, xb_d, xb_p, xb_d, fs_sem, fr_sem, dict(leaf=leaf, pair=other))

    def give_back(ci):
        cols = chunk(ci)
        return remote(ret_out.at[:, cols], ret_in.at[0, :, cols], es_sem.at[ci], er_sem.at[0, ci], leaf=leaf + step, pair=pair)

    def hand_over(ci):
        cols = chunk(ci)
        return remote(ret_out.at[:, cols], fwd_ref.at[:, cols], es_sem.at[ci], gr_sem.at[ci], leaf=leaf, pair=other)

    def forward(ci):
        cols = chunk(ci)
        return remote(fwd_ref.at[:, cols], ret_in.at[1, :, cols], gs_sem.at[ci], er_sem.at[1, ci], leaf=leaf + step, pair=pair)

    def give_rows(ci):
        cols = chunk(ci)
        return remote(pacc_ref.at[:, cols], ret_in.at[0, :, cols], ps_sem.at[ci], pr_sem.at[ci], leaf=far_leaf, pair=other)

    nc = n // CC

    def send_block(lo, hi):
        @pl.when(is_help)
        def _():
            for ci in range(lo, hi):
                for c in to_main(ci):
                    c.start()

        @pl.when(back_ok)
        def _():
            for ci in range(lo, hi):
                for c in to_help(ci):
                    c.start()

    for c in loads[:4]:
        c.wait()

    eye = lax.broadcasted_iota(jnp.int32, (feats, feats), 0) == lax.broadcasted_iota(jnp.int32, (feats, feats), 1)
    inv_col = jnp.sum(jnp.where(eye, jnp.broadcast_to(inv_ref[...], (feats, feats)), 0.0), axis=1, keepdims=True) * root_three

    def norm_rows(norm):
        n1 = norm.astype(bf16).astype(f32)
        n2 = (norm - n1).astype(bf16).astype(f32)
        return jnp.concatenate([n1, n2, norm - n1 - n2], axis=0)

    def parts(p_src, cols):
        p = p_src[:, cols] * inv_col
        h, l = split(p)
        hf, lf = h.astype(f32), l.astype(f32)
        q = hf + lf
        norm = norm_rows(jnp.sum(q * q, axis=0, keepdims=True))
        return h, l, hf, lf, norm

    def as_cols(h, l, norm):
        w = norm.shape[1]
        ext = jnp.concatenate([jnp.ones((3, w), f32), norm, jnp.zeros((feats - 6, w), f32)], axis=0)
        return jnp.concatenate([h, l, h, ext.astype(bf16)], axis=0)

    def as_rows(hf, lf, norm):
        w = norm.shape[1]
        ext = jnp.concatenate([norm, jnp.ones((3, w), f32), jnp.zeros((feats - 6, w), f32)], axis=0)
        h2 = hf * -2.0
        return jnp.concatenate([h2, h2, lf * -2.0, ext], axis=0).T.astype(bf16)

    def both_halves(d_src, cols):
        return jnp.concatenate(split(d_src[:, cols]), axis=0)

    def as_weights(dd):
        w = dd.shape[1]
        return jnp.concatenate([dd.astype(f32), jnp.zeros((128 - 2 * rhs, w), f32)], axis=0).T.astype(bf16)

    def prepare(ci):
        cols = pl.ds(pl.multiple_of(ci * CH, CH), CH)
        h, l, hf, lf, norm = parts(pts_ref, cols)
        b_ref[0, :, cols] = as_cols(h, l, norm)
        st_ref[cols, :] = as_rows(hf, lf, norm)
        dd = both_halves(dir_ref, cols)
        dd_ref[:, cols] = dd
        w_ref[0, cols, :] = as_weights(dd)
        ks_ref[3 * nskel :, cols] = jnp.zeros((TI - 3 * nskel, CH), bf16)
        acc_ref[:, cols] = jnp.zeros((rhs, CH), f32)
        pacc_ref[:, cols] = jnp.zeros((rhs, CH), f32)

    pl.loop(0, EARLY)(prepare)

    extra = jnp.where(jnp.logical_or(back_ok, helping), 1, 0)
    pl.semaphore_wait(barrier, nleaf - 1 + npair - 1 + extra)

    send_block(0, FIRST)

    pl.loop(EARLY, n // CH)(prepare)

    nt = n // TI

    def sweep(plan, xs, ys, rs):
        stage = [0, 0]

        def push(v, m):
            k = stage[m]
            stage[m] = 1 - k
            pltpu.matmul_push_rhs(v, k, m)
            return k

        def cross(t):
            for go in plan[t].get("first", ()):
                go()
            pltpu.matmul_acc_lhs(xs[t % 2], plan[t]["rows"](), load_staged_rhs=push(plan[t]["cols"](), 1))

        def spend(t, k):
            p = plan[t]
            if p["turn"] is not None:
                w = p["weights"]()
                w = jnp.concatenate([w, jnp.zeros_like(w)], axis=1)
                pltpu.matmul_acc_lhs(rs[p["turn"]], k, load_staged_rhs=push(w, 0))
            m = t % 2
            dd = p["dd"]()
            pltpu.matmul_acc_lhs(ys[m], dd[:rhs], load_staged_rhs=push(k, m))
            pltpu.matmul_acc_lhs(ys[m], dd[rhs:])

        def finish(t):
            p = plan[t]
            p["out"](pltpu.matmul_pop(ys[t % 2]))
            if p["turned"] is not None:
                r = pltpu.matmul_pop(rs[p["turn"]])[:, :128].T
                p["turned"](r[:rhs] + r[rhs : 2 * rhs])
            for go in p.get("then", ()):
                go()

        count = len(plan)
        cross(0)
        held = None
        for t in range(count + 2):
            k = None
            if t < count:
                k = matern_of(pltpu.matmul_pop(xs[t % 2])).astype(bf16)
            if t + 1 < count:
                cross(t + 1)
            if 0 < t <= count:
                spend(t - 1, held)
            held = k
            if t > 1:
                finish(t - 2)

    def get_chunk(ci):
        for c in to_main(ci):
            c.wait_recv()
        for c in relay(ci):
            c.start()

    def own_block(xs, ys, rs):
        half = nt // 2

        def rows_pair(k, reach):
            plan = []
            for i in range(2):
                def tile(d, i=i):
                    return pl.ds(pl.multiple_of(lax.rem(2 * k + i + nt - d, nt) * TI, TI), TI)

                def add(cols):
                    def go(v):
                        acc_ref[:, cols] += v
                    return go

                rows = tile(0)
                for d in range(reach + 1):
                    cols = tile(d)
                    plan.append(dict(
                        rows=lambda rows=rows: st_ref[rows, :],
                        cols=lambda cols=cols: b_ref[0, :, cols],
                        weights=lambda cols=cols: w_ref[0, cols, :],
                        dd=lambda rows=rows: dd_ref[:, rows],
                        turn=i if d else None,
                        out=add(cols),
                        turned=add(rows) if d == reach else None,
                    ))
            sweep(plan, xs, ys, rs)

        pl.loop(0, half // 2)(lambda k: rows_pair(k, half))

        @pl.loop(half // 2, half)
        def _(k):
            @pl.when(jnp.logical_and(is_main, k == half - 1))
            def _():
                get_chunk(0)

            rows_pair(k, half - 1)

    def cross_tile(st, dd, cols, where, turn, turned):
        def add(v):
            pacc_ref[:, cols] += v

        return dict(
            rows=st,
            cols=lambda: b_ref[where, :, cols],
            weights=lambda: w_ref[where, cols, :],
            dd=dd,
            turn=turn,
            out=add,
            turned=turned,
        )

    def main_chunk(ci, xs, ys, rs, ahead=False):
        plan = []
        for i in range(CC // TI):
            rows = pl.ds(pl.multiple_of(ci * CC + i * TI, TI), TI)
            _, _, hf, lf, norm = parts(xb_p, rows)
            st = as_rows(hf, lf, norm)
            dd = both_halves(xb_d, rows)

            def turned(v, rows=rows):
                ret_out[:, rows] = v

            for jt in range(nt):
                cols = slice(jt * TI, (jt + 1) * TI)
                plan.append(cross_tile(lambda st=st: st, lambda dd=dd: dd, cols, 0, i % 2, turned if jt == nt - 1 else None))
        if ahead:
            plan[AHEAD]["first"] = [lambda: get_chunk(ci + 1)]
        sweep(plan, xs, ys, rs)
        give_back(ci).start()

    def help_columns(ci):
        for c in to_help(ci):
            c.wait_recv()
        for i in range(CC // CH):
            cols = slice(ci * CC + i * CH, ci * CC + (i + 1) * CH)
            h, l, _, _, norm = parts(zb_p, cols)
            b_ref[1, :, cols] = as_cols(h, l, norm)
            w_ref[1, cols, :] = as_weights(both_halves(zb_d, cols))

    def help_rows(ci):
        for c in relay(ci):
            c.wait_recv()
        for i in range(CC // CH):
            rows = slice(ci * CC + i * CH, ci * CC + (i + 1) * CH)
            _, _, hf, lf, norm = parts(xb_p, rows)
            sz_ref[rows, :] = as_rows(hf, lf, norm)
            dz_ref[:, rows] = both_halves(xb_d, rows)

    def help_part(ci, xs, ys, rs):
        per = CC // TI
        last = ci == nc - 1
        early, late = ci * per, (ci + 1) * per
        plan = []

        def add_tile(it, jt, ends, fresh):
            rows = slice(it * TI, (it + 1) * TI)

            def turned(v):
                if fresh:
                    ret_out[:, rows] = v
                else:
                    ret_out[:, rows] += v

            plan.append(cross_tile(
                lambda: sz_ref[rows, :], lambda: dz_ref[:, rows], slice(jt * TI, (jt + 1) * TI), 1, it % 2,
                turned if ends else None))

        for it in range(early):
            for jt in range(early, late):
                add_tile(it, jt, jt == late - 1, False)
        if last:
            plan[-1]["then"] = [hand_over(c).start for c in range(ci)]
        start = len(plan)
        for c in range(ci + 1):
            for it in range(early, late):
                for jt in range(c * per, (c + 1) * per):
                    add_tile(it, jt, c == ci and jt == late - 1, True)
            if last:
                plan[-1]["then"] = [give_rows(c).start]
        if last:
            plan[-1]["then"].append(hand_over(ci).start)
        plan[start]["first"] = [lambda: help_rows(ci)]
        sweep(plan, xs, ys, rs)

    def wide(w):
        return jnp.concatenate([w, jnp.zeros((w.shape[0], TI - w.shape[1]), w.dtype)], axis=1)

    def deep_dot(accs, lhs, rhs_of, count):
        for k in range(count):
            m, r = k % 2, (k // 2) % 2
            pltpu.matmul_push_rhs(rhs_of(k), r, m)
            pltpu.matmul_acc_lhs(accs[m], lhs(k), load_staged_rhs=r)
        return pltpu.matmul_pop(accs[0]) + pltpu.matmul_pop(accs[1])

    def block(k):
        return slice(k * TI, (k + 1) * TI)

    def skeleton(p0, p1, c0, c1, f0, f1):
        index = jnp.broadcast_to(wide(skel_ref[...] + 1), (TI, TI)) - 1

        def chosen(k):
            return jnp.where(lax.broadcasted_iota(jnp.int32, (TI, TI), 0) + k * TI == index, 1.0, 0.0).astype(bf16)

        picked = deep_dot((p0, p1), lambda k: b_ref[0, : 2 * feats, block(k)], chosen, n // TI)[:, :128]
        skel_rows = (picked[:feats] + picked[feats:]).T[:nskel]
        norm_s = jnp.sum(skel_rows * skel_rows, axis=1, keepdims=True)
        sh, sl = split(skel_rows)
        sh, sl = sh.astype(f32) * -2.0, sl.astype(f32) * -2.0
        n1 = norm_s.astype(bf16).astype(f32)
        n2 = (norm_s - n1).astype(bf16).astype(f32)
        lane_s = lax.broadcasted_iota(jnp.int32, (nskel, feats), 1)
        ext_s = jnp.where(lane_s == 0, n1, jnp.where(lane_s == 1, n2, jnp.where(lane_s == 2, norm_s - n1 - n2, jnp.where(lane_s < 6, 1.0, 0.0))))
        probe = jnp.concatenate([sh, sh, sl, ext_s], axis=1).astype(bf16)
        cs = (c0, c1)
        for k in range(n // TI):
            m, r = k % 2, (k // 2) % 2
            pltpu.matmul_push_rhs(b_ref[0, :, block(k)], r, m)
            pltpu.matmul_acc_lhs(cs[m], probe, load_staged_rhs=r)
            h, l = split(matern_of(pltpu.matmul_pop(cs[m])))
            ks_ref[: 3 * nskel, block(k)] = jnp.concatenate([h, l, h], axis=0)
        part = deep_dot((f0, f1), lambda k: ks_ref[: 2 * nskel, block(k)], lambda k: wide(w_ref[0, block(k), :]), n // TI)
        coeff_t = part[:nskel, :rhs] + part[:nskel, rhs : 2 * rhs] + part[nskel:, :rhs] + part[nskel:, rhs : 2 * rhs]
        pad = jnp.zeros((nskel, 128 - feats - rhs - 2), f32)
        pack = jnp.concatenate([skel_rows, coeff_t, n1, norm_s - n1, pad], axis=1)
        ag_ref[my_rows, :] = pack
        tg_ref[pair] = pack

    my_rows = pl.ds(pl.multiple_of(leaf * nskel, 8), nskel)
    pl.run_scoped(
        skeleton,
        pltpu.ACC(0)((2 * feats, TI), f32), pltpu.ACC(1)((2 * feats, TI), f32),
        pltpu.ACC(0)((nskel, TI), f32), pltpu.ACC(1)((nskel, TI), f32),
        pltpu.ACC(0)((2 * nskel, TI), f32), pltpu.ACC(1)((2 * nskel, TI), f32),
    )

    stage_a = [
        remote(ag_ref.at[my_rows, :], ag_ref.at[my_rows, :], as_sem.at[k], ar_sem.at[k], leaf=leaf_peer(k))
        for k in range(1, nleaf)
    ]
    stage_t = [
        remote(tg_ref.at[pair], tg_ref.at[pair], bs_sem.at[k], br_sem.at[k], pair=pair_peer(k))
        for k in range(1, npair)
    ]
    stage_q = [
        remote(qo_ref.at[pair_peer(k)], qi_ref.at[pair], qs_sem.at[k], qr_sem.at[k], pair=pair_peer(k))
        for k in range(1, npair)
    ]
    for c in stage_a + stage_t:
        c.start()
    send_block(FIRST, nc)

    group = TI // (2 * nskel)

    def far_field(xs, rs):
        for k, c in enumerate(stage_a, 1):
            src_rows = pl.ds(pl.multiple_of(lax.rem(leaf + nleaf - k, nleaf) * nskel, 8), nskel)
            remote(ag_ref.at[src_rows, :], ag_ref.at[src_rows, :], as_sem.at[k], ar_sem.at[k], leaf=leaf_peer(k)).wait_recv()
        for k, c in enumerate(stage_t, 1):
            src = lax.rem(pair + npair - k, npair)
            remote(tg_ref.at[src], tg_ref.at[src], bs_sem.at[k], br_sem.at[k], pair=pair_peer(k)).wait_recv()
        lane_o = lax.broadcasted_iota(jnp.int32, (nskel, 128), 1)
        ones = jnp.logical_and(lane_o >= feats + rhs, lane_o < feats + rhs + 2)
        for first in range(0, npair, group):
            probes, norms = [], []
            for p in range(first, first + group):
                target = jnp.where(lane_o < feats, tg_ref[p], 0.0)
                norms.append(jnp.sum(target * target, axis=1, keepdims=True))
                oh, ol = split(target)
                oh = jnp.where(ones, 1.0, oh.astype(f32) * -2.0).astype(bf16)
                ol = (ol.astype(f32) * -2.0).astype(bf16)
                probes += [jnp.concatenate([oh, oh], axis=1), jnp.concatenate([ol, jnp.zeros_like(ol)], axis=1)]
            probe = jnp.concatenate(probes, axis=0)
            for g in range(nleaf * nskel // TI):
                both = jnp.concatenate(split(ag_ref[block(g), :]), axis=1)
                pltpu.matmul_push_rhs(both, 0, 0, transpose=True)
                pltpu.matmul_acc_lhs(rs[0], probe, load_staged_rhs=0)
                u = pltpu.matmul_pop(rs[0])
                near_mask = jnp.abs(lax.div(lax.broadcasted_iota(jnp.int32, (nskel, TI), 1) + g * TI, nskel) - leaf) <= 1
                weights = []
                for i in range(group):
                    lo = 2 * i * nskel
                    w = matern_of(norms[i] + u[lo : lo + nskel] + u[lo + nskel : lo + 2 * nskel])
                    same = jnp.full((nskel, TI), pair, jnp.int32) == first + i
                    weights += list(split(jnp.where(jnp.logical_and(same, near_mask), 0.0, w)))
                pltpu.matmul_push_rhs(both, 0, 1)
                pltpu.matmul_acc_lhs(xs[0], jnp.concatenate(weights, axis=0), load_staged_rhs=0)
            q = pltpu.matmul_pop(xs[0])
            q = q[:, :128] + q[:, 128:]
            for i in range(group):
                lo = 2 * i * nskel
                qo_ref[first + i] = q[lo : lo + nskel] + q[lo + nskel : lo + 2 * nskel]
        for c in stage_q:
            c.start()

    amplitude = 1.0 / math.sqrt(3.0 * n)
    lane = lax.broadcasted_iota(jnp.int32, (rhs, 128), 1)

    def near(x0, x1, y0, y1, r0, r1):
        xs, ys, rs = (x0, x1), (y0, y1), (r0, r1)
        own_block(xs, ys, rs)
        loads[4].wait()
        squares = jnp.sum(res_ref[...] * res_ref[...], axis=1, keepdims=True)
        curvature = jnp.sum(dir_ref[...] * (nugget * dir_ref[...] + amplitude * acc_ref[...]), axis=1, keepdims=True)
        curv_ref[...] = jnp.where(lane == 0, squares, jnp.where(lane == 1, curvature, 0.0))

        @pl.when(is_main)
        def _():
            @pl.loop(0, nc - 2)
            def _(ci):
                main_chunk(ci, xs, ys, rs, ahead=True)

            main_chunk(nc - 2, xs, ys, rs)

        @pl.when(helping)
        def _():
            for ci in range(nc - 1):
                help_columns(ci)
                help_part(ci, xs, ys, rs)

        far_field(xs, rs)

        @pl.when(is_main)
        def _():
            get_chunk(nc - 1)
            main_chunk(nc - 1, xs, ys, rs)

        @pl.when(helping)
        def _():
            help_columns(nc - 1)
            help_part(nc - 1, xs, ys, rs)

    pl.run_scoped(
        near,
        pltpu.ACC(1)((TI, TI), f32), pltpu.ACC(1)((TI, TI), f32),
        pltpu.ACC(0)((rhs, TI), f32), pltpu.ACC(1)((rhs, TI), f32),
        pltpu.ACC(0)((TI, TI), f32), pltpu.ACC(0)((TI, TI), f32),
    )

    def add_pair(d_ref):
        shared = jnp.sum(d_ref[...] * pacc_ref[...], axis=1, keepdims=True)
        curv_ref[...] += jnp.where(lane == 1, (2.0 * amplitude) * shared, 0.0)

    @pl.when(is_main)
    def _():
        add_pair(dir_ref)

    @pl.when(helping)
    def _():
        add_pair(zb_d)

    q_t = qo_ref[pair]
    for k in range(1, npair):
        src = lax.rem(pair + npair - k, npair)
        remote(qo_ref.at[src], qi_ref.at[src], qs_sem.at[k], qr_sem.at[k], pair=pair_peer(k)).wait_recv()
        q_t = q_t + qi_ref[src]
    far_row = (amplitude * far_weight) * jnp.sum(q_t * tg_ref[pair], axis=0, keepdims=True)[:, feats : feats + rhs]
    both = jnp.concatenate([curv_ref[...], jnp.zeros((128 - rhs, 128), f32)], axis=0).T
    both = jnp.concatenate([both[0:1, :rhs], both[1:2, :rhs] + far_row, jnp.zeros((1, 128 - 2 * rhs), f32)], axis=1)
    one_stage = nleaf * npair <= 64
    sends_b = []
    if one_stage:
        def partial(l, p):
            return red_a.at[p * nleaf + l]

        red_a[pair * nleaf + leaf] = both
        hops = [(a, b) for b in range(npair) for a in range(nleaf) if a or b]
        sends = [
            remote(partial(leaf, pair), partial(leaf, pair), cs_sem.at[a, b], cr_sem.at[a, b], leaf=leaf_peer(a), pair=pair_peer(b))
            for a, b in hops
        ]
    else:
        red_a[leaf] = both
        sends = [
            remote(red_a.at[leaf], red_a.at[leaf], cs_sem.at[k, 0], cr_sem.at[k, 0], leaf=leaf_peer(k))
            for k in range(1, nleaf)
        ]
    for c in sends:
        c.start()

    def spread(g0, g1):
        gs = (g0, g1)
        qh, ql = split(q_t[:, feats : feats + rhs].T)
        probe = wide(jnp.concatenate([qh, qh, ql], axis=1))
        for k in range(n // TI):
            m, r = k % 2, (k // 2) % 2
            pltpu.matmul_push_rhs(ks_ref[:, block(k)], r, m)
            pltpu.matmul_acc_lhs(gs[m], probe, load_staged_rhs=r)
            far = pltpu.matmul_pop(gs[m])
            prod_ref[:, block(k)] = nugget * dir_ref[:, block(k)] + amplitude * (acc_ref[:, block(k)] + far_weight * far)

    def pass_on(lo, hi):
        @pl.when(jnp.logical_and(is_main, chip_two))
        def _():
            for ci in range(lo, hi):
                hand_over(ci).wait_recv()
                forward(ci).start()

    pass_on(0, nc - 1)
    pl.run_scoped(spread, pltpu.ACC(0)((rhs, TI), f32), pltpu.ACC(1)((rhs, TI), f32))
    pass_on(nc - 1, nc)

    @pl.when(is_main)
    def _():
        prod_ref[...] += amplitude * pacc_ref[...]

    def returned(k, ci):
        cols = chunk(ci)
        return remote(ret_out.at[:, cols], ret_in.at[k, :, cols], es_sem.at[ci], er_sem.at[k, ci], leaf=home_leaf, pair=pair)

    @pl.when(back_ok)
    def _():
        for ci in range(nc):
            give_rows(ci).wait_recv()
        prod_ref[...] += amplitude * ret_in[0]

    @pl.when(is_help)
    def _():
        for ci in range(nc):
            returned(0, ci).wait_recv()
        prod_ref[...] += amplitude * ret_in[0]

    @pl.when(home_two)
    def _():
        for ci in range(nc):
            returned(1, ci).wait_recv()
        prod_ref[...] += amplitude * ret_in[1]

    store = pltpu.make_async_copy(prod_ref, prod_hbm, out_sem)
    store.start()

    if one_stage:
        for a, b in hops:
            src = partial(lax.rem(leaf + nleaf - a, nleaf), lax.rem(pair + npair - b, npair))
            remote(src, src, cs_sem.at[a, b], cr_sem.at[a, b], leaf=leaf_peer(a), pair=pair_peer(b)).wait_recv()
        total = jnp.sum(red_a[...], axis=0)
    else:
        for k in range(1, nleaf):
            src = lax.rem(leaf + nleaf - k, nleaf)
            remote(red_a.at[src], red_a.at[src], cs_sem.at[k, 0], cr_sem.at[k, 0], leaf=leaf_peer(k)).wait_recv()
        red_b[pair] = jnp.sum(red_a[:nleaf], axis=0)
        sends_b = [
            remote(red_b.at[pair], red_b.at[pair], ds_sem.at[k], dr_sem.at[k], pair=pair_peer(k))
            for k in range(1, npair)
        ]
        for c in sends_b:
            c.start()
        for k in range(1, npair):
            src = lax.rem(pair + npair - k, npair)
            remote(red_b.at[src], red_b.at[src], ds_sem.at[k], dr_sem.at[k], pair=pair_peer(k)).wait_recv()
        total = jnp.sum(red_b[...], axis=0)
    total = total * (1.0 / (n * nleaf * npair))
    dots_ref[...] = jnp.concatenate([total[:, :rhs], total[:, rhs : 2 * rhs]], axis=0)
    store_dots = pltpu.make_async_copy(dots_ref, dots_hbm, in_sem.at[0])
    store_dots.start()

    for c in sends + sends_b + stage_a + stage_t + stage_q:
        c.wait_send()

    @pl.when(is_main)
    def _():
        for ci in range(nc):
            give_back(ci).wait_send()

    @pl.when(jnp.logical_and(is_main, chip_two))
    def _():
        for ci in range(nc):
            forward(ci).wait_send()

    @pl.when(helping)
    def _():
        for ci in range(nc):
            hand_over(ci).wait_send()

    @pl.when(helping)
    def _():
        for ci in range(nc):
            give_rows(ci).wait_send()

    @pl.when(is_main)
    def _():
        for ci in range(nc):
            for c in relay(ci):
                c.wait_send()

    @pl.when(jnp.logical_and(is_help, jnp.logical_not(chip_two)))
    def _():
        for ci in range(nc):
            for c in relay(ci):
                c.wait_recv()

    @pl.when(is_help)
    def _():
        for ci in range(nc):
            for c in to_main(ci):
                c.wait_send()

    @pl.when(back_ok)
    def _():
        for ci in range(nc):
            for c in to_help(ci):
                c.wait_send()

    store.wait()
    store_dots.wait()


def on_device(points, inv_scales, direction, residual, skeleton):
    feats, n = points.shape
    rhs = direction.shape[0]
    nskel = skeleton.shape[1]
    nleaf = lax.axis_size("leaf")
    npair = lax.axis_size("pair")
    anywhere = pl.BlockSpec(memory_space=pl.ANY)
    dma = pltpu.SemaphoreType.DMA
    nc = n // CC
    return pl.pallas_call(
        functools.partial(kernel, nleaf, npair),
        out_shape=(jax.ShapeDtypeStruct((rhs, n), f32), jax.ShapeDtypeStruct((2, rhs), f32)),
        in_specs=[pl.BlockSpec(memory_space=pltpu.HBM)] * 5,
        out_specs=(anywhere, anywhere),
        scratch_shapes=[
            pltpu.VMEM((feats, n), f32),
            pltpu.VMEM((1, feats), f32),
            pltpu.VMEM((rhs, n), f32),
            pltpu.VMEM((rhs, n), f32),
            pltpu.VMEM((1, nskel), jnp.int32),
            pltpu.VMEM((rhs, n), f32),
            pltpu.VMEM((2, rhs), f32),
            pltpu.VMEM((feats, n), f32),
            pltpu.VMEM((rhs, n), f32),
            pltpu.VMEM((feats, n), f32),
            pltpu.VMEM((rhs, n), f32),
            pltpu.VMEM((rhs, n), f32),
            pltpu.VMEM((rhs, n), f32),
            pltpu.VMEM((2, rhs, n), f32),
            pltpu.VMEM((2, 4 * feats, n), bf16),
            pltpu.VMEM((n, 4 * feats), bf16),
            pltpu.VMEM((2 * rhs, n), bf16),
            pltpu.VMEM((2, n, 128), bf16),
            pltpu.VMEM((rhs, n), f32),
            pltpu.VMEM((rhs, n), f32),
            pltpu.VMEM((TI, n), bf16),
            pltpu.VMEM((nleaf * nskel, 128), f32),
            pltpu.VMEM((npair, nskel, 128), f32),
            pltpu.VMEM((npair, nskel, 128), f32),
            pltpu.VMEM((npair, nskel, 128), f32),
            pltpu.VMEM((n, 4 * feats), bf16),
            pltpu.VMEM((2 * rhs, n), bf16),
            pltpu.VMEM((nleaf * npair if nleaf * npair <= 64 else nleaf, 1, 128), f32),
            pltpu.VMEM((npair, 1, 128), f32),
            pltpu.VMEM((rhs, 128), f32),
            dma((5,)), dma,
            dma((2, nc)), dma((2, nc)),
            dma((2, nc)), dma((2, nc)),
            dma((nc,)), dma((2, nc)),
            dma((nc,)), dma((nc,)),
            dma((nc,)), dma((nc,)),
            dma((nleaf,)), dma((nleaf,)),
            dma((npair,)), dma((npair,)),
            dma((npair,)), dma((npair,)),
            dma((nleaf, npair)), dma((nleaf, npair)),
            dma((npair,)), dma((npair,)),
        ],
        compiler_params=pltpu.CompilerParams(collective_id=0, has_side_effects=True, vmem_limit_bytes=40 * 1024 * 1024),
        name="matern_step",
    )(*[pltpu.with_memory_space_constraint(v, pltpu.HBM) for v in (points, inv_scales.reshape(1, feats), direction, residual, skeleton)])


def solution(mesh):
    return jax.shard_map(
        on_device,
        mesh=mesh,
        in_specs=(
            P(None, ("pair", "leaf")),
            P(),
            P(None, ("pair", "leaf")),
            P(None, ("pair", "leaf")),
            P(("pair", "leaf"), None),
        ),
        out_specs=(P(None, ("pair", "leaf")), P()),
        check_vma=False,
    )
```

```python
import functools
import math

import jax
import jax.numpy as jnp
from jax import lax
from jax.experimental import pallas as pl
from jax.experimental.pallas import tpu as pltpu
from jax.sharding import PartitionSpec as P

root_three = math.sqrt(3.0)
neg_log2e = -1.4426950408889634
nugget = 0.5
far_weight = 0.125
tiny = 1e-30
f32 = jnp.float32
bf16 = jnp.bfloat16
TI = 256
CC = 512
FIRST = 3
EARLY = 2
AHEAD = 8
CH = 256


def matern_of(u):
    u = jnp.maximum(u, tiny)
    t = u * lax.rsqrt(u)
    return (1.0 + t) * jnp.exp2(t * neg_log2e)


def split(x):
    h = x.astype(bf16)
    return h, (x - h.astype(f32)).astype(bf16)


def kernel(
    nleaf, npair,
    pts_hbm, inv_hbm, dir_hbm, res_hbm, skel_hbm,
    prod_hbm, dots_hbm,
    pts_ref, inv_ref, dir_ref, res_ref, skel_ref, prod_ref, dots_ref,
    xb_p, xb_d, zb_p, zb_d, ret_out, fwd_ref, ret_in, b_ref, st_ref, dd_ref, w_ref, acc_ref, pacc_ref, ks_ref, ag_ref, tg_ref, qo_ref, qi_ref, sz_ref, dz_ref, red_a, red_b, curv_ref,
    in_sem, out_sem, hs_sem, hr_sem, fs_sem, fr_sem, es_sem, er_sem, gs_sem, gr_sem, ps_sem, pr_sem, as_sem, ar_sem, bs_sem, br_sem, qs_sem, qr_sem, cs_sem, cr_sem, ds_sem, dr_sem,
):
    feats, n = pts_ref.shape
    rhs = dir_ref.shape[0]
    nskel = skel_ref.shape[1]
    leaf = lax.axis_index("leaf")
    pair = lax.axis_index("pair")

    leaf_odd = lax.rem(leaf, 2)
    pair_odd = lax.rem(pair, 2)
    is_main = leaf_odd == pair_odd
    is_help = leaf_odd != pair_odd
    step = 1 - 2 * leaf_odd
    other = pair + 1 - 2 * pair_odd
    far_leaf = leaf + 2 * step
    chip_two = jnp.logical_and(far_leaf >= 0, far_leaf < nleaf)
    helping = jnp.logical_and(is_help, chip_two)
    back_leaf = leaf - 2 * step
    back_ok = jnp.logical_and(is_main, jnp.logical_and(back_leaf >= 0, back_leaf < nleaf))
    home_step = 1 - 2 * pair_odd
    home_leaf = leaf - home_step
    home_far = home_leaf + 2 * home_step
    home_two = jnp.logical_and(is_help, jnp.logical_and(home_far >= 0, home_far < nleaf))

    def remote(src, dst, ss, rs, **dev):
        return pltpu.make_async_remote_copy(
            src_ref=src, dst_ref=dst, send_sem=ss, recv_sem=rs, device_id=dev,
            device_id_type=pl.DeviceIdType.MESH)

    def leaf_peer(k):
        return lax.rem(leaf + k, nleaf)

    def pair_peer(k):
        return lax.rem(pair + k, npair)

    loads = [
        pltpu.make_async_copy(src, dst, in_sem.at[k])
        for k, (src, dst) in enumerate((
            (inv_hbm, inv_ref), (pts_hbm, pts_ref), (dir_hbm, dir_ref), (skel_hbm, skel_ref), (res_hbm, res_ref)))
    ]
    for c in loads:
        c.start()

    barrier = pltpu.get_barrier_semaphore()

    def greet(**dev):
        pl.semaphore_signal(barrier, inc=1, device_id=dev, device_id_type=pl.DeviceIdType.MESH)

    for k in range(1, nleaf):
        greet(leaf=leaf_peer(k))
    for k in range(1, npair):
        greet(pair=pair_peer(k))

    @pl.when(back_ok)
    def _():
        greet(leaf=back_leaf, pair=other)

    @pl.when(helping)
    def _():
        greet(leaf=far_leaf, pair=other)

    def chunk(ci):
        return pl.ds(pl.multiple_of(ci * CC, CC), CC)

    def block_copies(ci, src_p, src_d, dst_p, dst_d, ss, rs, dev):
        cols = chunk(ci)
        return (
            remote(src_p.at[:, cols], dst_p.at[:, cols], ss.at[0, ci], rs.at[0, ci], **dev),
            remote(src_d.at[:, cols], dst_d.at[:, cols], ss.at[1, ci], rs.at[1, ci], **dev),
        )

    def to_main(ci):
        return block_copies(ci, pts_ref, dir_ref, xb_p, xb_d, hs_sem, hr_sem, dict(leaf=home_leaf, pair=pair))

    def to_help(ci):
        return block_copies(ci, pts_ref, dir_ref, zb_p, zb_d, hs_sem, hr_sem, dict(leaf=back_leaf, pair=other))

    def relay(ci):
        return block_copies(ci, xb_p, xb_d, xb_p, xb_d, fs_sem, fr_sem, dict(leaf=leaf, pair=other))

    def give_back(ci):
        cols = chunk(ci)
        return remote(ret_out.at[:, cols], ret_in.at[0, :, cols], es_sem.at[ci], er_sem.at[0, ci], leaf=leaf + step, pair=pair)

    def hand_over(ci):
        cols = chunk(ci)
        return remote(ret_out.at[:, cols], fwd_ref.at[:, cols], es_sem.at[ci], gr_sem.at[ci], leaf=leaf, pair=other)

    def forward(ci):
        cols = chunk(ci)
        return remote(fwd_ref.at[:, cols], ret_in.at[1, :, cols], gs_sem.at[ci], er_sem.at[1, ci], leaf=leaf + step, pair=pair)

    def give_rows(ci):
        cols = chunk(ci)
        return remote(pacc_ref.at[:, cols], ret_in.at[0, :, cols], ps_sem.at[ci], pr_sem.at[ci], leaf=far_leaf, pair=other)

    nc = n // CC

    def send_block(lo, hi):
        @pl.when(is_help)
        def _():
            for ci in range(lo, hi):
                for c in to_main(ci):
                    c.start()

        @pl.when(back_ok)
        def _():
            for ci in range(lo, hi):
                for c in to_help(ci):
                    c.start()

    for c in loads[:4]:
        c.wait()

    eye = lax.broadcasted_iota(jnp.int32, (feats, feats), 0) == lax.broadcasted_iota(jnp.int32, (feats, feats), 1)
    inv_col = jnp.sum(jnp.where(eye, jnp.broadcast_to(inv_ref[...], (feats, feats)), 0.0), axis=1, keepdims=True) * root_three

    def norm_rows(norm):
        n1 = norm.astype(bf16).astype(f32)
        n2 = (norm - n1).astype(bf16).astype(f32)
        return jnp.concatenate([n1, n2, norm - n1 - n2], axis=0)

    def parts(p_src, cols):
        p = p_src[:, cols] * inv_col
        h, l = split(p)
        hf, lf = h.astype(f32), l.astype(f32)
        q = hf + lf
        norm = norm_rows(jnp.sum(q * q, axis=0, keepdims=True))
        return h, l, hf, lf, norm

    def as_cols(h, l, norm):
        w = norm.shape[1]
        ext = jnp.concatenate([jnp.ones((3, w), f32), norm, jnp.zeros((feats - 6, w), f32)], axis=0)
        return jnp.concatenate([h, l, h, ext.astype(bf16)], axis=0)

    def as_rows(hf, lf, norm):
        w = norm.shape[1]
        ext = jnp.concatenate([norm, jnp.ones((3, w), f32), jnp.zeros((feats - 6, w), f32)], axis=0)
        h2 = hf * -2.0
        return jnp.concatenate([h2, h2, lf * -2.0, ext], axis=0).T.astype(bf16)

    def both_halves(d_src, cols):
        return jnp.concatenate(split(d_src[:, cols]), axis=0)

    def as_weights(dd):
        w = dd.shape[1]
        return jnp.concatenate([dd.astype(f32), jnp.zeros((128 - 2 * rhs, w), f32)], axis=0).T.astype(bf16)

    def prepare(ci):
        cols = pl.ds(pl.multiple_of(ci * CH, CH), CH)
        h, l, hf, lf, norm = parts(pts_ref, cols)
        b_ref[0, :, cols] = as_cols(h, l, norm)
        st_ref[cols, :] = as_rows(hf, lf, norm)
        dd = both_halves(dir_ref, cols)
        dd_ref[:, cols] = dd
        w_ref[0, cols, :] = as_weights(dd)
        ks_ref[3 * nskel :, cols] = jnp.zeros((TI - 3 * nskel, CH), bf16)
        acc_ref[:, cols] = jnp.zeros((rhs, CH), f32)
        pacc_ref[:, cols] = jnp.zeros((rhs, CH), f32)

    pl.loop(0, EARLY)(prepare)

    extra = jnp.where(jnp.logical_or(back_ok, helping), 1, 0)
    pl.semaphore_wait(barrier, nleaf - 1 + npair - 1 + extra)

    send_block(0, FIRST)

    pl.loop(EARLY, n // CH)(prepare)

    nt = n // TI

    def sweep(plan, xs, ys, rs):
        stage = [0, 0]

        def push(v, m):
            k = stage[m]
            stage[m] = 1 - k
            pltpu.matmul_push_rhs(v, k, m)
            return k

        def cross(t):
            for go in plan[t].get("first", ()):
                go()
            pltpu.matmul_acc_lhs(xs[t % 2], plan[t]["rows"](), load_staged_rhs=push(plan[t]["cols"](), 1))

        def spend(t, k):
            p = plan[t]
            if p["turn"] is not None:
                w = p["weights"]()
                w = jnp.concatenate([w, jnp.zeros_like(w)], axis=1)
                pltpu.matmul_acc_lhs(rs[p["turn"]], k, load_staged_rhs=push(w, 0))
            m = t % 2
            dd = p["dd"]()
            pltpu.matmul_acc_lhs(ys[m], dd[:rhs], load_staged_rhs=push(k, m))
            pltpu.matmul_acc_lhs(ys[m], dd[rhs:])

        def finish(t):
            p = plan[t]
            p["out"](pltpu.matmul_pop(ys[t % 2]))
            if p["turned"] is not None:
                r = pltpu.matmul_pop(rs[p["turn"]])[:, :128].T
                p["turned"](r[:rhs] + r[rhs : 2 * rhs])
            for go in p.get("then", ()):
                go()

        count = len(plan)
        cross(0)
        held = None
        for t in range(count + 2):
            k = None
            if t < count:
                k = matern_of(pltpu.matmul_pop(xs[t % 2])).astype(bf16)
            if t + 1 < count:
                cross(t + 1)
            if 0 < t <= count:
                spend(t - 1, held)
            held = k
            if t > 1:
                finish(t - 2)

    def get_chunk(ci):
        for c in to_main(ci):
            c.wait_recv()
        for c in relay(ci):
            c.start()

    def own_block(xs, ys, rs):
        half = nt // 2

        def rows_pair(k, reach):
            plan = []
            for i in range(2):
                def tile(d, i=i):
                    return pl.ds(pl.multiple_of(lax.rem(2 * k + i + nt - d, nt) * TI, TI), TI)

                def add(cols):
                    def go(v):
                        acc_ref[:, cols] += v
                    return go

                rows = tile(0)
                for d in range(reach + 1):
                    cols = tile(d)
                    plan.append(dict(
                        rows=lambda rows=rows: st_ref[rows, :],
                        cols=lambda cols=cols: b_ref[0, :, cols],
                        weights=lambda cols=cols: w_ref[0, cols, :],
                        dd=lambda rows=rows: dd_ref[:, rows],
                        turn=i if d else None,
                        out=add(cols),
                        turned=add(rows) if d == reach else None,
                    ))
            sweep(plan, xs, ys, rs)

        pl.loop(0, half // 2)(lambda k: rows_pair(k, half))

        @pl.loop(half // 2, half)
        def _(k):
            @pl.when(jnp.logical_and(is_main, k == half - 1))
            def _():
                get_chunk(0)

            rows_pair(k, half - 1)

    def cross_tile(st, dd, cols, where, turn, turned):
        def add(v):
            pacc_ref[:, cols] += v

        return dict(
            rows=st,
            cols=lambda: b_ref[where, :, cols],
            weights=lambda: w_ref[where, cols, :],
            dd=dd,
            turn=turn,
            out=add,
            turned=turned,
        )

    def main_chunk(ci, xs, ys, rs, ahead=False):
        plan = []
        for i in range(CC // TI):
            rows = pl.ds(pl.multiple_of(ci * CC + i * TI, TI), TI)
            _, _, hf, lf, norm = parts(xb_p, rows)
            st = as_rows(hf, lf, norm)
            dd = both_halves(xb_d, rows)

            def turned(v, rows=rows):
                ret_out[:, rows] = v

            for jt in range(nt):
                cols = slice(jt * TI, (jt + 1) * TI)
                plan.append(cross_tile(lambda st=st: st, lambda dd=dd: dd, cols, 0, i % 2, turned if jt == nt - 1 else None))
        if ahead:
            plan[AHEAD]["first"] = [lambda: get_chunk(ci + 1)]
        sweep(plan, xs, ys, rs)
        give_back(ci).start()

    def help_columns(ci):
        for c in to_help(ci):
            c.wait_recv()
        for i in range(CC // CH):
            cols = slice(ci * CC + i * CH, ci * CC + (i + 1) * CH)
            h, l, _, _, norm = parts(zb_p, cols)
            b_ref[1, :, cols] = as_cols(h, l, norm)
            w_ref[1, cols, :] = as_weights(both_halves(zb_d, cols))

    def help_rows(ci):
        for c in relay(ci):
            c.wait_recv()
        for i in range(CC // CH):
            rows = slice(ci * CC + i * CH, ci * CC + (i + 1) * CH)
            _, _, hf, lf, norm = parts(xb_p, rows)
            sz_ref[rows, :] = as_rows(hf, lf, norm)
            dz_ref[:, rows] = both_halves(xb_d, rows)

    def help_part(ci, xs, ys, rs):
        per = CC // TI
        last = ci == nc - 1
        early, late = ci * per, (ci + 1) * per
        plan = []

        def add_tile(it, jt, ends, fresh):
            rows = slice(it * TI, (it + 1) * TI)

            def turned(v):
                if fresh:
                    ret_out[:, rows] = v
                else:
                    ret_out[:, rows] += v

            plan.append(cross_tile(
                lambda: sz_ref[rows, :], lambda: dz_ref[:, rows], slice(jt * TI, (jt + 1) * TI), 1, it % 2,
                turned if ends else None))

        for it in range(early):
            for jt in range(early, late):
                add_tile(it, jt, jt == late - 1, False)
        if last:
            plan[-1]["then"] = [hand_over(c).start for c in range(ci)]
        start = len(plan)
        for c in range(ci + 1):
            for it in range(early, late):
                for jt in range(c * per, (c + 1) * per):
                    add_tile(it, jt, c == ci and jt == late - 1, True)
            if last and c < nc - 2:
                plan[-1]["then"] = [give_rows(c).start]
        if last:
            plan[-1]["then"] = [hand_over(ci).start]
        plan[start]["first"] = [lambda: help_rows(ci)]
        sweep(plan, xs, ys, rs)

    def wide(w):
        return jnp.concatenate([w, jnp.zeros((w.shape[0], TI - w.shape[1]), w.dtype)], axis=1)

    def deep_dot(accs, lhs, rhs_of, count):
        for k in range(count):
            m, r = k % 2, (k // 2) % 2
            pltpu.matmul_push_rhs(rhs_of(k), r, m)
            pltpu.matmul_acc_lhs(accs[m], lhs(k), load_staged_rhs=r)
        return pltpu.matmul_pop(accs[0]) + pltpu.matmul_pop(accs[1])

    def block(k):
        return slice(k * TI, (k + 1) * TI)

    def skeleton(p0, p1, c0, c1, f0, f1):
        index = jnp.broadcast_to(wide(skel_ref[...] + 1), (TI, TI)) - 1

        def chosen(k):
            return jnp.where(lax.broadcasted_iota(jnp.int32, (TI, TI), 0) + k * TI == index, 1.0, 0.0).astype(bf16)

        picked = deep_dot((p0, p1), lambda k: b_ref[0, : 2 * feats, block(k)], chosen, n // TI)[:, :128]
        skel_rows = (picked[:feats] + picked[feats:]).T[:nskel]
        norm_s = jnp.sum(skel_rows * skel_rows, axis=1, keepdims=True)
        sh, sl = split(skel_rows)
        sh, sl = sh.astype(f32) * -2.0, sl.astype(f32) * -2.0
        n1 = norm_s.astype(bf16).astype(f32)
        n2 = (norm_s - n1).astype(bf16).astype(f32)
        lane_s = lax.broadcasted_iota(jnp.int32, (nskel, feats), 1)
        ext_s = jnp.where(lane_s == 0, n1, jnp.where(lane_s == 1, n2, jnp.where(lane_s == 2, norm_s - n1 - n2, jnp.where(lane_s < 6, 1.0, 0.0))))
        probe = jnp.concatenate([sh, sh, sl, ext_s], axis=1).astype(bf16)
        cs = (c0, c1)
        for k in range(n // TI):
            m, r = k % 2, (k // 2) % 2
            pltpu.matmul_push_rhs(b_ref[0, :, block(k)], r, m)
            pltpu.matmul_acc_lhs(cs[m], probe, load_staged_rhs=r)
            h, l = split(matern_of(pltpu.matmul_pop(cs[m])))
            ks_ref[: 3 * nskel, block(k)] = jnp.concatenate([h, l, h], axis=0)
        part = deep_dot((f0, f1), lambda k: ks_ref[: 2 * nskel, block(k)], lambda k: wide(w_ref[0, block(k), :]), n // TI)
        coeff_t = part[:nskel, :rhs] + part[:nskel, rhs : 2 * rhs] + part[nskel:, :rhs] + part[nskel:, rhs : 2 * rhs]
        pad = jnp.zeros((nskel, 128 - feats - rhs - 2), f32)
        pack = jnp.concatenate([skel_rows, coeff_t, n1, norm_s - n1, pad], axis=1)
        ag_ref[my_rows, :] = pack
        tg_ref[pair] = pack

    my_rows = pl.ds(pl.multiple_of(leaf * nskel, 8), nskel)
    pl.run_scoped(
        skeleton,
        pltpu.ACC(0)((2 * feats, TI), f32), pltpu.ACC(1)((2 * feats, TI), f32),
        pltpu.ACC(0)((nskel, TI), f32), pltpu.ACC(1)((nskel, TI), f32),
        pltpu.ACC(0)((2 * nskel, TI), f32), pltpu.ACC(1)((2 * nskel, TI), f32),
    )

    stage_a = [
        remote(ag_ref.at[my_rows, :], ag_ref.at[my_rows, :], as_sem.at[k], ar_sem.at[k], leaf=leaf_peer(k))
        for k in range(1, nleaf)
    ]
    stage_t = [
        remote(tg_ref.at[pair], tg_ref.at[pair], bs_sem.at[k], br_sem.at[k], pair=pair_peer(k))
        for k in range(1, npair)
    ]
    stage_q = [
        remote(qo_ref.at[pair_peer(k)], qi_ref.at[pair], qs_sem.at[k], qr_sem.at[k], pair=pair_peer(k))
        for k in range(1, npair)
    ]
    for c in stage_a + stage_t:
        c.start()
    send_block(FIRST, nc)

    group = TI // (2 * nskel)

    def far_field(xs, rs):
        for k, c in enumerate(stage_a, 1):
            src_rows = pl.ds(pl.multiple_of(lax.rem(leaf + nleaf - k, nleaf) * nskel, 8), nskel)
            remote(ag_ref.at[src_rows, :], ag_ref.at[src_rows, :], as_sem.at[k], ar_sem.at[k], leaf=leaf_peer(k)).wait_recv()
        for k, c in enumerate(stage_t, 1):
            src = lax.rem(pair + npair - k, npair)
            remote(tg_ref.at[src], tg_ref.at[src], bs_sem.at[k], br_sem.at[k], pair=pair_peer(k)).wait_recv()
        lane_o = lax.broadcasted_iota(jnp.int32, (nskel, 128), 1)
        ones = jnp.logical_and(lane_o >= feats + rhs, lane_o < feats + rhs + 2)
        for first in range(0, npair, group):
            probes, norms = [], []
            for p in range(first, first + group):
                target = jnp.where(lane_o < feats, tg_ref[p], 0.0)
                norms.append(jnp.sum(target * target, axis=1, keepdims=True))
                oh, ol = split(target)
                oh = jnp.where(ones, 1.0, oh.astype(f32) * -2.0).astype(bf16)
                ol = (ol.astype(f32) * -2.0).astype(bf16)
                probes += [jnp.concatenate([oh, oh], axis=1), jnp.concatenate([ol, jnp.zeros_like(ol)], axis=1)]
            probe = jnp.concatenate(probes, axis=0)
            for g in range(nleaf * nskel // TI):
                both = jnp.concatenate(split(ag_ref[block(g), :]), axis=1)
                pltpu.matmul_push_rhs(both, 0, 0, transpose=True)
                pltpu.matmul_acc_lhs(rs[0], probe, load_staged_rhs=0)
                u = pltpu.matmul_pop(rs[0])
                near_mask = jnp.abs(lax.div(lax.broadcasted_iota(jnp.int32, (nskel, TI), 1) + g * TI, nskel) - leaf) <= 1
                weights = []
                for i in range(group):
                    lo = 2 * i * nskel
                    w = matern_of(norms[i] + u[lo : lo + nskel] + u[lo + nskel : lo + 2 * nskel])
                    same = jnp.full((nskel, TI), pair, jnp.int32) == first + i
                    weights += list(split(jnp.where(jnp.logical_and(same, near_mask), 0.0, w)))
                pltpu.matmul_push_rhs(both, 0, 1)
                pltpu.matmul_acc_lhs(xs[0], jnp.concatenate(weights, axis=0), load_staged_rhs=0)
            q = pltpu.matmul_pop(xs[0])
            q = q[:, :128] + q[:, 128:]
            for i in range(group):
                lo = 2 * i * nskel
                qo_ref[first + i] = q[lo : lo + nskel] + q[lo + nskel : lo + 2 * nskel]
        for c in stage_q:
            c.start()

    amplitude = 1.0 / math.sqrt(3.0 * n)
    lane = lax.broadcasted_iota(jnp.int32, (rhs, 128), 1)

    def near(x0, x1, y0, y1, r0, r1):
        xs, ys, rs = (x0, x1), (y0, y1), (r0, r1)
        own_block(xs, ys, rs)
        loads[4].wait()
        squares = jnp.sum(res_ref[...] * res_ref[...], axis=1, keepdims=True)
        curvature = jnp.sum(dir_ref[...] * (nugget * dir_ref[...] + amplitude * acc_ref[...]), axis=1, keepdims=True)
        curv_ref[...] = jnp.where(lane == 0, squares, jnp.where(lane == 1, curvature, 0.0))

        @pl.when(is_main)
        def _():
            @pl.loop(0, nc - 2)
            def _(ci):
                main_chunk(ci, xs, ys, rs, ahead=True)

            main_chunk(nc - 2, xs, ys, rs)

        @pl.when(helping)
        def _():
            for ci in range(nc - 1):
                help_columns(ci)
                help_part(ci, xs, ys, rs)

        far_field(xs, rs)

        @pl.when(is_main)
        def _():
            get_chunk(nc - 1)
            main_chunk(nc - 1, xs, ys, rs)

        @pl.when(helping)
        def _():
            help_columns(nc - 1)
            help_part(nc - 1, xs, ys, rs)

    pl.run_scoped(
        near,
        pltpu.ACC(1)((TI, TI), f32), pltpu.ACC(1)((TI, TI), f32),
        pltpu.ACC(0)((rhs, TI), f32), pltpu.ACC(1)((rhs, TI), f32),
        pltpu.ACC(0)((TI, TI), f32), pltpu.ACC(0)((TI, TI), f32),
    )

    def add_pair(d_ref):
        shared = jnp.sum(d_ref[...] * pacc_ref[...], axis=1, keepdims=True)
        curv_ref[...] += jnp.where(lane == 1, (2.0 * amplitude) * shared, 0.0)

    @pl.when(is_main)
    def _():
        add_pair(dir_ref)

    @pl.when(helping)
    def _():
        add_pair(zb_d)

    q_t = qo_ref[pair]
    for k in range(1, npair):
        src = lax.rem(pair + npair - k, npair)
        remote(qo_ref.at[src], qi_ref.at[src], qs_sem.at[k], qr_sem.at[k], pair=pair_peer(k)).wait_recv()
        q_t = q_t + qi_ref[src]
    far_row = (amplitude * far_weight) * jnp.sum(q_t * tg_ref[pair], axis=0, keepdims=True)[:, feats : feats + rhs]
    both = jnp.concatenate([curv_ref[...], jnp.zeros((128 - rhs, 128), f32)], axis=0).T
    both = jnp.concatenate([both[0:1, :rhs], both[1:2, :rhs] + far_row, jnp.zeros((1, 128 - 2 * rhs), f32)], axis=1)
    one_stage = nleaf * npair <= 64
    sends_b = []
    if one_stage:
        def partial(l, p):
            return red_a.at[p * nleaf + l]

        red_a[pair * nleaf + leaf] = both
        hops = [(a, b) for b in range(npair) for a in range(nleaf) if a or b]
        sends = [
            remote(partial(leaf, pair), partial(leaf, pair), cs_sem.at[a, b], cr_sem.at[a, b], leaf=leaf_peer(a), pair=pair_peer(b))
            for a, b in hops
        ]
    else:
        red_a[leaf] = both
        sends = [
            remote(red_a.at[leaf], red_a.at[leaf], cs_sem.at[k, 0], cr_sem.at[k, 0], leaf=leaf_peer(k))
            for k in range(1, nleaf)
        ]
    for c in sends:
        c.start()

    def spread(g0, g1):
        gs = (g0, g1)
        qh, ql = split(q_t[:, feats : feats + rhs].T)
        probe = wide(jnp.concatenate([qh, qh, ql], axis=1))
        for k in range(n // TI):
            m, r = k % 2, (k // 2) % 2
            pltpu.matmul_push_rhs(ks_ref[:, block(k)], r, m)
            pltpu.matmul_acc_lhs(gs[m], probe, load_staged_rhs=r)
            far = pltpu.matmul_pop(gs[m])
            prod_ref[:, block(k)] = nugget * dir_ref[:, block(k)] + amplitude * (acc_ref[:, block(k)] + far_weight * far)

    @pl.when(helping)
    def _():
        for ci in range(max(nc - 2, 0), nc):
            give_rows(ci).start()

    def pass_on():
        @pl.when(jnp.logical_and(is_main, chip_two))
        def _():
            for ci in range(nc):
                hand_over(ci).wait_recv()
                forward(ci).start()

    pl.run_scoped(spread, pltpu.ACC(0)((rhs, TI), f32), pltpu.ACC(1)((rhs, TI), f32))
    pass_on()

    @pl.when(is_main)
    def _():
        prod_ref[...] += amplitude * pacc_ref[...]

    def returned(k, ci):
        cols = chunk(ci)
        return remote(ret_out.at[:, cols], ret_in.at[k, :, cols], es_sem.at[ci], er_sem.at[k, ci], leaf=home_leaf, pair=pair)

    @pl.when(back_ok)
    def _():
        for ci in range(nc):
            give_rows(ci).wait_recv()
        prod_ref[...] += amplitude * ret_in[0]

    @pl.when(is_help)
    def _():
        for ci in range(nc):
            returned(0, ci).wait_recv()
        prod_ref[...] += amplitude * ret_in[0]

    @pl.when(home_two)
    def _():
        for ci in range(nc):
            returned(1, ci).wait_recv()
        prod_ref[...] += amplitude * ret_in[1]

    store = pltpu.make_async_copy(prod_ref, prod_hbm, out_sem)
    store.start()

    if one_stage:
        for a, b in hops:
            src = partial(lax.rem(leaf + nleaf - a, nleaf), lax.rem(pair + npair - b, npair))
            remote(src, src, cs_sem.at[a, b], cr_sem.at[a, b], leaf=leaf_peer(a), pair=pair_peer(b)).wait_recv()
        total = jnp.sum(red_a[...], axis=0)
    else:
        for k in range(1, nleaf):
            src = lax.rem(leaf + nleaf - k, nleaf)
            remote(red_a.at[src], red_a.at[src], cs_sem.at[k, 0], cr_sem.at[k, 0], leaf=leaf_peer(k)).wait_recv()
        red_b[pair] = jnp.sum(red_a[:nleaf], axis=0)
        sends_b = [
            remote(red_b.at[pair], red_b.at[pair], ds_sem.at[k], dr_sem.at[k], pair=pair_peer(k))
            for k in range(1, npair)
        ]
        for c in sends_b:
            c.start()
        for k in range(1, npair):
            src = lax.rem(pair + npair - k, npair)
            remote(red_b.at[src], red_b.at[src], ds_sem.at[k], dr_sem.at[k], pair=pair_peer(k)).wait_recv()
        total = jnp.sum(red_b[...], axis=0)
    total = total * (1.0 / (n * nleaf * npair))
    dots_ref[...] = jnp.concatenate([total[:, :rhs], total[:, rhs : 2 * rhs]], axis=0)
    store_dots = pltpu.make_async_copy(dots_ref, dots_hbm, in_sem.at[0])
    store_dots.start()

    for c in sends + sends_b + stage_a + stage_t + stage_q:
        c.wait_send()

    @pl.when(is_main)
    def _():
        for ci in range(nc):
            give_back(ci).wait_send()

    @pl.when(jnp.logical_and(is_main, chip_two))
    def _():
        for ci in range(nc):
            forward(ci).wait_send()

    @pl.when(helping)
    def _():
        for ci in range(nc):
            hand_over(ci).wait_send()

    @pl.when(helping)
    def _():
        for ci in range(nc):
            give_rows(ci).wait_send()

    @pl.when(is_main)
    def _():
        for ci in range(nc):
            for c in relay(ci):
                c.wait_send()

    @pl.when(jnp.logical_and(is_help, jnp.logical_not(chip_two)))
    def _():
        for ci in range(nc):
            for c in relay(ci):
                c.wait_recv()

    @pl.when(is_help)
    def _():
        for ci in range(nc):
            for c in to_main(ci):
                c.wait_send()

    @pl.when(back_ok)
    def _():
        for ci in range(nc):
            for c in to_help(ci):
                c.wait_send()

    store.wait()
    store_dots.wait()


def on_device(points, inv_scales, direction, residual, skeleton):
    feats, n = points.shape
    rhs = direction.shape[0]
    nskel = skeleton.shape[1]
    nleaf = lax.axis_size("leaf")
    npair = lax.axis_size("pair")
    anywhere = pl.BlockSpec(memory_space=pl.ANY)
    dma = pltpu.SemaphoreType.DMA
    nc = n // CC
    return pl.pallas_call(
        functools.partial(kernel, nleaf, npair),
        out_shape=(jax.ShapeDtypeStruct((rhs, n), f32), jax.ShapeDtypeStruct((2, rhs), f32)),
        in_specs=[pl.BlockSpec(memory_space=pltpu.HBM)] * 5,
        out_specs=(anywhere, anywhere),
        scratch_shapes=[
            pltpu.VMEM((feats, n), f32),
            pltpu.VMEM((1, feats), f32),
            pltpu.VMEM((rhs, n), f32),
            pltpu.VMEM((rhs, n), f32),
            pltpu.VMEM((1, nskel), jnp.int32),
            pltpu.VMEM((rhs, n), f32),
            pltpu.VMEM((2, rhs), f32),
            pltpu.VMEM((feats, n), f32),
            pltpu.VMEM((rhs, n), f32),
            pltpu.VMEM((feats, n), f32),
            pltpu.VMEM((rhs, n), f32),
            pltpu.VMEM((rhs, n), f32),
            pltpu.VMEM((rhs, n), f32),
            pltpu.VMEM((2, rhs, n), f32),
            pltpu.VMEM((2, 4 * feats, n), bf16),
            pltpu.VMEM((n, 4 * feats), bf16),
            pltpu.VMEM((2 * rhs, n), bf16),
            pltpu.VMEM((2, n, 128), bf16),
            pltpu.VMEM((rhs, n), f32),
            pltpu.VMEM((rhs, n), f32),
            pltpu.VMEM((TI, n), bf16),
            pltpu.VMEM((nleaf * nskel, 128), f32),
            pltpu.VMEM((npair, nskel, 128), f32),
            pltpu.VMEM((npair, nskel, 128), f32),
            pltpu.VMEM((npair, nskel, 128), f32),
            pltpu.VMEM((n, 4 * feats), bf16),
            pltpu.VMEM((2 * rhs, n), bf16),
            pltpu.VMEM((nleaf * npair if nleaf * npair <= 64 else nleaf, 1, 128), f32),
            pltpu.VMEM((npair, 1, 128), f32),
            pltpu.VMEM((rhs, 128), f32),
            dma((5,)), dma,
            dma((2, nc)), dma((2, nc)),
            dma((2, nc)), dma((2, nc)),
            dma((nc,)), dma((2, nc)),
            dma((nc,)), dma((nc,)),
            dma((nc,)), dma((nc,)),
            dma((nleaf,)), dma((nleaf,)),
            dma((npair,)), dma((npair,)),
            dma((npair,)), dma((npair,)),
            dma((nleaf, npair)), dma((nleaf, npair)),
            dma((npair,)), dma((npair,)),
        ],
        compiler_params=pltpu.CompilerParams(collective_id=0, has_side_effects=True, vmem_limit_bytes=40 * 1024 * 1024),
        name="matern_step",
    )(*[pltpu.with_memory_space_constraint(v, pltpu.HBM) for v in (points, inv_scales.reshape(1, feats), direction, residual, skeleton)])


def solution(mesh):
    return jax.shard_map(
        on_device,
        mesh=mesh,
        in_specs=(
            P(None, ("pair", "leaf")),
            P(),
            P(None, ("pair", "leaf")),
            P(None, ("pair", "leaf")),
            P(("pair", "leaf"), None),
        ),
        out_specs=(P(None, ("pair", "leaf")), P()),
        check_vma=False,
    )
```

```python
import functools
import math

import jax
import jax.numpy as jnp
from jax import lax
from jax.experimental import pallas as pl
from jax.experimental.pallas import tpu as pltpu
from jax.sharding import PartitionSpec as P

root_three = math.sqrt(3.0)
neg_log2e = -1.4426950408889634
nugget = 0.5
far_weight = 0.125
tiny = 1e-30
f32 = jnp.float32
bf16 = jnp.bfloat16
TI = 256
CC = 512
FIRST = 3
EARLY = 4
AHEAD = 8
CH = 256


def matern_of(u):
    u = jnp.maximum(u, tiny)
    t = u * lax.rsqrt(u)
    return (1.0 + t) * jnp.exp2(t * neg_log2e)


def split(x):
    h = x.astype(bf16)
    return h, (x - h.astype(f32)).astype(bf16)


def kernel(
    nleaf, npair,
    pts_hbm, inv_hbm, dir_hbm, res_hbm, skel_hbm,
    prod_hbm, dots_hbm,
    pts_ref, inv_ref, dir_ref, res_ref, skel_ref, prod_ref, dots_ref,
    xb_p, xb_d, zb_p, zb_d, ret_out, fwd_ref, ret_in, b_ref, st_ref, dd_ref, w_ref, acc_ref, pacc_ref, ks_ref, ag_ref, tg_ref, qo_ref, qi_ref, sz_ref, dz_ref, red_a, red_b, curv_ref,
    in_sem, out_sem, hs_sem, hr_sem, fs_sem, fr_sem, es_sem, er_sem, gs_sem, gr_sem, ps_sem, pr_sem, as_sem, ar_sem, bs_sem, br_sem, qs_sem, qr_sem, cs_sem, cr_sem, ds_sem, dr_sem,
):
    feats, n = pts_ref.shape
    rhs = dir_ref.shape[0]
    nskel = skel_ref.shape[1]
    leaf = lax.axis_index("leaf")
    pair = lax.axis_index("pair")

    leaf_odd = lax.rem(leaf, 2)
    pair_odd = lax.rem(pair, 2)
    is_main = leaf_odd == pair_odd
    is_help = leaf_odd != pair_odd
    step = 1 - 2 * leaf_odd
    other = pair + 1 - 2 * pair_odd
    far_leaf = leaf + 2 * step
    chip_two = jnp.logical_and(far_leaf >= 0, far_leaf < nleaf)
    helping = jnp.logical_and(is_help, chip_two)
    back_leaf = leaf - 2 * step
    back_ok = jnp.logical_and(is_main, jnp.logical_and(back_leaf >= 0, back_leaf < nleaf))
    home_step = 1 - 2 * pair_odd
    home_leaf = leaf - home_step
    home_far = home_leaf + 2 * home_step
    home_two = jnp.logical_and(is_help, jnp.logical_and(home_far >= 0, home_far < nleaf))

    def remote(src, dst, ss, rs, **dev):
        return pltpu.make_async_remote_copy(
            src_ref=src, dst_ref=dst, send_sem=ss, recv_sem=rs, device_id=dev,
            device_id_type=pl.DeviceIdType.MESH)

    def leaf_peer(k):
        return lax.rem(leaf + k, nleaf)

    def pair_peer(k):
        return lax.rem(pair + k, npair)

    loads = [
        pltpu.make_async_copy(src, dst, in_sem.at[k])
        for k, (src, dst) in enumerate((
            (inv_hbm, inv_ref), (pts_hbm, pts_ref), (dir_hbm, dir_ref), (skel_hbm, skel_ref), (res_hbm, res_ref)))
    ]
    for c in loads:
        c.start()

    barrier = pltpu.get_barrier_semaphore()

    def greet(**dev):
        pl.semaphore_signal(barrier, inc=1, device_id=dev, device_id_type=pl.DeviceIdType.MESH)

    for k in range(1, nleaf):
        greet(leaf=leaf_peer(k))
    for k in range(1, npair):
        greet(pair=pair_peer(k))

    @pl.when(back_ok)
    def _():
        greet(leaf=back_leaf, pair=other)

    @pl.when(helping)
    def _():
        greet(leaf=far_leaf, pair=other)

    def chunk(ci):
        return pl.ds(pl.multiple_of(ci * CC, CC), CC)

    def block_copies(ci, src_p, src_d, dst_p, dst_d, ss, rs, dev):
        cols = chunk(ci)
        return (
            remote(src_p.at[:, cols], dst_p.at[:, cols], ss.at[0, ci], rs.at[0, ci], **dev),
            remote(src_d.at[:, cols], dst_d.at[:, cols], ss.at[1, ci], rs.at[1, ci], **dev),
        )

    def to_main(ci):
        return block_copies(ci, pts_ref, dir_ref, xb_p, xb_d, hs_sem, hr_sem, dict(leaf=home_leaf, pair=pair))

    def to_help(ci):
        return block_copies(ci, pts_ref, dir_ref, zb_p, zb_d, hs_sem, hr_sem, dict(leaf=back_leaf, pair=other))

    def relay(ci):
        return block_copies(ci, xb_p, xb_d, xb_p, xb_d, fs_sem, fr_sem, dict(leaf=leaf, pair=other))

    def give_back(ci):
        cols = chunk(ci)
        return remote(ret_out.at[:, cols], ret_in.at[0, :, cols], es_sem.at[ci], er_sem.at[0, ci], leaf=leaf + step, pair=pair)

    def hand_over(ci):
        cols = chunk(ci)
        return remote(ret_out.at[:, cols], fwd_ref.at[:, cols], es_sem.at[ci], gr_sem.at[ci], leaf=leaf, pair=other)

    def forward(ci):
        cols = chunk(ci)
        return remote(fwd_ref.at[:, cols], ret_in.at[1, :, cols], gs_sem.at[ci], er_sem.at[1, ci], leaf=leaf + step, pair=pair)

    def give_rows(ci):
        cols = chunk(ci)
        return remote(pacc_ref.at[:, cols], ret_in.at[0, :, cols], ps_sem.at[ci], pr_sem.at[ci], leaf=far_leaf, pair=other)

    nc = n // CC

    def send_block(lo, hi):
        @pl.when(is_help)
        def _():
            for ci in range(lo, hi):
                for c in to_main(ci):
                    c.start()

        @pl.when(back_ok)
        def _():
            for ci in range(lo, hi):
                for c in to_help(ci):
                    c.start()

    for c in loads[:4]:
        c.wait()

    eye = lax.broadcasted_iota(jnp.int32, (feats, feats), 0) == lax.broadcasted_iota(jnp.int32, (feats, feats), 1)
    inv_col = jnp.sum(jnp.where(eye, jnp.broadcast_to(inv_ref[...], (feats, feats)), 0.0), axis=1, keepdims=True) * root_three

    def norm_rows(norm):
        n1 = norm.astype(bf16).astype(f32)
        n2 = (norm - n1).astype(bf16).astype(f32)
        return jnp.concatenate([n1, n2, norm - n1 - n2], axis=0)

    def parts(p_src, cols):
        p = p_src[:, cols] * inv_col
        h, l = split(p)
        hf, lf = h.astype(f32), l.astype(f32)
        q = hf + lf
        norm = norm_rows(jnp.sum(q * q, axis=0, keepdims=True))
        return h, l, hf, lf, norm

    def as_cols(h, l, norm):
        w = norm.shape[1]
        ext = jnp.concatenate([jnp.ones((3, w), f32), norm, jnp.zeros((feats - 6, w), f32)], axis=0)
        return jnp.concatenate([h, l, h, ext.astype(bf16)], axis=0)

    def as_rows(hf, lf, norm):
        w = norm.shape[1]
        ext = jnp.concatenate([norm, jnp.ones((3, w), f32), jnp.zeros((feats - 6, w), f32)], axis=0)
        h2 = hf * -2.0
        return jnp.concatenate([h2, h2, lf * -2.0, ext], axis=0).T.astype(bf16)

    def both_halves(d_src, cols):
        return jnp.concatenate(split(d_src[:, cols]), axis=0)

    def as_weights(dd):
        w = dd.shape[1]
        return jnp.concatenate([dd.astype(f32), jnp.zeros((128 - 2 * rhs, w), f32)], axis=0).T.astype(bf16)

    def prepare(ci):
        cols = pl.ds(pl.multiple_of(ci * CH, CH), CH)
        h, l, hf, lf, norm = parts(pts_ref, cols)
        b_ref[0, :, cols] = as_cols(h, l, norm)
        st_ref[cols, :] = as_rows(hf, lf, norm)
        dd = both_halves(dir_ref, cols)
        dd_ref[:, cols] = dd
        w_ref[0, cols, :] = as_weights(dd)
        ks_ref[3 * nskel :, cols] = jnp.zeros((TI - 3 * nskel, CH), bf16)
        acc_ref[:, cols] = jnp.zeros((rhs, CH), f32)
        pacc_ref[:, cols] = jnp.zeros((rhs, CH), f32)

    pl.loop(0, EARLY)(prepare)

    extra = jnp.where(jnp.logical_or(back_ok, helping), 1, 0)
    pl.semaphore_wait(barrier, nleaf - 1 + npair - 1 + extra)

    send_block(0, FIRST)

    pl.loop(EARLY, n // CH)(prepare)

    nt = n // TI

    def sweep(plan, xs, ys, rs):
        stage = [0, 0]

        def push(v, m):
            k = stage[m]
            stage[m] = 1 - k
            pltpu.matmul_push_rhs(v, k, m)
            return k

        def cross(t):
            for go in plan[t].get("first", ()):
                go()
            pltpu.matmul_acc_lhs(xs[t % 2], plan[t]["rows"](), load_staged_rhs=push(plan[t]["cols"](), 1))

        def spend(t, k):
            p = plan[t]
            if p["turn"] is not None:
                w = p["weights"]()
                w = jnp.concatenate([w, jnp.zeros_like(w)], axis=1)
                pltpu.matmul_acc_lhs(rs[p["turn"]], k, load_staged_rhs=push(w, 0))
            m = t % 2
            dd = p["dd"]()
            pltpu.matmul_acc_lhs(ys[m], dd[:rhs], load_staged_rhs=push(k, m))
            pltpu.matmul_acc_lhs(ys[m], dd[rhs:])

        def finish(t):
            p = plan[t]
            p["out"](pltpu.matmul_pop(ys[t % 2]))
            if p["turned"] is not None:
                r = pltpu.matmul_pop(rs[p["turn"]])[:, :128].T
                p["turned"](r[:rhs] + r[rhs : 2 * rhs])
            for go in p.get("then", ()):
                go()

        count = len(plan)
        cross(0)
        held = None
        for t in range(count + 2):
            k = None
            if t < count:
                k = matern_of(pltpu.matmul_pop(xs[t % 2])).astype(bf16)
            if t + 1 < count:
                cross(t + 1)
            if 0 < t <= count:
                spend(t - 1, held)
            held = k
            if t > 1:
                finish(t - 2)

    def get_chunk(ci):
        for c in to_main(ci):
            c.wait_recv()
        for c in relay(ci):
            c.start()

    def own_block(xs, ys, rs):
        half = nt // 2

        def rows_pair(k, reach):
            plan = []
            for i in range(2):
                def tile(d, i=i):
                    return pl.ds(pl.multiple_of(lax.rem(2 * k + i + nt - d, nt) * TI, TI), TI)

                def add(cols):
                    def go(v):
                        acc_ref[:, cols] += v
                    return go

                rows = tile(0)
                for d in range(reach + 1):
                    cols = tile(d)
                    plan.append(dict(
                        rows=lambda rows=rows: st_ref[rows, :],
                        cols=lambda cols=cols: b_ref[0, :, cols],
                        weights=lambda cols=cols: w_ref[0, cols, :],
                        dd=lambda rows=rows: dd_ref[:, rows],
                        turn=i if d else None,
                        out=add(cols),
                        turned=add(rows) if d == reach else None,
                    ))
            sweep(plan, xs, ys, rs)

        pl.loop(0, half // 2)(lambda k: rows_pair(k, half))

        @pl.loop(half // 2, half)
        def _(k):
            @pl.when(jnp.logical_and(is_main, k == half - 1))
            def _():
                get_chunk(0)

            rows_pair(k, half - 1)

    def cross_tile(st, dd, cols, where, turn, turned):
        def add(v):
            pacc_ref[:, cols] += v

        return dict(
            rows=st,
            cols=lambda: b_ref[where, :, cols],
            weights=lambda: w_ref[where, cols, :],
            dd=dd,
            turn=turn,
            out=add,
            turned=turned,
        )

    def main_chunk(ci, xs, ys, rs, ahead=False):
        plan = []
        for i in range(CC // TI):
            rows = pl.ds(pl.multiple_of(ci * CC + i * TI, TI), TI)
            _, _, hf, lf, norm = parts(xb_p, rows)
            st = as_rows(hf, lf, norm)
            dd = both_halves(xb_d, rows)

            def turned(v, rows=rows):
                ret_out[:, rows] = v

            for jt in range(nt):
                cols = slice(jt * TI, (jt + 1) * TI)
                plan.append(cross_tile(lambda st=st: st, lambda dd=dd: dd, cols, 0, i % 2, turned if jt == nt - 1 else None))
        if ahead:
            plan[AHEAD]["first"] = [lambda: get_chunk(ci + 1)]
        sweep(plan, xs, ys, rs)
        give_back(ci).start()

    def help_columns(ci):
        for c in to_help(ci):
            c.wait_recv()
        for i in range(CC // CH):
            cols = slice(ci * CC + i * CH, ci * CC + (i + 1) * CH)
            h, l, _, _, norm = parts(zb_p, cols)
            b_ref[1, :, cols] = as_cols(h, l, norm)
            w_ref[1, cols, :] = as_weights(both_halves(zb_d, cols))

    def help_rows(ci):
        for c in relay(ci):
            c.wait_recv()
        for i in range(CC // CH):
            rows = slice(ci * CC + i * CH, ci * CC + (i + 1) * CH)
            _, _, hf, lf, norm = parts(xb_p, rows)
            sz_ref[rows, :] = as_rows(hf, lf, norm)
            dz_ref[:, rows] = both_halves(xb_d, rows)

    def help_part(ci, xs, ys, rs):
        per = CC // TI
        last = ci == nc - 1
        early, late = ci * per, (ci + 1) * per
        plan = []

        def add_tile(it, jt, ends, fresh):
            rows = slice(it * TI, (it + 1) * TI)

            def turned(v):
                if fresh:
                    ret_out[:, rows] = v
                else:
                    ret_out[:, rows] += v

            plan.append(cross_tile(
                lambda: sz_ref[rows, :], lambda: dz_ref[:, rows], slice(jt * TI, (jt + 1) * TI), 1, it % 2,
                turned if ends else None))

        for it in range(early):
            for jt in range(early, late):
                add_tile(it, jt, jt == late - 1, False)
        if last:
            plan[-1]["then"] = [hand_over(c).start for c in range(ci)]
        start = len(plan)
        for c in range(ci + 1):
            for it in range(early, late):
                for jt in range(c * per, (c + 1) * per):
                    add_tile(it, jt, c == ci and jt == late - 1, True)
            if last and c < nc - 2:
                plan[-1]["then"] = [give_rows(c).start]
        if last:
            plan[-1]["then"] = [hand_over(ci).start]
        plan[start]["first"] = [lambda: help_rows(ci)]
        sweep(plan, xs, ys, rs)

    def wide(w):
        return jnp.concatenate([w, jnp.zeros((w.shape[0], TI - w.shape[1]), w.dtype)], axis=1)

    def deep_dot(accs, lhs, rhs_of, count):
        for k in range(count):
            m, r = k % 2, (k // 2) % 2
            pltpu.matmul_push_rhs(rhs_of(k), r, m)
            pltpu.matmul_acc_lhs(accs[m], lhs(k), load_staged_rhs=r)
        return pltpu.matmul_pop(accs[0]) + pltpu.matmul_pop(accs[1])

    def block(k):
        return slice(k * TI, (k + 1) * TI)

    def skeleton(p0, p1, c0, c1, f0, f1):
        index = jnp.broadcast_to(wide(skel_ref[...] + 1), (TI, TI)) - 1

        def chosen(k):
            return jnp.where(lax.broadcasted_iota(jnp.int32, (TI, TI), 0) + k * TI == index, 1.0, 0.0).astype(bf16)

        picked = deep_dot((p0, p1), lambda k: b_ref[0, : 2 * feats, block(k)], chosen, n // TI)[:, :128]
        skel_rows = (picked[:feats] + picked[feats:]).T[:nskel]
        norm_s = jnp.sum(skel_rows * skel_rows, axis=1, keepdims=True)
        sh, sl = split(skel_rows)
        sh, sl = sh.astype(f32) * -2.0, sl.astype(f32) * -2.0
        n1 = norm_s.astype(bf16).astype(f32)
        n2 = (norm_s - n1).astype(bf16).astype(f32)
        lane_s = lax.broadcasted_iota(jnp.int32, (nskel, feats), 1)
        ext_s = jnp.where(lane_s == 0, n1, jnp.where(lane_s == 1, n2, jnp.where(lane_s == 2, norm_s - n1 - n2, jnp.where(lane_s < 6, 1.0, 0.0))))
        probe = jnp.concatenate([sh, sh, sl, ext_s], axis=1).astype(bf16)
        cs = (c0, c1)
        for k in range(n // TI):
            m, r = k % 2, (k // 2) % 2
            pltpu.matmul_push_rhs(b_ref[0, :, block(k)], r, m)
            pltpu.matmul_acc_lhs(cs[m], probe, load_staged_rhs=r)
            h, l = split(matern_of(pltpu.matmul_pop(cs[m])))
            ks_ref[: 3 * nskel, block(k)] = jnp.concatenate([h, l, h], axis=0)
        part = deep_dot((f0, f1), lambda k: ks_ref[: 2 * nskel, block(k)], lambda k: wide(w_ref[0, block(k), :]), n // TI)
        coeff_t = part[:nskel, :rhs] + part[:nskel, rhs : 2 * rhs] + part[nskel:, :rhs] + part[nskel:, rhs : 2 * rhs]
        pad = jnp.zeros((nskel, 128 - feats - rhs - 2), f32)
        pack = jnp.concatenate([skel_rows, coeff_t, n1, norm_s - n1, pad], axis=1)
        ag_ref[my_rows, :] = pack
        tg_ref[pair] = pack

    my_rows = pl.ds(pl.multiple_of(leaf * nskel, 8), nskel)
    pl.run_scoped(
        skeleton,
        pltpu.ACC(0)((2 * feats, TI), f32), pltpu.ACC(1)((2 * feats, TI), f32),
        pltpu.ACC(0)((nskel, TI), f32), pltpu.ACC(1)((nskel, TI), f32),
        pltpu.ACC(0)((2 * nskel, TI), f32), pltpu.ACC(1)((2 * nskel, TI), f32),
    )

    stage_a = [
        remote(ag_ref.at[my_rows, :], ag_ref.at[my_rows, :], as_sem.at[k], ar_sem.at[k], leaf=leaf_peer(k))
        for k in range(1, nleaf)
    ]
    stage_t = [
        remote(tg_ref.at[pair], tg_ref.at[pair], bs_sem.at[k], br_sem.at[k], pair=pair_peer(k))
        for k in range(1, npair)
    ]
    stage_q = [
        remote(qo_ref.at[pair_peer(k)], qi_ref.at[pair], qs_sem.at[k], qr_sem.at[k], pair=pair_peer(k))
        for k in range(1, npair)
    ]
    for c in stage_a + stage_t:
        c.start()
    send_block(FIRST, nc)

    group = TI // (2 * nskel)

    def far_field(xs, rs):
        for k, c in enumerate(stage_a, 1):
            src_rows = pl.ds(pl.multiple_of(lax.rem(leaf + nleaf - k, nleaf) * nskel, 8), nskel)
            remote(ag_ref.at[src_rows, :], ag_ref.at[src_rows, :], as_sem.at[k], ar_sem.at[k], leaf=leaf_peer(k)).wait_recv()
        for k, c in enumerate(stage_t, 1):
            src = lax.rem(pair + npair - k, npair)
            remote(tg_ref.at[src], tg_ref.at[src], bs_sem.at[k], br_sem.at[k], pair=pair_peer(k)).wait_recv()
        lane_o = lax.broadcasted_iota(jnp.int32, (nskel, 128), 1)
        ones = jnp.logical_and(lane_o >= feats + rhs, lane_o < feats + rhs + 2)
        for first in range(0, npair, group):
            probes, norms = [], []
            for p in range(first, first + group):
                target = jnp.where(lane_o < feats, tg_ref[p], 0.0)
                norms.append(jnp.sum(target * target, axis=1, keepdims=True))
                oh, ol = split(target)
                oh = jnp.where(ones, 1.0, oh.astype(f32) * -2.0).astype(bf16)
                ol = (ol.astype(f32) * -2.0).astype(bf16)
                probes += [jnp.concatenate([oh, oh], axis=1), jnp.concatenate([ol, jnp.zeros_like(ol)], axis=1)]
            probe = jnp.concatenate(probes, axis=0)
            for g in range(nleaf * nskel // TI):
                both = jnp.concatenate(split(ag_ref[block(g), :]), axis=1)
                pltpu.matmul_push_rhs(both, 0, 0, transpose=True)
                pltpu.matmul_acc_lhs(rs[0], probe, load_staged_rhs=0)
                u = pltpu.matmul_pop(rs[0])
                near_mask = jnp.abs(lax.div(lax.broadcasted_iota(jnp.int32, (nskel, TI), 1) + g * TI, nskel) - leaf) <= 1
                weights = []
                for i in range(group):
                    lo = 2 * i * nskel
                    w = matern_of(norms[i] + u[lo : lo + nskel] + u[lo + nskel : lo + 2 * nskel])
                    same = jnp.full((nskel, TI), pair, jnp.int32) == first + i
                    weights += list(split(jnp.where(jnp.logical_and(same, near_mask), 0.0, w)))
                pltpu.matmul_push_rhs(both, 0, 1)
                pltpu.matmul_acc_lhs(xs[0], jnp.concatenate(weights, axis=0), load_staged_rhs=0)
            q = pltpu.matmul_pop(xs[0])
            q = q[:, :128] + q[:, 128:]
            for i in range(group):
                lo = 2 * i * nskel
                qo_ref[first + i] = q[lo : lo + nskel] + q[lo + nskel : lo + 2 * nskel]
        for c in stage_q:
            c.start()

    amplitude = 1.0 / math.sqrt(3.0 * n)
    lane = lax.broadcasted_iota(jnp.int32, (rhs, 128), 1)

    def near(x0, x1, y0, y1, r0, r1):
        xs, ys, rs = (x0, x1), (y0, y1), (r0, r1)
        own_block(xs, ys, rs)
        loads[4].wait()
        squares = jnp.sum(res_ref[...] * res_ref[...], axis=1, keepdims=True)
        curvature = jnp.sum(dir_ref[...] * (nugget * dir_ref[...] + amplitude * acc_ref[...]), axis=1, keepdims=True)
        curv_ref[...] = jnp.where(lane == 0, squares, jnp.where(lane == 1, curvature, 0.0))

        @pl.when(is_main)
        def _():
            @pl.loop(0, nc - 2)
            def _(ci):
                main_chunk(ci, xs, ys, rs, ahead=True)

            main_chunk(nc - 2, xs, ys, rs)

        @pl.when(helping)
        def _():
            for ci in range(nc - 1):
                help_columns(ci)
                help_part(ci, xs, ys, rs)

        far_field(xs, rs)

        @pl.when(is_main)
        def _():
            get_chunk(nc - 1)
            main_chunk(nc - 1, xs, ys, rs)

        @pl.when(helping)
        def _():
            help_columns(nc - 1)
            help_part(nc - 1, xs, ys, rs)

    pl.run_scoped(
        near,
        pltpu.ACC(1)((TI, TI), f32), pltpu.ACC(1)((TI, TI), f32),
        pltpu.ACC(0)((rhs, TI), f32), pltpu.ACC(1)((rhs, TI), f32),
        pltpu.ACC(0)((TI, TI), f32), pltpu.ACC(0)((TI, TI), f32),
    )

    def add_pair(d_ref):
        shared = jnp.sum(d_ref[...] * pacc_ref[...], axis=1, keepdims=True)
        curv_ref[...] += jnp.where(lane == 1, (2.0 * amplitude) * shared, 0.0)

    @pl.when(is_main)
    def _():
        add_pair(dir_ref)

    @pl.when(helping)
    def _():
        add_pair(zb_d)

    q_t = qo_ref[pair]
    for k in range(1, npair):
        src = lax.rem(pair + npair - k, npair)
        remote(qo_ref.at[src], qi_ref.at[src], qs_sem.at[k], qr_sem.at[k], pair=pair_peer(k)).wait_recv()
        q_t = q_t + qi_ref[src]
    far_row = (amplitude * far_weight) * jnp.sum(q_t * tg_ref[pair], axis=0, keepdims=True)[:, feats : feats + rhs]
    both = jnp.concatenate([curv_ref[...], jnp.zeros((128 - rhs, 128), f32)], axis=0).T
    both = jnp.concatenate([both[0:1, :rhs], both[1:2, :rhs] + far_row, jnp.zeros((1, 128 - 2 * rhs), f32)], axis=1)
    one_stage = nleaf * npair <= 64
    sends_b = []
    if one_stage:
        def partial(l, p):
            return red_a.at[p * nleaf + l]

        red_a[pair * nleaf + leaf] = both
        hops = [(a, b) for b in range(npair) for a in range(nleaf) if a or b]
        sends = [
            remote(partial(leaf, pair), partial(leaf, pair), cs_sem.at[a, b], cr_sem.at[a, b], leaf=leaf_peer(a), pair=pair_peer(b))
            for a, b in hops
        ]
    else:
        red_a[leaf] = both
        sends = [
            remote(red_a.at[leaf], red_a.at[leaf], cs_sem.at[k, 0], cr_sem.at[k, 0], leaf=leaf_peer(k))
            for k in range(1, nleaf)
        ]
    for c in sends:
        c.start()

    def spread(g0, g1):
        gs = (g0, g1)
        qh, ql = split(q_t[:, feats : feats + rhs].T)
        probe = wide(jnp.concatenate([qh, qh, ql], axis=1))
        for k in range(n // TI):
            m, r = k % 2, (k // 2) % 2
            pltpu.matmul_push_rhs(ks_ref[:, block(k)], r, m)
            pltpu.matmul_acc_lhs(gs[m], probe, load_staged_rhs=r)
            far = pltpu.matmul_pop(gs[m])
            prod_ref[:, block(k)] = nugget * dir_ref[:, block(k)] + amplitude * (acc_ref[:, block(k)] + far_weight * far)

    @pl.when(helping)
    def _():
        for ci in range(max(nc - 2, 0), nc):
            give_rows(ci).start()

    def pass_on():
        @pl.when(jnp.logical_and(is_main, chip_two))
        def _():
            for ci in range(nc):
                hand_over(ci).wait_recv()
                forward(ci).start()

    pl.run_scoped(spread, pltpu.ACC(0)((rhs, TI), f32), pltpu.ACC(1)((rhs, TI), f32))
    pass_on()

    @pl.when(is_main)
    def _():
        prod_ref[...] += amplitude * pacc_ref[...]

    def returned(k, ci):
        cols = chunk(ci)
        return remote(ret_out.at[:, cols], ret_in.at[k, :, cols], es_sem.at[ci], er_sem.at[k, ci], leaf=home_leaf, pair=pair)

    @pl.when(back_ok)
    def _():
        for ci in range(nc):
            give_rows(ci).wait_recv()
        prod_ref[...] += amplitude * ret_in[0]

    @pl.when(is_help)
    def _():
        for ci in range(nc):
            returned(0, ci).wait_recv()
        prod_ref[...] += amplitude * ret_in[0]

    @pl.when(home_two)
    def _():
        for ci in range(nc):
            returned(1, ci).wait_recv()
        prod_ref[...] += amplitude * ret_in[1]

    store = pltpu.make_async_copy(prod_ref, prod_hbm, out_sem)
    store.start()

    if one_stage:
        for a, b in hops:
            src = partial(lax.rem(leaf + nleaf - a, nleaf), lax.rem(pair + npair - b, npair))
            remote(src, src, cs_sem.at[a, b], cr_sem.at[a, b], leaf=leaf_peer(a), pair=pair_peer(b)).wait_recv()
        total = jnp.sum(red_a[...], axis=0)
    else:
        for k in range(1, nleaf):
            src = lax.rem(leaf + nleaf - k, nleaf)
            remote(red_a.at[src], red_a.at[src], cs_sem.at[k, 0], cr_sem.at[k, 0], leaf=leaf_peer(k)).wait_recv()
        red_b[pair] = jnp.sum(red_a[:nleaf], axis=0)
        sends_b = [
            remote(red_b.at[pair], red_b.at[pair], ds_sem.at[k], dr_sem.at[k], pair=pair_peer(k))
            for k in range(1, npair)
        ]
        for c in sends_b:
            c.start()
        for k in range(1, npair):
            src = lax.rem(pair + npair - k, npair)
            remote(red_b.at[src], red_b.at[src], ds_sem.at[k], dr_sem.at[k], pair=pair_peer(k)).wait_recv()
        total = jnp.sum(red_b[...], axis=0)
    total = total * (1.0 / (n * nleaf * npair))
    dots_ref[...] = jnp.concatenate([total[:, :rhs], total[:, rhs : 2 * rhs]], axis=0)
    store_dots = pltpu.make_async_copy(dots_ref, dots_hbm, in_sem.at[0])
    store_dots.start()

    for c in sends + sends_b + stage_a + stage_t + stage_q:
        c.wait_send()

    @pl.when(is_main)
    def _():
        for ci in range(nc):
            give_back(ci).wait_send()

    @pl.when(jnp.logical_and(is_main, chip_two))
    def _():
        for ci in range(nc):
            forward(ci).wait_send()

    @pl.when(helping)
    def _():
        for ci in range(nc):
            hand_over(ci).wait_send()

    @pl.when(helping)
    def _():
        for ci in range(nc):
            give_rows(ci).wait_send()

    @pl.when(is_main)
    def _():
        for ci in range(nc):
            for c in relay(ci):
                c.wait_send()

    @pl.when(jnp.logical_and(is_help, jnp.logical_not(chip_two)))
    def _():
        for ci in range(nc):
            for c in relay(ci):
                c.wait_recv()

    @pl.when(is_help)
    def _():
        for ci in range(nc):
            for c in to_main(ci):
                c.wait_send()

    @pl.when(back_ok)
    def _():
        for ci in range(nc):
            for c in to_help(ci):
                c.wait_send()

    store.wait()
    store_dots.wait()


def on_device(points, inv_scales, direction, residual, skeleton):
    feats, n = points.shape
    rhs = direction.shape[0]
    nskel = skeleton.shape[1]
    nleaf = lax.axis_size("leaf")
    npair = lax.axis_size("pair")
    anywhere = pl.BlockSpec(memory_space=pl.ANY)
    dma = pltpu.SemaphoreType.DMA
    nc = n // CC
    return pl.pallas_call(
        functools.partial(kernel, nleaf, npair),
        out_shape=(jax.ShapeDtypeStruct((rhs, n), f32), jax.ShapeDtypeStruct((2, rhs), f32)),
        in_specs=[pl.BlockSpec(memory_space=pltpu.HBM)] * 5,
        out_specs=(anywhere, anywhere),
        scratch_shapes=[
            pltpu.VMEM((feats, n), f32),
            pltpu.VMEM((1, feats), f32),
            pltpu.VMEM((rhs, n), f32),
            pltpu.VMEM((rhs, n), f32),
            pltpu.VMEM((1, nskel), jnp.int32),
            pltpu.VMEM((rhs, n), f32),
            pltpu.VMEM((2, rhs), f32),
            pltpu.VMEM((feats, n), f32),
            pltpu.VMEM((rhs, n), f32),
            pltpu.VMEM((feats, n), f32),
            pltpu.VMEM((rhs, n), f32),
            pltpu.VMEM((rhs, n), f32),
            pltpu.VMEM((rhs, n), f32),
            pltpu.VMEM((2, rhs, n), f32),
            pltpu.VMEM((2, 4 * feats, n), bf16),
            pltpu.VMEM((n, 4 * feats), bf16),
            pltpu.VMEM((2 * rhs, n), bf16),
            pltpu.VMEM((2, n, 128), bf16),
            pltpu.VMEM((rhs, n), f32),
            pltpu.VMEM((rhs, n), f32),
            pltpu.VMEM((TI, n), bf16),
            pltpu.VMEM((nleaf * nskel, 128), f32),
            pltpu.VMEM((npair, nskel, 128), f32),
            pltpu.VMEM((npair, nskel, 128), f32),
            pltpu.VMEM((npair, nskel, 128), f32),
            pltpu.VMEM((n, 4 * feats), bf16),
            pltpu.VMEM((2 * rhs, n), bf16),
            pltpu.VMEM((nleaf * npair if nleaf * npair <= 64 else nleaf, 1, 128), f32),
            pltpu.VMEM((npair, 1, 128), f32),
            pltpu.VMEM((rhs, 128), f32),
            dma((5,)), dma,
            dma((2, nc)), dma((2, nc)),
            dma((2, nc)), dma((2, nc)),
            dma((nc,)), dma((2, nc)),
            dma((nc,)), dma((nc,)),
            dma((nc,)), dma((nc,)),
            dma((nleaf,)), dma((nleaf,)),
            dma((npair,)), dma((npair,)),
            dma((npair,)), dma((npair,)),
            dma((nleaf, npair)), dma((nleaf, npair)),
            dma((npair,)), dma((npair,)),
        ],
        compiler_params=pltpu.CompilerParams(collective_id=0, has_side_effects=True, vmem_limit_bytes=40 * 1024 * 1024),
        name="matern_step",
    )(*[pltpu.with_memory_space_constraint(v, pltpu.HBM) for v in (points, inv_scales.reshape(1, feats), direction, residual, skeleton)])


def solution(mesh):
    return jax.shard_map(
        on_device,
        mesh=mesh,
        in_specs=(
            P(None, ("pair", "leaf")),
            P(),
            P(None, ("pair", "leaf")),
            P(None, ("pair", "leaf")),
            P(("pair", "leaf"), None),
        ),
        out_specs=(P(None, ("pair", "leaf")), P()),
        check_vma=False,
    )
```

```python
import functools
import math

import jax
import jax.numpy as jnp
from jax import lax
from jax.experimental import pallas as pl
from jax.experimental.pallas import tpu as pltpu
from jax.sharding import PartitionSpec as P

root_three = math.sqrt(3.0)
neg_log2e = -1.4426950408889634
nugget = 0.5
far_weight = 0.125
tiny = 1e-30
f32 = jnp.float32
bf16 = jnp.bfloat16
TI = 256
CC = 512
FIRST = 3
EARLY = 4
AHEAD = 8
CH = 256


def matern_of(u):
    u = jnp.maximum(u, tiny)
    t = u * lax.rsqrt(u)
    return (1.0 + t) * jnp.exp2(t * neg_log2e)


def split(x):
    h = x.astype(bf16)
    return h, (x - h.astype(f32)).astype(bf16)


def kernel(
    nleaf, npair,
    pts_hbm, inv_hbm, dir_hbm, res_hbm, skel_hbm,
    prod_hbm, dots_ref,
    pts_ref, inv_ref, dir_ref, res_ref, skel_ref, prod_ref,
    xb_p, xb_d, zb_p, zb_d, ret_out, fwd_ref, ret_in, b_ref, st_ref, dd_ref, w_ref, acc_ref, pacc_ref, ks_ref, ag_ref, tg_ref, qo_ref, qi_ref, sz_ref, dz_ref, red_a, red_b, curv_ref,
    in_sem, out_sem, hs_sem, hr_sem, fs_sem, fr_sem, es_sem, er_sem, gs_sem, gr_sem, ps_sem, pr_sem, as_sem, ar_sem, bs_sem, br_sem, qs_sem, qr_sem, cs_sem, cr_sem, ds_sem, dr_sem,
):
    feats, n = pts_ref.shape
    rhs = dir_ref.shape[0]
    nskel = skel_ref.shape[1]
    leaf = lax.axis_index("leaf")
    pair = lax.axis_index("pair")

    leaf_odd = lax.rem(leaf, 2)
    pair_odd = lax.rem(pair, 2)
    is_main = leaf_odd == pair_odd
    is_help = leaf_odd != pair_odd
    step = 1 - 2 * leaf_odd
    other = pair + 1 - 2 * pair_odd
    far_leaf = leaf + 2 * step
    chip_two = jnp.logical_and(far_leaf >= 0, far_leaf < nleaf)
    helping = jnp.logical_and(is_help, chip_two)
    back_leaf = leaf - 2 * step
    back_ok = jnp.logical_and(is_main, jnp.logical_and(back_leaf >= 0, back_leaf < nleaf))
    home_step = 1 - 2 * pair_odd
    home_leaf = leaf - home_step
    home_far = home_leaf + 2 * home_step
    home_two = jnp.logical_and(is_help, jnp.logical_and(home_far >= 0, home_far < nleaf))

    def remote(src, dst, ss, rs, **dev):
        return pltpu.make_async_remote_copy(
            src_ref=src, dst_ref=dst, send_sem=ss, recv_sem=rs, device_id=dev,
            device_id_type=pl.DeviceIdType.MESH)

    def leaf_peer(k):
        return lax.rem(leaf + k, nleaf)

    def pair_peer(k):
        return lax.rem(pair + k, npair)

    loads = [
        pltpu.make_async_copy(src, dst, in_sem.at[k])
        for k, (src, dst) in enumerate((
            (inv_hbm, inv_ref), (pts_hbm, pts_ref), (dir_hbm, dir_ref), (skel_hbm, skel_ref), (res_hbm, res_ref)))
    ]
    for c in loads:
        c.start()

    barrier = pltpu.get_barrier_semaphore()

    def greet(**dev):
        pl.semaphore_signal(barrier, inc=1, device_id=dev, device_id_type=pl.DeviceIdType.MESH)

    for k in range(1, nleaf):
        greet(leaf=leaf_peer(k))
    for k in range(1, npair):
        greet(pair=pair_peer(k))

    @pl.when(back_ok)
    def _():
        greet(leaf=back_leaf, pair=other)

    @pl.when(helping)
    def _():
        greet(leaf=far_leaf, pair=other)

    def chunk(ci):
        return pl.ds(pl.multiple_of(ci * CC, CC), CC)

    def block_copies(ci, src_p, src_d, dst_p, dst_d, ss, rs, dev):
        cols = chunk(ci)
        return (
            remote(src_p.at[:, cols], dst_p.at[:, cols], ss.at[0, ci], rs.at[0, ci], **dev),
            remote(src_d.at[:, cols], dst_d.at[:, cols], ss.at[1, ci], rs.at[1, ci], **dev),
        )

    def to_main(ci):
        return block_copies(ci, pts_ref, dir_ref, xb_p, xb_d, hs_sem, hr_sem, dict(leaf=home_leaf, pair=pair))

    def to_help(ci):
        return block_copies(ci, pts_ref, dir_ref, zb_p, zb_d, hs_sem, hr_sem, dict(leaf=back_leaf, pair=other))

    def relay(ci):
        return block_copies(ci, xb_p, xb_d, xb_p, xb_d, fs_sem, fr_sem, dict(leaf=leaf, pair=other))

    def give_back(ci):
        cols = chunk(ci)
        return remote(ret_out.at[:, cols], ret_in.at[0, :, cols], es_sem.at[ci], er_sem.at[0, ci], leaf=leaf + step, pair=pair)

    def hand_over(ci):
        cols = chunk(ci)
        return remote(ret_out.at[:, cols], fwd_ref.at[:, cols], es_sem.at[ci], gr_sem.at[ci], leaf=leaf, pair=other)

    def forward(ci):
        cols = chunk(ci)
        return remote(fwd_ref.at[:, cols], ret_in.at[1, :, cols], gs_sem.at[ci], er_sem.at[1, ci], leaf=leaf + step, pair=pair)

    def give_rows(ci):
        cols = chunk(ci)
        return remote(pacc_ref.at[:, cols], ret_in.at[0, :, cols], ps_sem.at[ci], pr_sem.at[ci], leaf=far_leaf, pair=other)

    nc = n // CC

    def send_block(lo, hi):
        @pl.when(is_help)
        def _():
            for ci in range(lo, hi):
                for c in to_main(ci):
                    c.start()

        @pl.when(back_ok)
        def _():
            for ci in range(lo, hi):
                for c in to_help(ci):
                    c.start()

    for c in loads[:4]:
        c.wait()

    eye = lax.broadcasted_iota(jnp.int32, (feats, feats), 0) == lax.broadcasted_iota(jnp.int32, (feats, feats), 1)
    inv_col = jnp.sum(jnp.where(eye, jnp.broadcast_to(inv_ref[...], (feats, feats)), 0.0), axis=1, keepdims=True) * root_three

    def norm_rows(norm):
        n1 = norm.astype(bf16).astype(f32)
        n2 = (norm - n1).astype(bf16).astype(f32)
        return jnp.concatenate([n1, n2, norm - n1 - n2], axis=0)

    def parts(p_src, cols):
        p = p_src[:, cols] * inv_col
        h, l = split(p)
        hf, lf = h.astype(f32), l.astype(f32)
        q = hf + lf
        norm = norm_rows(jnp.sum(q * q, axis=0, keepdims=True))
        return h, l, hf, lf, norm

    def as_cols(h, l, norm):
        w = norm.shape[1]
        ext = jnp.concatenate([jnp.ones((3, w), f32), norm, jnp.zeros((feats - 6, w), f32)], axis=0)
        return jnp.concatenate([h, l, h, ext.astype(bf16)], axis=0)

    def as_rows(hf, lf, norm):
        w = norm.shape[1]
        ext = jnp.concatenate([norm, jnp.ones((3, w), f32), jnp.zeros((feats - 6, w), f32)], axis=0)
        h2 = hf * -2.0
        return jnp.concatenate([h2, h2, lf * -2.0, ext], axis=0).T.astype(bf16)

    def both_halves(d_src, cols):
        return jnp.concatenate(split(d_src[:, cols]), axis=0)

    def as_weights(dd):
        w = dd.shape[1]
        return jnp.concatenate([dd.astype(f32), jnp.zeros((128 - 2 * rhs, w), f32)], axis=0).T.astype(bf16)

    def prepare(ci):
        cols = pl.ds(pl.multiple_of(ci * CH, CH), CH)
        h, l, hf, lf, norm = parts(pts_ref, cols)
        b_ref[0, :, cols] = as_cols(h, l, norm)
        st_ref[cols, :] = as_rows(hf, lf, norm)
        dd = both_halves(dir_ref, cols)
        dd_ref[:, cols] = dd
        w_ref[0, cols, :] = as_weights(dd)
        ks_ref[3 * nskel :, cols] = jnp.zeros((TI - 3 * nskel, CH), bf16)
        acc_ref[:, cols] = jnp.zeros((rhs, CH), f32)
        pacc_ref[:, cols] = jnp.zeros((rhs, CH), f32)

    pl.loop(0, EARLY)(prepare)

    extra = jnp.where(jnp.logical_or(back_ok, helping), 1, 0)
    pl.semaphore_wait(barrier, nleaf - 1 + npair - 1 + extra)

    send_block(0, FIRST)

    pl.loop(EARLY, n // CH)(prepare)

    nt = n // TI

    def sweep(plan, xs, ys, rs):
        stage = [0, 0]

        def push(v, m):
            k = stage[m]
            stage[m] = 1 - k
            pltpu.matmul_push_rhs(v, k, m)
            return k

        def cross(t):
            for go in plan[t].get("first", ()):
                go()
            pltpu.matmul_acc_lhs(xs[t % 2], plan[t]["rows"](), load_staged_rhs=push(plan[t]["cols"](), 1))

        def spend(t, k):
            p = plan[t]
            if p["turn"] is not None:
                w = p["weights"]()
                w = jnp.concatenate([w, jnp.zeros_like(w)], axis=1)
                pltpu.matmul_acc_lhs(rs[p["turn"]], k, load_staged_rhs=push(w, 0))
            m = t % 2
            dd = p["dd"]()
            pltpu.matmul_acc_lhs(ys[m], dd[:rhs], load_staged_rhs=push(k, m))
            pltpu.matmul_acc_lhs(ys[m], dd[rhs:])

        def finish(t):
            p = plan[t]
            p["out"](pltpu.matmul_pop(ys[t % 2]))
            if p["turned"] is not None:
                r = pltpu.matmul_pop(rs[p["turn"]])[:, :128].T
                p["turned"](r[:rhs] + r[rhs : 2 * rhs])
            for go in p.get("then", ()):
                go()

        count = len(plan)
        cross(0)
        held = None
        for t in range(count + 2):
            k = None
            if t < count:
                k = matern_of(pltpu.matmul_pop(xs[t % 2])).astype(bf16)
            if t + 1 < count:
                cross(t + 1)
            if 0 < t <= count:
                spend(t - 1, held)
            held = k
            if t > 1:
                finish(t - 2)

    def get_chunk(ci):
        for c in to_main(ci):
            c.wait_recv()
        for c in relay(ci):
            c.start()

    def own_block(xs, ys, rs):
        half = nt // 2

        def rows_pair(k, reach):
            plan = []
            for i in range(2):
                def tile(d, i=i):
                    return pl.ds(pl.multiple_of(lax.rem(2 * k + i + nt - d, nt) * TI, TI), TI)

                def add(cols):
                    def go(v):
                        acc_ref[:, cols] += v
                    return go

                rows = tile(0)
                for d in range(reach + 1):
                    cols = tile(d)
                    plan.append(dict(
                        rows=lambda rows=rows: st_ref[rows, :],
                        cols=lambda cols=cols: b_ref[0, :, cols],
                        weights=lambda cols=cols: w_ref[0, cols, :],
                        dd=lambda rows=rows: dd_ref[:, rows],
                        turn=i if d else None,
                        out=add(cols),
                        turned=add(rows) if d == reach else None,
                    ))
            sweep(plan, xs, ys, rs)

        pl.loop(0, half // 2)(lambda k: rows_pair(k, half))

        @pl.loop(half // 2, half)
        def _(k):
            @pl.when(jnp.logical_and(is_main, k == half - 1))
            def _():
                get_chunk(0)

            rows_pair(k, half - 1)

    def cross_tile(st, dd, cols, where, turn, turned):
        def add(v):
            pacc_ref[:, cols] += v

        return dict(
            rows=st,
            cols=lambda: b_ref[where, :, cols],
            weights=lambda: w_ref[where, cols, :],
            dd=dd,
            turn=turn,
            out=add,
            turned=turned,
        )

    def main_chunk(ci, xs, ys, rs, ahead=False):
        plan = []
        for i in range(CC // TI):
            rows = pl.ds(pl.multiple_of(ci * CC + i * TI, TI), TI)
            _, _, hf, lf, norm = parts(xb_p, rows)
            st = as_rows(hf, lf, norm)
            dd = both_halves(xb_d, rows)

            def turned(v, rows=rows):
                ret_out[:, rows] = v

            for jt in range(nt):
                cols = slice(jt * TI, (jt + 1) * TI)
                plan.append(cross_tile(lambda st=st: st, lambda dd=dd: dd, cols, 0, i % 2, turned if jt == nt - 1 else None))
        if ahead:
            plan[AHEAD]["first"] = [lambda: get_chunk(ci + 1)]
        sweep(plan, xs, ys, rs)
        give_back(ci).start()

    def help_columns(ci):
        for c in to_help(ci):
            c.wait_recv()
        for i in range(CC // CH):
            cols = slice(ci * CC + i * CH, ci * CC + (i + 1) * CH)
            h, l, _, _, norm = parts(zb_p, cols)
            b_ref[1, :, cols] = as_cols(h, l, norm)
            w_ref[1, cols, :] = as_weights(both_halves(zb_d, cols))

    def help_rows(ci):
        for c in relay(ci):
            c.wait_recv()
        for i in range(CC // CH):
            rows = slice(ci * CC + i * CH, ci * CC + (i + 1) * CH)
            _, _, hf, lf, norm = parts(xb_p, rows)
            sz_ref[rows, :] = as_rows(hf, lf, norm)
            dz_ref[:, rows] = both_halves(xb_d, rows)

    def help_part(ci, xs, ys, rs):
        per = CC // TI
        last = ci == nc - 1
        early, late = ci * per, (ci + 1) * per
        plan = []

        def add_tile(it, jt, ends, fresh):
            rows = slice(it * TI, (it + 1) * TI)

            def turned(v):
                if fresh:
                    ret_out[:, rows] = v
                else:
                    ret_out[:, rows] += v

            plan.append(cross_tile(
                lambda: sz_ref[rows, :], lambda: dz_ref[:, rows], slice(jt * TI, (jt + 1) * TI), 1, it % 2,
                turned if ends else None))

        for it in range(early):
            for jt in range(early, late):
                add_tile(it, jt, jt == late - 1, False)
        if last:
            plan[-1]["then"] = [hand_over(c).start for c in range(ci)]
        start = len(plan)
        for c in range(ci + 1):
            for it in range(early, late):
                for jt in range(c * per, (c + 1) * per):
                    add_tile(it, jt, c == ci and jt == late - 1, True)
            if last and c < nc - 2:
                plan[-1]["then"] = [give_rows(c).start]
        if last:
            plan[-1]["then"] = [hand_over(ci).start]
        plan[start]["first"] = [lambda: help_rows(ci)]
        sweep(plan, xs, ys, rs)

    def wide(w):
        return jnp.concatenate([w, jnp.zeros((w.shape[0], TI - w.shape[1]), w.dtype)], axis=1)

    def deep_dot(accs, lhs, rhs_of, count):
        for k in range(count):
            m, r = k % 2, (k // 2) % 2
            pltpu.matmul_push_rhs(rhs_of(k), r, m)
            pltpu.matmul_acc_lhs(accs[m], lhs(k), load_staged_rhs=r)
        return pltpu.matmul_pop(accs[0]) + pltpu.matmul_pop(accs[1])

    def block(k):
        return slice(k * TI, (k + 1) * TI)

    def skeleton(p0, p1, c0, c1, f0, f1):
        index = jnp.broadcast_to(wide(skel_ref[...] + 1), (TI, TI)) - 1

        def chosen(k):
            return jnp.where(lax.broadcasted_iota(jnp.int32, (TI, TI), 0) + k * TI == index, 1.0, 0.0).astype(bf16)

        picked = deep_dot((p0, p1), lambda k: b_ref[0, : 2 * feats, block(k)], chosen, n // TI)[:, :128]
        skel_rows = (picked[:feats] + picked[feats:]).T[:nskel]
        norm_s = jnp.sum(skel_rows * skel_rows, axis=1, keepdims=True)
        sh, sl = split(skel_rows)
        sh, sl = sh.astype(f32) * -2.0, sl.astype(f32) * -2.0
        n1 = norm_s.astype(bf16).astype(f32)
        n2 = (norm_s - n1).astype(bf16).astype(f32)
        lane_s = lax.broadcasted_iota(jnp.int32, (nskel, feats), 1)
        ext_s = jnp.where(lane_s == 0, n1, jnp.where(lane_s == 1, n2, jnp.where(lane_s == 2, norm_s - n1 - n2, jnp.where(lane_s < 6, 1.0, 0.0))))
        probe = jnp.concatenate([sh, sh, sl, ext_s], axis=1).astype(bf16)
        cs = (c0, c1)
        for k in range(n // TI):
            m, r = k % 2, (k // 2) % 2
            pltpu.matmul_push_rhs(b_ref[0, :, block(k)], r, m)
            pltpu.matmul_acc_lhs(cs[m], probe, load_staged_rhs=r)
            h, l = split(matern_of(pltpu.matmul_pop(cs[m])))
            ks_ref[: 3 * nskel, block(k)] = jnp.concatenate([h, l, h], axis=0)
        part = deep_dot((f0, f1), lambda k: ks_ref[: 2 * nskel, block(k)], lambda k: wide(w_ref[0, block(k), :]), n // TI)
        coeff_t = part[:nskel, :rhs] + part[:nskel, rhs : 2 * rhs] + part[nskel:, :rhs] + part[nskel:, rhs : 2 * rhs]
        pad = jnp.zeros((nskel, 128 - feats - rhs - 2), f32)
        pack = jnp.concatenate([skel_rows, coeff_t, n1, norm_s - n1, pad], axis=1)
        ag_ref[my_rows, :] = pack
        tg_ref[pair] = pack

    my_rows = pl.ds(pl.multiple_of(leaf * nskel, 8), nskel)
    pl.run_scoped(
        skeleton,
        pltpu.ACC(0)((2 * feats, TI), f32), pltpu.ACC(1)((2 * feats, TI), f32),
        pltpu.ACC(0)((nskel, TI), f32), pltpu.ACC(1)((nskel, TI), f32),
        pltpu.ACC(0)((2 * nskel, TI), f32), pltpu.ACC(1)((2 * nskel, TI), f32),
    )

    stage_a = [
        remote(ag_ref.at[my_rows, :], ag_ref.at[my_rows, :], as_sem.at[k], ar_sem.at[k], leaf=leaf_peer(k))
        for k in range(1, nleaf)
    ]
    stage_t = [
        remote(tg_ref.at[pair], tg_ref.at[pair], bs_sem.at[k], br_sem.at[k], pair=pair_peer(k))
        for k in range(1, npair)
    ]
    stage_q = [
        remote(qo_ref.at[pair_peer(k)], qi_ref.at[pair], qs_sem.at[k], qr_sem.at[k], pair=pair_peer(k))
        for k in range(1, npair)
    ]
    for c in stage_a + stage_t:
        c.start()
    send_block(FIRST, nc)

    group = TI // (2 * nskel)

    def far_field(xs, rs):
        for k, c in enumerate(stage_a, 1):
            src_rows = pl.ds(pl.multiple_of(lax.rem(leaf + nleaf - k, nleaf) * nskel, 8), nskel)
            remote(ag_ref.at[src_rows, :], ag_ref.at[src_rows, :], as_sem.at[k], ar_sem.at[k], leaf=leaf_peer(k)).wait_recv()
        for k, c in enumerate(stage_t, 1):
            src = lax.rem(pair + npair - k, npair)
            remote(tg_ref.at[src], tg_ref.at[src], bs_sem.at[k], br_sem.at[k], pair=pair_peer(k)).wait_recv()
        lane_o = lax.broadcasted_iota(jnp.int32, (nskel, 128), 1)
        ones = jnp.logical_and(lane_o >= feats + rhs, lane_o < feats + rhs + 2)
        for first in range(0, npair, group):
            probes, norms = [], []
            for p in range(first, first + group):
                target = jnp.where(lane_o < feats, tg_ref[p], 0.0)
                norms.append(jnp.sum(target * target, axis=1, keepdims=True))
                oh, ol = split(target)
                oh = jnp.where(ones, 1.0, oh.astype(f32) * -2.0).astype(bf16)
                ol = (ol.astype(f32) * -2.0).astype(bf16)
                probes += [jnp.concatenate([oh, oh], axis=1), jnp.concatenate([ol, jnp.zeros_like(ol)], axis=1)]
            probe = jnp.concatenate(probes, axis=0)
            for g in range(nleaf * nskel // TI):
                both = jnp.concatenate(split(ag_ref[block(g), :]), axis=1)
                pltpu.matmul_push_rhs(both, 0, 0, transpose=True)
                pltpu.matmul_acc_lhs(rs[0], probe, load_staged_rhs=0)
                u = pltpu.matmul_pop(rs[0])
                near_mask = jnp.abs(lax.div(lax.broadcasted_iota(jnp.int32, (nskel, TI), 1) + g * TI, nskel) - leaf) <= 1
                weights = []
                for i in range(group):
                    lo = 2 * i * nskel
                    w = matern_of(norms[i] + u[lo : lo + nskel] + u[lo + nskel : lo + 2 * nskel])
                    same = jnp.full((nskel, TI), pair, jnp.int32) == first + i
                    weights += list(split(jnp.where(jnp.logical_and(same, near_mask), 0.0, w)))
                pltpu.matmul_push_rhs(both, 0, 1)
                pltpu.matmul_acc_lhs(xs[0], jnp.concatenate(weights, axis=0), load_staged_rhs=0)
            q = pltpu.matmul_pop(xs[0])
            q = q[:, :128] + q[:, 128:]
            for i in range(group):
                lo = 2 * i * nskel
                qo_ref[first + i] = q[lo : lo + nskel] + q[lo + nskel : lo + 2 * nskel]
        for c in stage_q:
            c.start()

    amplitude = 1.0 / math.sqrt(3.0 * n)
    lane = lax.broadcasted_iota(jnp.int32, (rhs, 128), 1)

    def near(x0, x1, y0, y1, r0, r1):
        xs, ys, rs = (x0, x1), (y0, y1), (r0, r1)
        own_block(xs, ys, rs)
        loads[4].wait()
        squares = jnp.sum(res_ref[...] * res_ref[...], axis=1, keepdims=True)
        curvature = jnp.sum(dir_ref[...] * (nugget * dir_ref[...] + amplitude * acc_ref[...]), axis=1, keepdims=True)
        curv_ref[...] = jnp.where(lane == 0, squares, jnp.where(lane == 1, curvature, 0.0))

        @pl.when(is_main)
        def _():
            @pl.loop(0, nc - 2)
            def _(ci):
                main_chunk(ci, xs, ys, rs, ahead=True)

            main_chunk(nc - 2, xs, ys, rs)

        @pl.when(helping)
        def _():
            for ci in range(nc - 1):
                help_columns(ci)
                help_part(ci, xs, ys, rs)

        far_field(xs, rs)

        @pl.when(is_main)
        def _():
            get_chunk(nc - 1)
            main_chunk(nc - 1, xs, ys, rs)

        @pl.when(helping)
        def _():
            help_columns(nc - 1)
            help_part(nc - 1, xs, ys, rs)

    pl.run_scoped(
        near,
        pltpu.ACC(1)((TI, TI), f32), pltpu.ACC(1)((TI, TI), f32),
        pltpu.ACC(0)((rhs, TI), f32), pltpu.ACC(1)((rhs, TI), f32),
        pltpu.ACC(0)((TI, TI), f32), pltpu.ACC(0)((TI, TI), f32),
    )

    def add_pair(d_ref):
        shared = jnp.sum(d_ref[...] * pacc_ref[...], axis=1, keepdims=True)
        curv_ref[...] += jnp.where(lane == 1, (2.0 * amplitude) * shared, 0.0)

    @pl.when(is_main)
    def _():
        add_pair(dir_ref)

    @pl.when(helping)
    def _():
        add_pair(zb_d)

    q_t = qo_ref[pair]
    for k in range(1, npair):
        src = lax.rem(pair + npair - k, npair)
        remote(qo_ref.at[src], qi_ref.at[src], qs_sem.at[k], qr_sem.at[k], pair=pair_peer(k)).wait_recv()
        q_t = q_t + qi_ref[src]
    far_row = (amplitude * far_weight) * jnp.sum(q_t * tg_ref[pair], axis=0, keepdims=True)[:, feats : feats + rhs]
    both = jnp.concatenate([curv_ref[...], jnp.zeros((128 - rhs, 128), f32)], axis=0).T
    both = jnp.concatenate([both[0:1, :rhs], both[1:2, :rhs] + far_row, jnp.zeros((1, 128 - 2 * rhs), f32)], axis=1)
    one_stage = nleaf * npair <= 64
    sends_b = []
    if one_stage:
        def partial(l, p):
            return red_a.at[p * nleaf + l]

        red_a[pair * nleaf + leaf] = both
        hops = [(a, b) for b in range(npair) for a in range(nleaf) if a or b]
        sends = [
            remote(partial(leaf, pair), partial(leaf, pair), cs_sem.at[a, b], cr_sem.at[a, b], leaf=leaf_peer(a), pair=pair_peer(b))
            for a, b in hops
        ]
    else:
        red_a[leaf] = both
        sends = [
            remote(red_a.at[leaf], red_a.at[leaf], cs_sem.at[k, 0], cr_sem.at[k, 0], leaf=leaf_peer(k))
            for k in range(1, nleaf)
        ]
    for c in sends:
        c.start()

    def spread(g0, g1):
        gs = (g0, g1)
        qh, ql = split(q_t[:, feats : feats + rhs].T)
        probe = wide(jnp.concatenate([qh, qh, ql], axis=1))
        for k in range(n // TI):
            m, r = k % 2, (k // 2) % 2
            pltpu.matmul_push_rhs(ks_ref[:, block(k)], r, m)
            pltpu.matmul_acc_lhs(gs[m], probe, load_staged_rhs=r)
            far = pltpu.matmul_pop(gs[m])
            prod_ref[:, block(k)] = nugget * dir_ref[:, block(k)] + amplitude * (acc_ref[:, block(k)] + far_weight * far)

    @pl.when(helping)
    def _():
        for ci in range(max(nc - 2, 0), nc):
            give_rows(ci).start()

    def pass_on():
        @pl.when(jnp.logical_and(is_main, chip_two))
        def _():
            for ci in range(nc):
                hand_over(ci).wait_recv()
                forward(ci).start()

    pl.run_scoped(spread, pltpu.ACC(0)((rhs, TI), f32), pltpu.ACC(1)((rhs, TI), f32))
    pass_on()

    @pl.when(is_main)
    def _():
        prod_ref[...] += amplitude * pacc_ref[...]

    def returned(k, ci):
        cols = chunk(ci)
        return remote(ret_out.at[:, cols], ret_in.at[k, :, cols], es_sem.at[ci], er_sem.at[k, ci], leaf=home_leaf, pair=pair)

    @pl.when(back_ok)
    def _():
        for ci in range(nc):
            give_rows(ci).wait_recv()
        prod_ref[...] += amplitude * ret_in[0]

    @pl.when(is_help)
    def _():
        for ci in range(nc):
            returned(0, ci).wait_recv()
        prod_ref[...] += amplitude * ret_in[0]

    @pl.when(home_two)
    def _():
        for ci in range(nc):
            returned(1, ci).wait_recv()
        prod_ref[...] += amplitude * ret_in[1]

    store = pltpu.make_async_copy(prod_ref, prod_hbm, out_sem)
    store.start()

    if one_stage:
        for a, b in hops:
            src = partial(lax.rem(leaf + nleaf - a, nleaf), lax.rem(pair + npair - b, npair))
            remote(src, src, cs_sem.at[a, b], cr_sem.at[a, b], leaf=leaf_peer(a), pair=pair_peer(b)).wait_recv()
        total = jnp.sum(red_a[...], axis=0)
    else:
        for k in range(1, nleaf):
            src = lax.rem(leaf + nleaf - k, nleaf)
            remote(red_a.at[src], red_a.at[src], cs_sem.at[k, 0], cr_sem.at[k, 0], leaf=leaf_peer(k)).wait_recv()
        red_b[pair] = jnp.sum(red_a[:nleaf], axis=0)
        sends_b = [
            remote(red_b.at[pair], red_b.at[pair], ds_sem.at[k], dr_sem.at[k], pair=pair_peer(k))
            for k in range(1, npair)
        ]
        for c in sends_b:
            c.start()
        for k in range(1, npair):
            src = lax.rem(pair + npair - k, npair)
            remote(red_b.at[src], red_b.at[src], ds_sem.at[k], dr_sem.at[k], pair=pair_peer(k)).wait_recv()
        total = jnp.sum(red_b[...], axis=0)
    total = total * (1.0 / (n * nleaf * npair))
    dots_ref[...] = jnp.concatenate([total[:, :rhs], total[:, rhs : 2 * rhs]], axis=0)

    for c in sends + sends_b + stage_a + stage_t + stage_q:
        c.wait_send()

    @pl.when(is_main)
    def _():
        for ci in range(nc):
            give_back(ci).wait_send()

    @pl.when(jnp.logical_and(is_main, chip_two))
    def _():
        for ci in range(nc):
            forward(ci).wait_send()

    @pl.when(helping)
    def _():
        for ci in range(nc):
            hand_over(ci).wait_send()

    @pl.when(helping)
    def _():
        for ci in range(nc):
            give_rows(ci).wait_send()

    @pl.when(is_main)
    def _():
        for ci in range(nc):
            for c in relay(ci):
                c.wait_send()

    @pl.when(jnp.logical_and(is_help, jnp.logical_not(chip_two)))
    def _():
        for ci in range(nc):
            for c in relay(ci):
                c.wait_recv()

    @pl.when(is_help)
    def _():
        for ci in range(nc):
            for c in to_main(ci):
                c.wait_send()

    @pl.when(back_ok)
    def _():
        for ci in range(nc):
            for c in to_help(ci):
                c.wait_send()

    store.wait()


def on_device(points, inv_scales, direction, residual, skeleton):
    feats, n = points.shape
    rhs = direction.shape[0]
    nskel = skeleton.shape[1]
    nleaf = lax.axis_size("leaf")
    npair = lax.axis_size("pair")
    anywhere = pl.BlockSpec(memory_space=pl.ANY)
    dma = pltpu.SemaphoreType.DMA
    nc = n // CC
    return pl.pallas_call(
        functools.partial(kernel, nleaf, npair),
        out_shape=(jax.ShapeDtypeStruct((rhs, n), f32), jax.ShapeDtypeStruct((2, rhs), f32)),
        in_specs=[pl.BlockSpec(memory_space=pltpu.HBM)] * 5,
        out_specs=(anywhere, pl.BlockSpec(memory_space=pltpu.VMEM)),
        scratch_shapes=[
            pltpu.VMEM((feats, n), f32),
            pltpu.VMEM((1, feats), f32),
            pltpu.VMEM((rhs, n), f32),
            pltpu.VMEM((rhs, n), f32),
            pltpu.VMEM((1, nskel), jnp.int32),
            pltpu.VMEM((rhs, n), f32),
            pltpu.VMEM((feats, n), f32),
            pltpu.VMEM((rhs, n), f32),
            pltpu.VMEM((feats, n), f32),
            pltpu.VMEM((rhs, n), f32),
            pltpu.VMEM((rhs, n), f32),
            pltpu.VMEM((rhs, n), f32),
            pltpu.VMEM((2, rhs, n), f32),
            pltpu.VMEM((2, 4 * feats, n), bf16),
            pltpu.VMEM((n, 4 * feats), bf16),
            pltpu.VMEM((2 * rhs, n), bf16),
            pltpu.VMEM((2, n, 128), bf16),
            pltpu.VMEM((rhs, n), f32),
            pltpu.VMEM((rhs, n), f32),
            pltpu.VMEM((TI, n), bf16),
            pltpu.VMEM((nleaf * nskel, 128), f32),
            pltpu.VMEM((npair, nskel, 128), f32),
            pltpu.VMEM((npair, nskel, 128), f32),
            pltpu.VMEM((npair, nskel, 128), f32),
            pltpu.VMEM((n, 4 * feats), bf16),
            pltpu.VMEM((2 * rhs, n), bf16),
            pltpu.VMEM((nleaf * npair if nleaf * npair <= 64 else nleaf, 1, 128), f32),
            pltpu.VMEM((npair, 1, 128), f32),
            pltpu.VMEM((rhs, 128), f32),
            dma((5,)), dma,
            dma((2, nc)), dma((2, nc)),
            dma((2, nc)), dma((2, nc)),
            dma((nc,)), dma((2, nc)),
            dma((nc,)), dma((nc,)),
            dma((nc,)), dma((nc,)),
            dma((nleaf,)), dma((nleaf,)),
            dma((npair,)), dma((npair,)),
            dma((npair,)), dma((npair,)),
            dma((nleaf, npair)), dma((nleaf, npair)),
            dma((npair,)), dma((npair,)),
        ],
        compiler_params=pltpu.CompilerParams(collective_id=0, has_side_effects=True, vmem_limit_bytes=40 * 1024 * 1024),
        name="matern_step",
    )(*[pltpu.with_memory_space_constraint(v, pltpu.HBM) for v in (points, inv_scales.reshape(1, feats), direction, residual, skeleton)])


def solution(mesh):
    return jax.shard_map(
        on_device,
        mesh=mesh,
        in_specs=(
            P(None, ("pair", "leaf")),
            P(),
            P(None, ("pair", "leaf")),
            P(None, ("pair", "leaf")),
            P(("pair", "leaf"), None),
        ),
        out_specs=(P(None, ("pair", "leaf")), P()),
        check_vma=False,
    )
```

```python
import functools
import math

import jax
import jax.numpy as jnp
from jax import lax
from jax.experimental import pallas as pl
from jax.experimental.pallas import tpu as pltpu
from jax.sharding import PartitionSpec as P

root_three = math.sqrt(3.0)
neg_log2e = -1.4426950408889634
nugget = 0.5
far_weight = 0.125
tiny = 1e-30
f32 = jnp.float32
bf16 = jnp.bfloat16
TI = 256
CC = 512
FIRST = 3
EARLY = 4
AHEAD = 8
CH = 256


def matern_of(u):
    u = jnp.maximum(u, tiny)
    t = u * lax.rsqrt(u)
    return (1.0 + t) * jnp.exp2(t * neg_log2e)


def split(x):
    h = x.astype(bf16)
    return h, (x - h.astype(f32)).astype(bf16)


def kernel(
    nleaf, npair,
    pts_hbm, inv_hbm, dir_hbm, res_hbm, skel_hbm,
    prod_hbm, dots_hbm,
    pts_ref, inv_ref, dir_ref, res_ref, skel_ref, prod_ref, dots_ref,
    xb_p, xb_d, zb_p, zb_d, ret_out, fwd_ref, ret_in, b_ref, st_ref, dd_ref, w_ref, acc_ref, pacc_ref, ks_ref, ag_ref, tg_ref, qo_ref, qi_ref, sz_ref, dz_ref, red_a, red_b, curv_ref,
    in_sem, out_sem, hs_sem, hr_sem, fs_sem, fr_sem, es_sem, er_sem, gs_sem, gr_sem, ps_sem, pr_sem, as_sem, ar_sem, bs_sem, br_sem, qs_sem, qr_sem, cs_sem, cr_sem, ds_sem, dr_sem,
):
    feats, n = pts_ref.shape
    rhs = dir_ref.shape[0]
    nskel = skel_ref.shape[1]
    leaf = lax.axis_index("leaf")
    pair = lax.axis_index("pair")

    leaf_odd = lax.rem(leaf, 2)
    pair_odd = lax.rem(pair, 2)
    is_main = leaf_odd == pair_odd
    is_help = leaf_odd != pair_odd
    step = 1 - 2 * leaf_odd
    other = pair + 1 - 2 * pair_odd
    far_leaf = leaf + 2 * step
    chip_two = jnp.logical_and(far_leaf >= 0, far_leaf < nleaf)
    helping = jnp.logical_and(is_help, chip_two)
    back_leaf = leaf - 2 * step
    back_ok = jnp.logical_and(is_main, jnp.logical_and(back_leaf >= 0, back_leaf < nleaf))
    home_step = 1 - 2 * pair_odd
    home_leaf = leaf - home_step
    home_far = home_leaf + 2 * home_step
    home_two = jnp.logical_and(is_help, jnp.logical_and(home_far >= 0, home_far < nleaf))

    def remote(src, dst, ss, rs, **dev):
        return pltpu.make_async_remote_copy(
            src_ref=src, dst_ref=dst, send_sem=ss, recv_sem=rs, device_id=dev,
            device_id_type=pl.DeviceIdType.MESH)

    def leaf_peer(k):
        return lax.rem(leaf + k, nleaf)

    def pair_peer(k):
        return lax.rem(pair + k, npair)

    loads = [
        pltpu.make_async_copy(src, dst, in_sem.at[k])
        for k, (src, dst) in enumerate((
            (inv_hbm, inv_ref), (pts_hbm, pts_ref), (dir_hbm, dir_ref), (skel_hbm, skel_ref), (res_hbm, res_ref)))
    ]
    for c in loads:
        c.start()

    barrier = pltpu.get_barrier_semaphore()

    def greet(**dev):
        pl.semaphore_signal(barrier, inc=1, device_id=dev, device_id_type=pl.DeviceIdType.MESH)

    for k in range(1, nleaf):
        greet(leaf=leaf_peer(k))
    for k in range(1, npair):
        greet(pair=pair_peer(k))

    @pl.when(back_ok)
    def _():
        greet(leaf=back_leaf, pair=other)

    @pl.when(helping)
    def _():
        greet(leaf=far_leaf, pair=other)

    def chunk(ci):
        return pl.ds(pl.multiple_of(ci * CC, CC), CC)

    def block_copies(ci, src_p, src_d, dst_p, dst_d, ss, rs, dev):
        cols = chunk(ci)
        return (
            remote(src_p.at[:, cols], dst_p.at[:, cols], ss.at[0, ci], rs.at[0, ci], **dev),
            remote(src_d.at[:, cols], dst_d.at[:, cols], ss.at[1, ci], rs.at[1, ci], **dev),
        )

    def to_main(ci):
        return block_copies(ci, pts_ref, dir_ref, xb_p, xb_d, hs_sem, hr_sem, dict(leaf=home_leaf, pair=pair))

    def to_help(ci):
        return block_copies(ci, pts_ref, dir_ref, zb_p, zb_d, hs_sem, hr_sem, dict(leaf=back_leaf, pair=other))

    def relay(ci):
        return block_copies(ci, xb_p, xb_d, xb_p, xb_d, fs_sem, fr_sem, dict(leaf=leaf, pair=other))

    def give_back(ci):
        cols = chunk(ci)
        return remote(ret_out.at[:, cols], ret_in.at[0, :, cols], es_sem.at[ci], er_sem.at[0, ci], leaf=leaf + step, pair=pair)

    def hand_over(ci):
        cols = chunk(ci)
        return remote(ret_out.at[:, cols], fwd_ref.at[:, cols], es_sem.at[ci], gr_sem.at[ci], leaf=leaf, pair=other)

    def forward(ci):
        cols = chunk(ci)
        return remote(fwd_ref.at[:, cols], ret_in.at[1, :, cols], gs_sem.at[ci], er_sem.at[1, ci], leaf=leaf + step, pair=pair)

    def give_rows(ci):
        cols = chunk(ci)
        return remote(pacc_ref.at[:, cols], ret_in.at[0, :, cols], ps_sem.at[ci], pr_sem.at[ci], leaf=far_leaf, pair=other)

    nc = n // CC

    def send_block(lo, hi):
        @pl.when(is_help)
        def _():
            for ci in range(lo, hi):
                for c in to_main(ci):
                    c.start()

        @pl.when(back_ok)
        def _():
            for ci in range(lo, hi):
                for c in to_help(ci):
                    c.start()

    for c in loads[:4]:
        c.wait()

    eye = lax.broadcasted_iota(jnp.int32, (feats, feats), 0) == lax.broadcasted_iota(jnp.int32, (feats, feats), 1)
    inv_col = jnp.sum(jnp.where(eye, jnp.broadcast_to(inv_ref[...], (feats, feats)), 0.0), axis=1, keepdims=True) * root_three

    def norm_rows(norm):
        n1 = norm.astype(bf16).astype(f32)
        n2 = (norm - n1).astype(bf16).astype(f32)
        return jnp.concatenate([n1, n2, norm - n1 - n2], axis=0)

    def parts(p_src, cols):
        p = p_src[:, cols] * inv_col
        h, l = split(p)
        hf, lf = h.astype(f32), l.astype(f32)
        q = hf + lf
        norm = norm_rows(jnp.sum(q * q, axis=0, keepdims=True))
        return h, l, hf, lf, norm

    def as_cols(h, l, norm):
        w = norm.shape[1]
        ext = jnp.concatenate([jnp.ones((3, w), f32), norm, jnp.zeros((feats - 6, w), f32)], axis=0)
        return jnp.concatenate([h, l, h, ext.astype(bf16)], axis=0)

    def as_rows(hf, lf, norm):
        w = norm.shape[1]
        ext = jnp.concatenate([norm, jnp.ones((3, w), f32), jnp.zeros((feats - 6, w), f32)], axis=0)
        h2 = hf * -2.0
        return jnp.concatenate([h2, h2, lf * -2.0, ext], axis=0).T.astype(bf16)

    def both_halves(d_src, cols):
        return jnp.concatenate(split(d_src[:, cols]), axis=0)

    def as_weights(dd):
        w = dd.shape[1]
        return jnp.concatenate([dd.astype(f32), jnp.zeros((128 - 2 * rhs, w), f32)], axis=0).T.astype(bf16)

    def prepare(ci):
        cols = pl.ds(pl.multiple_of(ci * CH, CH), CH)
        h, l, hf, lf, norm = parts(pts_ref, cols)
        b_ref[0, :, cols] = as_cols(h, l, norm)
        st_ref[cols, :] = as_rows(hf, lf, norm)
        dd = both_halves(dir_ref, cols)
        dd_ref[:, cols] = dd
        w_ref[0, cols, :] = as_weights(dd)
        ks_ref[3 * nskel :, cols] = jnp.zeros((TI - 3 * nskel, CH), bf16)
        acc_ref[:, cols] = jnp.zeros((rhs, CH), f32)
        pacc_ref[:, cols] = jnp.zeros((rhs, CH), f32)

    pl.loop(0, EARLY)(prepare)

    extra = jnp.where(jnp.logical_or(back_ok, helping), 1, 0)
    pl.semaphore_wait(barrier, nleaf - 1 + npair - 1 + extra)

    send_block(0, FIRST)

    pl.loop(EARLY, n // CH)(prepare)

    nt = n // TI

    def sweep(plan, xs, ys, rs):
        stage = [0, 0]

        def push(v, m):
            k = stage[m]
            stage[m] = 1 - k
            pltpu.matmul_push_rhs(v, k, m)
            return k

        def cross(t):
            for go in plan[t].get("first", ()):
                go()
            pltpu.matmul_acc_lhs(xs[t % 2], plan[t]["rows"](), load_staged_rhs=push(plan[t]["cols"](), 1))

        def spend(t, k):
            p = plan[t]
            if p["turn"] is not None:
                w = p["weights"]()
                w = jnp.concatenate([w, jnp.zeros_like(w)], axis=1)
                pltpu.matmul_acc_lhs(rs[p["turn"]], k, load_staged_rhs=push(w, 0))
            m = t % 2
            dd = p["dd"]()
            pltpu.matmul_acc_lhs(ys[m], dd[:rhs], load_staged_rhs=push(k, m))
            pltpu.matmul_acc_lhs(ys[m], dd[rhs:])

        def finish(t):
            p = plan[t]
            p["out"](pltpu.matmul_pop(ys[t % 2]))
            if p["turned"] is not None:
                r = pltpu.matmul_pop(rs[p["turn"]])[:, :128].T
                p["turned"](r[:rhs] + r[rhs : 2 * rhs])
            for go in p.get("then", ()):
                go()

        count = len(plan)
        cross(0)
        held = None
        for t in range(count + 2):
            k = None
            if t < count:
                k = matern_of(pltpu.matmul_pop(xs[t % 2])).astype(bf16)
            if t + 1 < count:
                cross(t + 1)
            if 0 < t <= count:
                spend(t - 1, held)
            held = k
            if t > 1:
                finish(t - 2)

    def get_chunk(ci):
        for c in to_main(ci):
            c.wait_recv()
        for c in relay(ci):
            c.start()

    def own_block(xs, ys, rs):
        half = nt // 2

        def rows_pair(k, reach):
            plan = []
            for i in range(2):
                def tile(d, i=i):
                    return pl.ds(pl.multiple_of(lax.rem(2 * k + i + nt - d, nt) * TI, TI), TI)

                def add(cols):
                    def go(v):
                        acc_ref[:, cols] += v
                    return go

                rows = tile(0)
                for d in range(reach + 1):
                    cols = tile(d)
                    plan.append(dict(
                        rows=lambda rows=rows: st_ref[rows, :],
                        cols=lambda cols=cols: b_ref[0, :, cols],
                        weights=lambda cols=cols: w_ref[0, cols, :],
                        dd=lambda rows=rows: dd_ref[:, rows],
                        turn=i if d else None,
                        out=add(cols),
                        turned=add(rows) if d == reach else None,
                    ))
            sweep(plan, xs, ys, rs)

        pl.loop(0, half // 2)(lambda k: rows_pair(k, half))

        @pl.loop(half // 2, half)
        def _(k):
            @pl.when(jnp.logical_and(is_main, k == half - 1))
            def _():
                get_chunk(0)

            rows_pair(k, half - 1)

    def cross_tile(st, dd, cols, where, turn, turned):
        def add(v):
            pacc_ref[:, cols] += v

        return dict(
            rows=st,
            cols=lambda: b_ref[where, :, cols],
            weights=lambda: w_ref[where, cols, :],
            dd=dd,
            turn=turn,
            out=add,
            turned=turned,
        )

    def main_chunk(ci, xs, ys, rs, ahead=False):
        plan = []
        for i in range(CC // TI):
            rows = pl.ds(pl.multiple_of(ci * CC + i * TI, TI), TI)
            _, _, hf, lf, norm = parts(xb_p, rows)
            st = as_rows(hf, lf, norm)
            dd = both_halves(xb_d, rows)

            def turned(v, rows=rows):
                ret_out[:, rows] = v

            for jt in range(nt):
                cols = slice(jt * TI, (jt + 1) * TI)
                plan.append(cross_tile(lambda st=st: st, lambda dd=dd: dd, cols, 0, i % 2, turned if jt == nt - 1 else None))
        if ahead:
            plan[AHEAD]["first"] = [lambda: get_chunk(ci + 1)]
        sweep(plan, xs, ys, rs)
        give_back(ci).start()

    def help_columns(ci):
        for c in to_help(ci):
            c.wait_recv()
        for i in range(CC // CH):
            cols = slice(ci * CC + i * CH, ci * CC + (i + 1) * CH)
            h, l, _, _, norm = parts(zb_p, cols)
            b_ref[1, :, cols] = as_cols(h, l, norm)
            w_ref[1, cols, :] = as_weights(both_halves(zb_d, cols))

    def help_rows(ci):
        for c in relay(ci):
            c.wait_recv()
        for i in range(CC // CH):
            rows = slice(ci * CC + i * CH, ci * CC + (i + 1) * CH)
            _, _, hf, lf, norm = parts(xb_p, rows)
            sz_ref[rows, :] = as_rows(hf, lf, norm)
            dz_ref[:, rows] = both_halves(xb_d, rows)

    def help_part(ci, xs, ys, rs):
        per = CC // TI
        last = ci == nc - 1
        early, late = ci * per, (ci + 1) * per
        plan = []

        def add_tile(it, jt, ends, fresh):
            rows = slice(it * TI, (it + 1) * TI)

            def turned(v):
                if fresh:
                    ret_out[:, rows] = v
                else:
                    ret_out[:, rows] += v

            plan.append(cross_tile(
                lambda: sz_ref[rows, :], lambda: dz_ref[:, rows], slice(jt * TI, (jt + 1) * TI), 1, it % 2,
                turned if ends else None))

        for it in range(early):
            for jt in range(early, late):
                add_tile(it, jt, jt == late - 1, False)
        if last:
            plan[-1]["then"] = [hand_over(c).start for c in range(ci)]
        start = len(plan)
        for c in range(ci + 1):
            for it in range(early, late):
                for jt in range(c * per, (c + 1) * per):
                    add_tile(it, jt, c == ci and jt == late - 1, True)
            if last and c < nc - 3:
                plan[-1]["then"] = [give_rows(c).start]
        if last:
            plan[-1]["then"] = [hand_over(ci).start]
        plan[start]["first"] = [lambda: help_rows(ci)]
        sweep(plan, xs, ys, rs)

    def wide(w):
        return jnp.concatenate([w, jnp.zeros((w.shape[0], TI - w.shape[1]), w.dtype)], axis=1)

    def deep_dot(accs, lhs, rhs_of, count):
        for k in range(count):
            m, r = k % 2, (k // 2) % 2
            pltpu.matmul_push_rhs(rhs_of(k), r, m)
            pltpu.matmul_acc_lhs(accs[m], lhs(k), load_staged_rhs=r)
        return pltpu.matmul_pop(accs[0]) + pltpu.matmul_pop(accs[1])

    def block(k):
        return slice(k * TI, (k + 1) * TI)

    def skeleton(p0, p1, c0, c1, f0, f1):
        index = jnp.broadcast_to(wide(skel_ref[...] + 1), (TI, TI)) - 1

        def chosen(k):
            return jnp.where(lax.broadcasted_iota(jnp.int32, (TI, TI), 0) + k * TI == index, 1.0, 0.0).astype(bf16)

        picked = deep_dot((p0, p1), lambda k: b_ref[0, : 2 * feats, block(k)], chosen, n // TI)[:, :128]
        skel_rows = (picked[:feats] + picked[feats:]).T[:nskel]
        norm_s = jnp.sum(skel_rows * skel_rows, axis=1, keepdims=True)
        sh, sl = split(skel_rows)
        sh, sl = sh.astype(f32) * -2.0, sl.astype(f32) * -2.0
        n1 = norm_s.astype(bf16).astype(f32)
        n2 = (norm_s - n1).astype(bf16).astype(f32)
        lane_s = lax.broadcasted_iota(jnp.int32, (nskel, feats), 1)
        ext_s = jnp.where(lane_s == 0, n1, jnp.where(lane_s == 1, n2, jnp.where(lane_s == 2, norm_s - n1 - n2, jnp.where(lane_s < 6, 1.0, 0.0))))
        probe = jnp.concatenate([sh, sh, sl, ext_s], axis=1).astype(bf16)
        cs = (c0, c1)
        for k in range(n // TI):
            m, r = k % 2, (k // 2) % 2
            pltpu.matmul_push_rhs(b_ref[0, :, block(k)], r, m)
            pltpu.matmul_acc_lhs(cs[m], probe, load_staged_rhs=r)
            h, l = split(matern_of(pltpu.matmul_pop(cs[m])))
            ks_ref[: 3 * nskel, block(k)] = jnp.concatenate([h, l, h], axis=0)
        part = deep_dot((f0, f1), lambda k: ks_ref[: 2 * nskel, block(k)], lambda k: wide(w_ref[0, block(k), :]), n // TI)
        coeff_t = part[:nskel, :rhs] + part[:nskel, rhs : 2 * rhs] + part[nskel:, :rhs] + part[nskel:, rhs : 2 * rhs]
        pad = jnp.zeros((nskel, 128 - feats - rhs - 2), f32)
        pack = jnp.concatenate([skel_rows, coeff_t, n1, norm_s - n1, pad], axis=1)
        ag_ref[my_rows, :] = pack
        tg_ref[pair] = pack

    my_rows = pl.ds(pl.multiple_of(leaf * nskel, 8), nskel)
    pl.run_scoped(
        skeleton,
        pltpu.ACC(0)((2 * feats, TI), f32), pltpu.ACC(1)((2 * feats, TI), f32),
        pltpu.ACC(0)((nskel, TI), f32), pltpu.ACC(1)((nskel, TI), f32),
        pltpu.ACC(0)((2 * nskel, TI), f32), pltpu.ACC(1)((2 * nskel, TI), f32),
    )

    stage_a = [
        remote(ag_ref.at[my_rows, :], ag_ref.at[my_rows, :], as_sem.at[k], ar_sem.at[k], leaf=leaf_peer(k))
        for k in range(1, nleaf)
    ]
    stage_t = [
        remote(tg_ref.at[pair], tg_ref.at[pair], bs_sem.at[k], br_sem.at[k], pair=pair_peer(k))
        for k in range(1, npair)
    ]
    stage_q = [
        remote(qo_ref.at[pair_peer(k)], qi_ref.at[pair], qs_sem.at[k], qr_sem.at[k], pair=pair_peer(k))
        for k in range(1, npair)
    ]
    for c in stage_a + stage_t:
        c.start()
    send_block(FIRST, nc)

    group = TI // (2 * nskel)

    def far_field(xs, rs):
        for k, c in enumerate(stage_a, 1):
            src_rows = pl.ds(pl.multiple_of(lax.rem(leaf + nleaf - k, nleaf) * nskel, 8), nskel)
            remote(ag_ref.at[src_rows, :], ag_ref.at[src_rows, :], as_sem.at[k], ar_sem.at[k], leaf=leaf_peer(k)).wait_recv()
        for k, c in enumerate(stage_t, 1):
            src = lax.rem(pair + npair - k, npair)
            remote(tg_ref.at[src], tg_ref.at[src], bs_sem.at[k], br_sem.at[k], pair=pair_peer(k)).wait_recv()
        lane_o = lax.broadcasted_iota(jnp.int32, (nskel, 128), 1)
        ones = jnp.logical_and(lane_o >= feats + rhs, lane_o < feats + rhs + 2)
        for first in range(0, npair, group):
            probes, norms = [], []
            for p in range(first, first + group):
                target = jnp.where(lane_o < feats, tg_ref[p], 0.0)
                norms.append(jnp.sum(target * target, axis=1, keepdims=True))
                oh, ol = split(target)
                oh = jnp.where(ones, 1.0, oh.astype(f32) * -2.0).astype(bf16)
                ol = (ol.astype(f32) * -2.0).astype(bf16)
                probes += [jnp.concatenate([oh, oh], axis=1), jnp.concatenate([ol, jnp.zeros_like(ol)], axis=1)]
            probe = jnp.concatenate(probes, axis=0)
            for g in range(nleaf * nskel // TI):
                both = jnp.concatenate(split(ag_ref[block(g), :]), axis=1)
                pltpu.matmul_push_rhs(both, 0, 0, transpose=True)
                pltpu.matmul_acc_lhs(rs[0], probe, load_staged_rhs=0)
                u = pltpu.matmul_pop(rs[0])
                near_mask = jnp.abs(lax.div(lax.broadcasted_iota(jnp.int32, (nskel, TI), 1) + g * TI, nskel) - leaf) <= 1
                weights = []
                for i in range(group):
                    lo = 2 * i * nskel
                    w = matern_of(norms[i] + u[lo : lo + nskel] + u[lo + nskel : lo + 2 * nskel])
                    same = jnp.full((nskel, TI), pair, jnp.int32) == first + i
                    weights += list(split(jnp.where(jnp.logical_and(same, near_mask), 0.0, w)))
                pltpu.matmul_push_rhs(both, 0, 1)
                pltpu.matmul_acc_lhs(xs[0], jnp.concatenate(weights, axis=0), load_staged_rhs=0)
            q = pltpu.matmul_pop(xs[0])
            q = q[:, :128] + q[:, 128:]
            for i in range(group):
                lo = 2 * i * nskel
                qo_ref[first + i] = q[lo : lo + nskel] + q[lo + nskel : lo + 2 * nskel]
        for c in stage_q:
            c.start()

    amplitude = 1.0 / math.sqrt(3.0 * n)
    lane = lax.broadcasted_iota(jnp.int32, (rhs, 128), 1)

    def near(x0, x1, y0, y1, r0, r1):
        xs, ys, rs = (x0, x1), (y0, y1), (r0, r1)
        own_block(xs, ys, rs)
        loads[4].wait()
        squares = jnp.sum(res_ref[...] * res_ref[...], axis=1, keepdims=True)
        curvature = jnp.sum(dir_ref[...] * (nugget * dir_ref[...] + amplitude * acc_ref[...]), axis=1, keepdims=True)
        curv_ref[...] = jnp.where(lane == 0, squares, jnp.where(lane == 1, curvature, 0.0))

        @pl.when(is_main)
        def _():
            @pl.loop(0, nc - 2)
            def _(ci):
                main_chunk(ci, xs, ys, rs, ahead=True)

            main_chunk(nc - 2, xs, ys, rs)

        @pl.when(helping)
        def _():
            for ci in range(nc - 1):
                help_columns(ci)
                help_part(ci, xs, ys, rs)

        far_field(xs, rs)

        @pl.when(is_main)
        def _():
            get_chunk(nc - 1)
            main_chunk(nc - 1, xs, ys, rs)

        @pl.when(helping)
        def _():
            help_columns(nc - 1)
            help_part(nc - 1, xs, ys, rs)

    pl.run_scoped(
        near,
        pltpu.ACC(1)((TI, TI), f32), pltpu.ACC(1)((TI, TI), f32),
        pltpu.ACC(0)((rhs, TI), f32), pltpu.ACC(1)((rhs, TI), f32),
        pltpu.ACC(0)((TI, TI), f32), pltpu.ACC(0)((TI, TI), f32),
    )

    def add_pair(d_ref):
        shared = jnp.sum(d_ref[...] * pacc_ref[...], axis=1, keepdims=True)
        curv_ref[...] += jnp.where(lane == 1, (2.0 * amplitude) * shared, 0.0)

    @pl.when(is_main)
    def _():
        add_pair(dir_ref)

    @pl.when(helping)
    def _():
        add_pair(zb_d)

    q_t = qo_ref[pair]
    for k in range(1, npair):
        src = lax.rem(pair + npair - k, npair)
        remote(qo_ref.at[src], qi_ref.at[src], qs_sem.at[k], qr_sem.at[k], pair=pair_peer(k)).wait_recv()
        q_t = q_t + qi_ref[src]
    far_row = (amplitude * far_weight) * jnp.sum(q_t * tg_ref[pair], axis=0, keepdims=True)[:, feats : feats + rhs]
    both = jnp.concatenate([curv_ref[...], jnp.zeros((128 - rhs, 128), f32)], axis=0).T
    both = jnp.concatenate([both[0:1, :rhs], both[1:2, :rhs] + far_row, jnp.zeros((1, 128 - 2 * rhs), f32)], axis=1)
    one_stage = nleaf * npair <= 64
    sends_b = []
    if one_stage:
        def partial(l, p):
            return red_a.at[p * nleaf + l]

        red_a[pair * nleaf + leaf] = both
        hops = [(a, b) for b in range(npair) for a in range(nleaf) if a or b]
        sends = [
            remote(partial(leaf, pair), partial(leaf, pair), cs_sem.at[a, b], cr_sem.at[a, b], leaf=leaf_peer(a), pair=pair_peer(b))
            for a, b in hops
        ]
    else:
        red_a[leaf] = both
        sends = [
            remote(red_a.at[leaf], red_a.at[leaf], cs_sem.at[k, 0], cr_sem.at[k, 0], leaf=leaf_peer(k))
            for k in range(1, nleaf)
        ]
    for c in sends:
        c.start()

    def spread(g0, g1):
        gs = (g0, g1)
        qh, ql = split(q_t[:, feats : feats + rhs].T)
        probe = wide(jnp.concatenate([qh, qh, ql], axis=1))
        for k in range(n // TI):
            m, r = k % 2, (k // 2) % 2
            pltpu.matmul_push_rhs(ks_ref[:, block(k)], r, m)
            pltpu.matmul_acc_lhs(gs[m], probe, load_staged_rhs=r)
            far = pltpu.matmul_pop(gs[m])
            prod_ref[:, block(k)] = nugget * dir_ref[:, block(k)] + amplitude * (acc_ref[:, block(k)] + far_weight * far)

    @pl.when(helping)
    def _():
        for ci in range(max(nc - 3, 0), nc):
            give_rows(ci).start()

    def pass_on():
        @pl.when(jnp.logical_and(is_main, chip_two))
        def _():
            for ci in range(nc):
                hand_over(ci).wait_recv()
                forward(ci).start()

    pl.run_scoped(spread, pltpu.ACC(0)((rhs, TI), f32), pltpu.ACC(1)((rhs, TI), f32))
    pass_on()

    @pl.when(is_main)
    def _():
        prod_ref[...] += amplitude * pacc_ref[...]

    def returned(k, ci):
        cols = chunk(ci)
        return remote(ret_out.at[:, cols], ret_in.at[k, :, cols], es_sem.at[ci], er_sem.at[k, ci], leaf=home_leaf, pair=pair)

    @pl.when(back_ok)
    def _():
        for ci in range(nc):
            give_rows(ci).wait_recv()
        prod_ref[...] += amplitude * ret_in[0]

    @pl.when(is_help)
    def _():
        for ci in range(nc):
            returned(0, ci).wait_recv()
        prod_ref[...] += amplitude * ret_in[0]

    @pl.when(home_two)
    def _():
        for ci in range(nc):
            returned(1, ci).wait_recv()
        prod_ref[...] += amplitude * ret_in[1]

    store = pltpu.make_async_copy(prod_ref, prod_hbm, out_sem)
    store.start()

    if one_stage:
        for a, b in hops:
            src = partial(lax.rem(leaf + nleaf - a, nleaf), lax.rem(pair + npair - b, npair))
            remote(src, src, cs_sem.at[a, b], cr_sem.at[a, b], leaf=leaf_peer(a), pair=pair_peer(b)).wait_recv()
        total = jnp.sum(red_a[...], axis=0)
    else:
        for k in range(1, nleaf):
            src = lax.rem(leaf + nleaf - k, nleaf)
            remote(red_a.at[src], red_a.at[src], cs_sem.at[k, 0], cr_sem.at[k, 0], leaf=leaf_peer(k)).wait_recv()
        red_b[pair] = jnp.sum(red_a[:nleaf], axis=0)
        sends_b = [
            remote(red_b.at[pair], red_b.at[pair], ds_sem.at[k], dr_sem.at[k], pair=pair_peer(k))
            for k in range(1, npair)
        ]
        for c in sends_b:
            c.start()
        for k in range(1, npair):
            src = lax.rem(pair + npair - k, npair)
            remote(red_b.at[src], red_b.at[src], ds_sem.at[k], dr_sem.at[k], pair=pair_peer(k)).wait_recv()
        total = jnp.sum(red_b[...], axis=0)
    total = total * (1.0 / (n * nleaf * npair))
    dots_ref[...] = jnp.concatenate([total[:, :rhs], total[:, rhs : 2 * rhs]], axis=0)
    store_dots = pltpu.make_async_copy(dots_ref, dots_hbm, in_sem.at[0])
    store_dots.start()

    for c in sends + sends_b + stage_a + stage_t + stage_q:
        c.wait_send()

    @pl.when(is_main)
    def _():
        for ci in range(nc):
            give_back(ci).wait_send()

    @pl.when(jnp.logical_and(is_main, chip_two))
    def _():
        for ci in range(nc):
            forward(ci).wait_send()

    @pl.when(helping)
    def _():
        for ci in range(nc):
            hand_over(ci).wait_send()

    @pl.when(helping)
    def _():
        for ci in range(nc):
            give_rows(ci).wait_send()

    @pl.when(is_main)
    def _():
        for ci in range(nc):
            for c in relay(ci):
                c.wait_send()

    @pl.when(jnp.logical_and(is_help, jnp.logical_not(chip_two)))
    def _():
        for ci in range(nc):
            for c in relay(ci):
                c.wait_recv()

    @pl.when(is_help)
    def _():
        for ci in range(nc):
            for c in to_main(ci):
                c.wait_send()

    @pl.when(back_ok)
    def _():
        for ci in range(nc):
            for c in to_help(ci):
                c.wait_send()

    store.wait()
    store_dots.wait()


def on_device(points, inv_scales, direction, residual, skeleton):
    feats, n = points.shape
    rhs = direction.shape[0]
    nskel = skeleton.shape[1]
    nleaf = lax.axis_size("leaf")
    npair = lax.axis_size("pair")
    anywhere = pl.BlockSpec(memory_space=pl.ANY)
    dma = pltpu.SemaphoreType.DMA
    nc = n // CC
    return pl.pallas_call(
        functools.partial(kernel, nleaf, npair),
        out_shape=(jax.ShapeDtypeStruct((rhs, n), f32), jax.ShapeDtypeStruct((2, rhs), f32)),
        in_specs=[pl.BlockSpec(memory_space=pltpu.HBM)] * 5,
        out_specs=(anywhere, anywhere),
        scratch_shapes=[
            pltpu.VMEM((feats, n), f32),
            pltpu.VMEM((1, feats), f32),
            pltpu.VMEM((rhs, n), f32),
            pltpu.VMEM((rhs, n), f32),
            pltpu.VMEM((1, nskel), jnp.int32),
            pltpu.VMEM((rhs, n), f32),
            pltpu.VMEM((2, rhs), f32),
            pltpu.VMEM((feats, n), f32),
            pltpu.VMEM((rhs, n), f32),
            pltpu.VMEM((feats, n), f32),
            pltpu.VMEM((rhs, n), f32),
            pltpu.VMEM((rhs, n), f32),
            pltpu.VMEM((rhs, n), f32),
            pltpu.VMEM((2, rhs, n), f32),
            pltpu.VMEM((2, 4 * feats, n), bf16),
            pltpu.VMEM((n, 4 * feats), bf16),
            pltpu.VMEM((2 * rhs, n), bf16),
            pltpu.VMEM((2, n, 128), bf16),
            pltpu.VMEM((rhs, n), f32),
            pltpu.VMEM((rhs, n), f32),
            pltpu.VMEM((TI, n), bf16),
            pltpu.VMEM((nleaf * nskel, 128), f32),
            pltpu.VMEM((npair, nskel, 128), f32),
            pltpu.VMEM((npair, nskel, 128), f32),
            pltpu.VMEM((npair, nskel, 128), f32),
            pltpu.VMEM((n, 4 * feats), bf16),
            pltpu.VMEM((2 * rhs, n), bf16),
            pltpu.VMEM((nleaf * npair if nleaf * npair <= 64 else nleaf, 1, 128), f32),
            pltpu.VMEM((npair, 1, 128), f32),
            pltpu.VMEM((rhs, 128), f32),
            dma((5,)), dma,
            dma((2, nc)), dma((2, nc)),
            dma((2, nc)), dma((2, nc)),
            dma((nc,)), dma((2, nc)),
            dma((nc,)), dma((nc,)),
            dma((nc,)), dma((nc,)),
            dma((nleaf,)), dma((nleaf,)),
            dma((npair,)), dma((npair,)),
            dma((npair,)), dma((npair,)),
            dma((nleaf, npair)), dma((nleaf, npair)),
            dma((npair,)), dma((npair,)),
        ],
        compiler_params=pltpu.CompilerParams(collective_id=0, has_side_effects=True, vmem_limit_bytes=40 * 1024 * 1024),
        name="matern_step",
    )(*[pltpu.with_memory_space_constraint(v, pltpu.HBM) for v in (points, inv_scales.reshape(1, feats), direction, residual, skeleton)])


def solution(mesh):
    return jax.shard_map(
        on_device,
        mesh=mesh,
        in_specs=(
            P(None, ("pair", "leaf")),
            P(),
            P(None, ("pair", "leaf")),
            P(None, ("pair", "leaf")),
            P(("pair", "leaf"), None),
        ),
        out_specs=(P(None, ("pair", "leaf")), P()),
        check_vma=False,
    )
```
